32 devices in a mesh: groups: 2 (over y), depth: 4 (over z), rows: 2 (over x), cols: 2 (over core).
Axes of the slice: x: 2, y: 2, z: 4, core: 2. Of those that a mesh axis runs over, the one named last changes fastest.
Arguments:
- volume: bfloat16 [4, 16, 16, 3072], P('groups', 'depth', 'rows', 'cols'), parts along dimension 0, may hold values from -6 to 6
- grad_out: bfloat16 [4, 16, 16, 3072], P('groups', 'depth', 'rows', 'cols'), parts along dimension 0, may hold values from -6 to 6
- report: bfloat16 [1536], P('groups'), parts along dimension 0, may hold values from -6 to 6
- conv_kernel: bfloat16 [96, 1, 7, 7, 7], replicated, may hold values from -0.3125 to 0.3125
- conv_bias: float32 [96], replicated, may hold values from -4 to 4
- film_weight: bfloat16 [768, 192], replicated, may hold values from -0.21875 to 0.21875
- film_bias: float32 [192], replicated, may hold values from -3 to 3
- in_weight: bfloat16 [96, 384], replicated, may hold values from -0.625 to 0.625
- in_bias: float32 [384], replicated, may hold values from -3 to 3
- out_weight: bfloat16 [384, 96], replicated, may hold values from -0.3125 to 0.3125
Outputs:
- grad_input: bfloat16 [4, 16, 16, 3072], P('groups', 'depth', 'rows', 'cols'), parts along dimension 0
- grad_kernel: float32 [192, 1, 7, 7, 7], P('groups'), parts along dimension 0
- grad_conv_bias: float32 [192], P('groups'), parts along dimension 0
- grad_film: float32 [384], P('groups'), parts along dimension 0
- grad_in_weight: float32 [192, 384], P('groups'), parts along dimension 0
- grad_in_bias: float32 [768], P('groups'), parts along dimension 0
- grad_out_weight: float32 [768, 96], P('groups'), parts along dimension 0
The draws below stay inside these ranges and needn't reach their ends.
There are 2 independent parts, one for each index of `groups`. The reference program is written for one: setup_inputs(seed, part) draws one part's arguments, and reference() takes and returns one part's arrays. A program takes and returns all parts, laid end to end along the dimension named above; an argument that names none is the same for every part. Nothing has to cross between parts.
All inputs are finite; a program needn't handle non-finite values.
Results may differ from the reference program's by a relative error of at most 0.0062.
Values may be sent and summed in bfloat16 or wider, within the bound.
A program may use at most 64 MiB of HBM per device.

```python
import math
import jax
import jax.numpy as jnp
from jax import lax

C = 96
F = 384
E = 768
K = 7
B = 2
DEPTH = 16
HEIGHT = 16
WIDTH = 32
VOXELS = 8192
N_DEPTH = 4


def block_scale(stream_key, extent, shards, low, largest):
    def one(dim, parts):
        heights = jax.random.uniform(jax.random.fold_in(jax.random.fold_in(stream_key, 6), dim), (parts,), jnp.float32, low / len(shards), largest / len(shards))
        return jnp.repeat(jnp.exp(heights), extent[dim] // parts).reshape((-1,) + (1,) * (len(extent) - dim - 1))

    gain = one(*shards[0])
    for cut in shards[1:]:
        gain = gain * one(*cut)
    return gain


def noise(key, extent, spread, limit, shards=(), dtype=jnp.bfloat16):
    entries = spread * jax.random.normal(key, extent, jnp.float32)
    if shards:
        entries = entries * block_scale(key, extent, shards, -0.22, 0.18)
    return jnp.clip(entries, -limit, limit).astype(dtype)


def setup_inputs(seed: int = 0, part: int = 0) -> dict:
    key_of = jax.random.split(jax.random.key(seed), 11)
    part_splits = jax.random.split(jax.random.fold_in(key_of[10], part), 11)
    return {
        "volume": noise(part_splits[0], (B, DEPTH, HEIGHT, WIDTH * C), 1.0, 6.0, ((1, 4), (2, 2), (3, 2))),
        "grad_out": noise(part_splits[1], (B, DEPTH, HEIGHT, WIDTH * C), 1.0, 6.0, ((1, 4), (2, 2), (3, 2))),
        "report": noise(part_splits[2], (E,), 1.0, 6.0),
        "conv_kernel": noise(key_of[3], (C, 1, K, K, K), (K * K * K) ** -0.5, 0.3125),
        "conv_bias": noise(key_of[4], (C,), 1.0, 4.0, (), jnp.float32),
        "film_weight": noise(key_of[5], (E, 2 * C), E ** -0.5, 0.21875),
        "film_bias": noise(key_of[6], (2 * C,), 0.5, 3.0, (), jnp.float32),
        "in_weight": noise(key_of[7], (C, F), C ** -0.5, 0.625),
        "in_bias": noise(key_of[8], (F,), 0.5, 3.0, (), jnp.float32),
        "out_weight": noise(key_of[9], (F, C), F ** -0.5, 0.3125),
    }


epsilon = 1e-06
conv_dims = ('NCDHW', 'OIDHW', 'NCDHW')

def depthwise(padded, kernel):
    return lax.conv_general_dilated(padded[None], kernel, (1, 1, 1), 'VALID', dimension_numbers=conv_dims, feature_group_count=kernel.shape[0], preferred_element_type=jnp.float32)[0]

def pointwise(conv_flat, grad_flat, film_vec, in_weight, in_bias, out_weight):
    channels = conv_flat.shape[0]
    chan_mean = lax.optimization_barrier(jnp.mean(conv_flat, axis=0))
    centred = conv_flat - chan_mean
    variance = lax.optimization_barrier(jnp.mean(centred * centred, axis=0))
    inverse = lax.rsqrt(variance + epsilon)
    normed = centred * inverse
    scale_vec = 1.0 + film_vec[:channels, None]
    hidden_in = (normed * scale_vec + film_vec[channels:, None]).astype(jnp.bfloat16)
    pre_act = jnp.dot(in_weight.T, hidden_in, preferred_element_type=jnp.float32) + in_bias[:, None]
    post_act, gelu_back = jax.vjp(jax.nn.gelu, pre_act)
    act_low = post_act.astype(jnp.bfloat16)
    grad_act = jnp.dot(out_weight, grad_flat, preferred_element_type=jnp.float32)
    grad_pre = gelu_back(grad_act)[0]
    grad_low = grad_pre.astype(jnp.bfloat16)
    grad_hidden = jnp.dot(in_weight, grad_low, preferred_element_type=jnp.float32)
    grad_out_w = jnp.dot(act_low, grad_flat.T, preferred_element_type=jnp.float32)
    grad_in_w = jnp.dot(hidden_in, grad_low.T, preferred_element_type=jnp.float32)
    grad_in_b = lax.optimization_barrier(jnp.sum(grad_pre, axis=1))
    grad_film = jnp.concatenate([lax.optimization_barrier(jnp.sum(grad_hidden * normed, axis=1)), lax.optimization_barrier(jnp.sum(grad_hidden, axis=1))])
    grad_normed = grad_hidden * scale_vec
    slope = ((grad_normed - lax.optimization_barrier(jnp.mean(grad_normed, axis=0)) - normed * lax.optimization_barrier(jnp.mean(grad_normed * normed, axis=0))) * inverse).astype(jnp.bfloat16)
    return (slope, (grad_in_w, grad_in_b, grad_out_w, grad_film))

def channels_first(crop):
    return jnp.transpose(crop.reshape(DEPTH, HEIGHT, WIDTH, C), (3, 0, 1, 2))

def reference(volume, grad_out, report, conv_kernel, conv_bias, film_weight, film_bias, in_weight, in_bias, out_weight):
    half_width = K // 2
    film_vec = jnp.dot(report[None, :], film_weight, preferred_element_type=jnp.float32)[0] + film_bias
    pad_spec = ((0, 0), (half_width, half_width), (half_width, half_width), (half_width, half_width))
    flipped = conv_kernel[:, :, ::-1, ::-1, ::-1]

    def one_crop(crop_pair):
        crop = channels_first(crop_pair[0])
        crop_grad = channels_first(crop_pair[1])
        padded = jnp.pad(crop, pad_spec)
        conv_out = depthwise(padded, conv_kernel) + conv_bias[:, None, None, None]
        blocks = N_DEPTH
        conv_blocks = jnp.moveaxis(conv_out.reshape(C, blocks, -1), 1, 0)
        grad_blocks = jnp.moveaxis(crop_grad.reshape(C, blocks, -1), 1, 0)

        def one_block(block_pair):
            return pointwise(block_pair[0], block_pair[1], film_vec, in_weight, in_bias, out_weight)
        slope_blocks, block_grads = lax.map(one_block, (conv_blocks, grad_blocks))
        slope_vol = jnp.moveaxis(slope_blocks, 0, 1).reshape(crop.shape)
        totals = jax.tree.map(lambda stacked: lax.optimization_barrier(jnp.sum(stacked, axis=0)), block_grads)
        slope_pad = jnp.pad(slope_vol, pad_spec)
        crop_input = (crop_grad.astype(jnp.float32) + depthwise(slope_pad, flipped)).astype(jnp.bfloat16)
        crop_input = jnp.transpose(crop_input, (1, 2, 3, 0)).reshape(DEPTH, HEIGHT, WIDTH * C)
        kernel_sum = lax.conv_general_dilated(padded[None], slope_vol[:, None], (1, 1, 1), 'VALID', dimension_numbers=conv_dims, feature_group_count=C, preferred_element_type=jnp.float32).reshape(conv_kernel.shape)
        bias_sum = lax.optimization_barrier(jnp.sum(slope_vol.astype(jnp.float32), axis=(1, 2, 3)))
        return (crop_input, (kernel_sum, bias_sum) + tuple(totals))
    grad_input, crop_sums = lax.map(one_crop, (volume, grad_out))
    sums = jax.tree.map(lambda stacked: lax.optimization_barrier(jnp.sum(stacked, axis=0)), crop_sums)
    factor = 1.0 / math.sqrt(B * VOXELS)
    return (grad_input, sums[0] * factor, sums[1] * factor, sums[5] * factor, sums[2] * factor, sums[3] * factor, sums[4] * factor)
```

```python
import functools
import math

import jax
import jax.numpy as jnp
import numpy as np
from jax import lax
from jax.experimental import pallas as pl
from jax.experimental.pallas import tpu as pltpu
from jax.sharding import PartitionSpec as P

K = 7
HALF = K // 2
LANES = 128
SUB = 8
EDGE = 4
EPSILON = 1e-06
MESH = pl.DeviceIdType.MESH
GELU_C = math.sqrt(2.0 / math.pi)
DIRS = tuple(
    (dz, dx, dc)
    for dz in (-1, 0, 1)
    for dx in (-1, 0, 1)
    for dc in (-1, 0, 1)
    if (dz, dx, dc) != (0, 0, 0)
)


def both(*conds):
    out = conds[0]
    for cond in conds[1:]:
        out = jnp.logical_and(out, cond)
    return out


def split_bf16(array):
    high = array.astype(jnp.bfloat16)
    low = (array - high.astype(np.float64)).astype(jnp.bfloat16)
    return high, low


def fourier_tables(rows, width):
    points_h, points_w = rows + 2 * HALF, width + 2 * HALF
    half_w = points_w // 2 + 1
    freqs = [(a, b) for b in range(half_w) for a in range(points_h)]
    freqs += [None] * (-len(freqs) % SUB)

    def phases(cells):
        table = np.zeros((len(freqs), len(cells)))
        live = np.zeros((len(freqs), len(cells)))
        for f, freq in enumerate(freqs):
            for n, cell in enumerate(cells):
                if freq is not None and cell is not None:
                    turns = (freq[0] * cell[0] % points_h) / points_h
                    turns += (freq[1] * cell[1] % points_w) / points_w
                    table[f, n] = 2.0 * np.pi * turns
                    live[f, n] = 1.0
        return table, live

    def interleave(real, imag):
        tiles = len(freqs) // SUB
        both_parts = np.stack(
            [real.reshape(tiles, SUB, -1), imag.reshape(tiles, SUB, -1)], axis=1
        )
        return both_parts.reshape(2 * len(freqs), -1)

    def analysis(cells, sign):
        angle, live = phases(cells)
        high, low = split_bf16(interleave(np.cos(angle) * live, sign * np.sin(angle) * live))
        return np.concatenate([high, low], axis=0)

    def synthesis(cells):
        angle, live = phases(cells)
        weight = np.array(
            [
                0.0 if f is None else (1.0 if f[1] in (0, points_w // 2) else 2.0)
                for f in freqs
            ]
        )[:, None] / (points_h * points_w)
        table = interleave(np.cos(angle) * weight * live, -np.sin(angle) * weight * live).T
        high, low = split_bf16(table)
        return np.concatenate([high, high, low], axis=1)

    def padded(h, w):
        inside = -HALF <= h < rows + HALF and -HALF <= w < width + HALF
        return (h + HALF, w + HALF) if inside else None

    columns = width + 2 * EDGE
    plane = []
    for s in range(columns // 2):
        for r in range(2 * SUB):
            plane.append(padded(r % SUB, s + columns // 2 * (r // SUB) - EDGE))
    slots = width // 2 + 2 * EDGE
    for s in range(slots):
        for r in range(2 * SUB):
            h = r % EDGE + (-EDGE if r < SUB else rows)
            top = r % SUB < EDGE
            if top:
                col = None if s < EDGE else (s if s < slots - EDGE else s + width // 2)
            else:
                col = None if s >= slots - EDGE else (s if s < EDGE else s + width // 2)
            plane.append(None if col is None else padded(h, col - EDGE))
    own = [
        (r % SUB, s + width // 2 * (r // SUB)) for s in range(width // 2) for r in range(2 * SUB)
    ]
    taps = [(j, k) if k < K else None for j in range(K) for k in range(SUB)]
    lags = [(n // K, n % K) if n < K * K else None for n in range(K * SUB)]
    return {
        "plane": analysis(plane, -1.0),
        "own": analysis(own, -1.0),
        "taps": analysis(taps, 1.0),
        "forward": synthesis(own),
        "backward": synthesis([(h + K - 1, w + K - 1) for h, w in own]),
        "lags": synthesis(lags),
    }


class Halo:
    def __init__(self, own, edges, main, side, sems, where, counts):
        self.own, self.edges, self.main, self.side = own, edges, main, side
        self.send, self.recv = sems
        self.grp, self.z, self.x, self.c = where
        self.nz, self.nx, self.nc = counts
        self.depth, self.lanes = own.shape[1], own.shape[3]
        self.edge_lanes = (self.main.shape[3] - self.lanes) // 2

    def inside(self, dz, dx, dc):
        z, x, c = self.z + dz, self.x + dx, self.c + dc
        return both(z >= 0, z < self.nz, x >= 0, x < self.nx, c >= 0, c < self.nc)

    def copy(self, crop, idx):
        dz, dx, dc = DIRS[idx]
        depth, lanes, edge = self.depth, self.lanes, self.edge_lanes
        src_d = {-1: slice(0, HALF), 0: slice(0, depth), 1: slice(depth - HALF, depth)}[dz]
        dst_d = {
            -1: slice(HALF + depth, 2 * HALF + depth),
            0: slice(HALF, HALF + depth),
            1: slice(0, HALF),
        }[dz]
        every = slice(None)
        full = lanes if dx == 0 else lanes // 2
        src_l = {-1: slice(0, edge), 0: slice(0, full), 1: slice(full - edge, full)}[dc]
        dst_l = {
            -1: slice(edge + full, 2 * edge + full),
            0: slice(edge, edge + full),
            1: slice(0, edge),
        }[dc]
        if dx == 0:
            src = self.own.at[crop, src_d, every, src_l]
            dst = self.main.at[crop, dst_d, every, dst_l]
        else:
            src = self.edges.at[0 if dx < 0 else 1, crop, src_d, every, src_l]
            dst = self.side.at[crop, 1 if dx < 0 else 0, dst_d, every, dst_l]
        return pltpu.make_async_remote_copy(
            src_ref=src,
            dst_ref=dst,
            send_sem=self.send.at[crop, idx],
            recv_sem=self.recv.at[crop, idx],
            device_id=(self.grp, self.z + dz, self.x + dx, self.c + dc),
            device_id_type=MESH,
        )

    def fill_edges(self):
        depth, edge = self.depth, self.edge_lanes

        def clear(cond, *areas):
            @pl.when(cond)
            def _():
                for ref, area in areas:
                    view = ref.at[area]
                    view[...] = jnp.zeros(view.shape, view.dtype)

        every = slice(None)
        low, high = slice(0, HALF), slice(HALF + depth, 2 * HALF + depth)
        main, side = self.main, self.side
        clear(self.z == 0, (main, (every, low)), (side, (every, every, low)))
        clear(self.z == self.nz - 1, (main, (every, high)), (side, (every, every, high)))
        clear(self.x == 0, (side, (every, 0)))
        clear(self.x == self.nx - 1, (side, (every, 1)))
        rest = (every, every, every)
        clear(self.c == 0, (main, rest + (slice(0, edge),)), (side, (every,) + rest + (slice(0, edge),)))
        clear(
            self.c == self.nc - 1,
            (main, rest + (slice(main.shape[3] - edge, main.shape[3]),)),
            (side, (every,) + rest + (slice(side.shape[4] - edge, side.shape[4]),)),
        )

    def cut_edges(self, crop):
        half = self.lanes // 2
        for d in range(self.depth):
            for which, first in enumerate((0, EDGE)):
                for part in range(2):
                    self.edges[which, crop, d, part * EDGE : (part + 1) * EDGE, :] = self.own[
                        crop, d, first : first + EDGE, part * half : (part + 1) * half
                    ]

    def start(self, crop):
        for idx, step in enumerate(DIRS):
            @pl.when(self.inside(*step))
            def _():
                self.copy(crop, idx).start()

    def centre(self, crop):
        depth, lanes, edge = self.depth, self.lanes, self.edge_lanes
        self.main[crop, HALF : HALF + depth, :, edge : edge + lanes] = self.own[crop]

    def arrive(self, crop):
        for idx, (dz, dx, dc) in enumerate(DIRS):
            @pl.when(self.inside(-dz, -dx, -dc))
            def _():
                self.copy(crop, idx).wait_recv()

    def finish(self, crop):
        for idx, step in enumerate(DIRS):
            @pl.when(self.inside(*step))
            def _():
                self.copy(crop, idx).wait_send()


def slot_slices(array, channels):
    return [array[:, s * channels : (s + 1) * channels] for s in range(array.shape[1] // channels)]


def gather_plane(main, side, crop, plane, xs, lane, channels):
    wide = main[crop, plane]
    half = wide.shape[1] // 2
    wide = jnp.concatenate([wide[:, :half], wide[:, half:]], axis=0)
    rim = jnp.concatenate([side[crop, 0, plane], side[crop, 1, plane]], axis=0)
    for n, cell in enumerate(slot_slices(wide, channels) + slot_slices(rim, channels)):
        xs[n * 2 * SUB : (n + 1) * 2 * SUB, lane : lane + channels] = cell


def spectra(main, side, crop, xs, table, out, channels):
    planes = main.shape[1]
    rows = out.shape[2]

    def step(pair, _):
        for q in range(2):
            gather_plane(main, side, crop, 2 * pair + q, xs, q * LANES, channels)
        res = jnp.dot(table[...], xs[...], preferred_element_type=jnp.float32)
        res = res[:rows] + res[rows:]
        for q in range(2):
            out[crop, 2 * pair + q] = res[:, q * LANES : (q + 1) * LANES]
        return 0

    lax.fori_loop(0, planes // 2, step, 0)


def store_split(ref, tile, lane, re, im):
    value = jnp.concatenate([re, im], axis=0)
    high = value.astype(jnp.bfloat16)
    low = (value - high.astype(jnp.float32)).astype(jnp.bfloat16)
    rows = ref.shape[0] // 3
    for n, part in enumerate((high, low, high)):
        first = pl.multiple_of(tile * 2 * SUB, 2 * SUB) + n * rows
        ref[pl.ds(first, 2 * SUB), lane : lane + LANES] = part


def tile_of(ref, lead, tile):
    first = pl.multiple_of(tile * 2 * SUB, 2 * SUB)
    return ref[lead + (pl.ds(first, SUB),)], ref[lead + (pl.ds(first + SUB, SUB),)]


def conv_products(xhat, khat, crop, depth, yhat, flip):
    tiles = yhat.shape[0] // (3 * 2 * SUB)

    def step(tile, _):
        taps = [tile_of(khat, (i,), tile) for i in range(K)]
        data = [tile_of(xhat, (crop, p), tile) for p in range(depth + K - 1)]
        for d in range(depth):
            re = im = None
            for i in range(K):
                kr, ki = taps[i]
                xr, xi = data[d + K - 1 - i if flip else d + i]
                if flip:
                    a, b = xr * kr + xi * ki, xi * kr - xr * ki
                else:
                    a, b = xr * kr - xi * ki, xr * ki + xi * kr
                re, im = (a, b) if re is None else (re + a, im + b)
            store_split(yhat, tile, d * LANES, re, im)
        return 0

    lax.fori_loop(0, tiles, step, 0)


def lag_products(xhat, ohat, crops, depth, ghat):
    tiles = ghat.shape[0] // (3 * 2 * SUB)

    def step(tile, _):
        accs = [[None, None] for _ in range(K)]
        for crop in range(crops):
            data = [tile_of(xhat, (crop, p), tile) for p in range(depth + K - 1)]
            slope = [tile_of(ohat, (crop, d), tile) for d in range(depth)]
            for i in range(K):
                for d in range(depth):
                    xr, xi = data[d + i]
                    sr, si = slope[d]
                    a, b = xr * sr + xi * si, xi * sr - xr * si
                    acc = accs[i]
                    accs[i] = [a, b] if acc[0] is None else [acc[0] + a, acc[1] + b]
        for i in range(K):
            store_split(ghat, tile, i * LANES, accs[i][0], accs[i][1])
        return 0

    lax.fori_loop(0, tiles, step, 0)


def to_native(slots, channels):
    line = jnp.concatenate([slot[:, :channels] for slot in slots], axis=1)
    return jnp.concatenate([line[:SUB], line[SUB:]], axis=1)


def kernel(
    counts, channels, row_of, factor,
    x_raw, g_raw, kernel_ref, bias_ref, report_ref, fw_ref, small_ref, inw_raw, outw_raw,
    f_plane, f_own, f_taps, s_fwd, s_bwd, s_lags,
    gi_ref, gk_ref, gb_ref, gsmall_ref, ginw_ref, goutw_ref,
    inw_ref, outw_ref, red_ref, x_main, x_side, x_edges, s_own, s_main, s_side, s_edges,
    gs, xs, own_rhs, taps_s, khat, xhat, shat, ohat, yhat, ghat, conv_s,
    vec_ref, accw, accb, accf, part, part_low, inbox, mine, full,
    x_send, x_recv, sl_send, sl_recv,
    rs_send, rs_recv, ag_send, ag_recv,
):
    nz, nx, nc = counts
    total = nz * nx * nc
    grp, z, x, c = (lax.axis_index(name) for name in ("groups", "depth", "rows", "cols"))
    me = (z * nx + x) * nc + c
    crops, depth = x_raw.shape[:2]
    hidden = inw_raw.shape[1]
    chunk = part.shape[0] // total
    voxels = s_fwd.shape[0]
    bf, f32 = jnp.bfloat16, jnp.float32

    def peer(offset):
        other = lax.rem(me + offset, total)
        return other, (grp, other // (nx * nc), (other // nc) % nx, other % nc)

    barrier = pltpu.get_barrier_semaphore()

    def greet(offset, _):
        pl.semaphore_signal(barrier, inc=1, device_id=peer(offset)[1], device_id_type=MESH)
        return 0

    lax.fori_loop(1, total, greet, 0)
    where = (grp, z, x, c)
    halo_x = Halo(x_raw, x_edges, x_main, x_side, (x_send, x_recv), where, counts)
    halo_s = Halo(s_own, s_edges, s_main, s_side, (sl_send, sl_recv), where, counts)
    for crop in range(crops):
        halo_x.cut_edges(crop)
    pl.semaphore_wait(barrier, total - 1)
    for crop in range(crops):
        halo_x.start(crop)
    halo_x.fill_edges()
    halo_s.fill_edges()
    for crop in range(crops):
        halo_x.centre(crop)
    spare = LANES - channels
    for raw, ready in ((inw_raw, inw_ref), (outw_raw, outw_ref)):
        ready[0:channels, :] = raw[...]
        ready[channels:, :] = jnp.zeros((spare, hidden), bf)
    xs[...] = jnp.zeros_like(xs)
    gs[...] = jnp.zeros_like(gs)
    taps_s[...] = jnp.zeros_like(taps_s)
    for i in range(K):
        for j in range(K):
            taps_s[j * SUB : j * SUB + K, i * LANES : i * LANES + channels] = kernel_ref[
                i, j
            ].astype(f32)
    res = jnp.dot(f_taps[...], taps_s[...].astype(bf), preferred_element_type=f32)
    half = res.shape[0] // 2
    res = res[:half] + res[half:]
    for i in range(K):
        khat[i] = res[:, i * LANES : (i + 1) * LANES]
    for crop in range(crops):
        for d in range(depth):
            wide = g_raw[crop, d]
            middle = wide.shape[1] // 2
            wide = jnp.concatenate([wide[:, :middle], wide[:, middle:]], axis=0)
            for n, cell in enumerate(slot_slices(wide, channels)):
                first = n * 2 * SUB
                gs[crop, d, first : first + 2 * SUB, 0:channels] = cell
    vec_ref[...] = jnp.zeros_like(vec_ref)
    vec_ref[0:1, 0:channels] = bias_ref[...]
    for side in range(2):
        film = lax.dot_general(
            report_ref[...], fw_ref[side * channels : (side + 1) * channels, :],
            (((1,), (1,)), ((), ())), preferred_element_type=f32,
        )
        film = film + small_ref[side : side + 1, 0:channels]
        vec_ref[side + 1 : side + 2, 0:channels] = film + (1.0 if side == 0 else 0.0)
    accw[...] = jnp.zeros_like(accw)
    accb[...] = jnp.zeros_like(accb)
    accf[...] = jnp.zeros_like(accf)
    tail = row_of["small"]
    part[tail:, :] = jnp.zeros((part.shape[0] - tail, LANES), f32)

    conv_bias, scale, shift = vec_ref[0:1, :], vec_ref[1:2, :], vec_ref[2:3, :]
    in_bias = jnp.concatenate(
        [small_ref[2 + b : 3 + b, :] for b in range(hidden // LANES)], axis=1
    )
    real = lax.broadcasted_iota(jnp.int32, (1, LANES), 1) < channels

    def mlp(crop, d):
        conv = conv_s[d] + conv_bias
        mean = jnp.sum(conv, axis=1, keepdims=True) * (1.0 / channels)
        centred = jnp.where(real, conv - mean, 0.0)
        variance = jnp.sum(centred * centred, axis=1, keepdims=True) * (1.0 / channels)
        inverse = lax.rsqrt(variance + EPSILON)
        normed = centred * inverse
        hidden_in = (normed * scale + shift).astype(bf)
        grad = gs[crop, d]
        pre = jnp.dot(hidden_in, inw_ref[...], preferred_element_type=f32) + in_bias
        square = pre * pre
        th = jnp.tanh(GELU_C * (pre + 0.044715 * (square * pre)))
        act_low = (0.5 * pre * (1.0 + th)).astype(bf)
        slope_act = 0.5 * (1.0 + th) + 0.5 * pre * (1.0 - th * th) * (
            GELU_C * (1.0 + (3.0 * 0.044715) * square)
        )
        grad_act = jnp.dot(grad, outw_ref[...], preferred_element_type=f32)
        grad_pre = grad_act * slope_act
        grad_low = grad_pre.astype(bf)
        grad_hidden = lax.dot_general(
            grad_low, inw_ref[...], (((1,), (1,)), ((), ())), preferred_element_type=f32
        )
        over_voxels = (((0,), (0,)), ((), ()))
        accw[0] += lax.dot_general(hidden_in, grad_low, over_voxels, preferred_element_type=f32)
        accw[1] += lax.dot_general(grad, act_low, over_voxels, preferred_element_type=f32)
        accb[0:1, :] += jnp.sum(grad_pre, axis=0, keepdims=True)
        accf[1:2, :] += jnp.sum(grad_hidden * normed, axis=0, keepdims=True)
        accf[2:3, :] += jnp.sum(grad_hidden, axis=0, keepdims=True)
        grad_normed = grad_hidden * scale
        mean_g = jnp.sum(grad_normed, axis=1, keepdims=True) * (1.0 / channels)
        mean_gn = jnp.sum(grad_normed * normed, axis=1, keepdims=True) * (1.0 / channels)
        slope = ((grad_normed - mean_g - normed * mean_gn) * inverse).astype(bf)
        accf[0:1, :] += jnp.sum(slope.astype(f32), axis=0, keepdims=True)
        own_rhs[crop, d] = slope
        s_own[crop, d] = to_native(
            [slope[n * 2 * SUB : (n + 1) * 2 * SUB] for n in range(voxels // (2 * SUB))], channels
        )

    def forward(crop, _):
        halo_x.arrive(crop)
        spectra(x_main, x_side, crop, xs, f_plane, xhat, channels)
        conv_products(xhat, khat, crop, depth, yhat, False)
        conv = jnp.dot(s_fwd[...], yhat[...], preferred_element_type=f32)
        for d in range(depth):
            conv_s[d] = conv[:, d * LANES : (d + 1) * LANES]

        def each_plane(d, _):
            mlp(crop, d)
            return 0

        lax.fori_loop(0, depth, each_plane, 0)
        halo_s.cut_edges(crop)
        halo_s.start(crop)
        halo_s.centre(crop)
        return 0

    lax.fori_loop(0, crops, forward, 0)

    def own_spectra(step, _):
        crop, pair = step // (depth // 2), step % (depth // 2)
        rhs = jnp.concatenate([own_rhs[crop, 2 * pair], own_rhs[crop, 2 * pair + 1]], axis=1)
        res = jnp.dot(f_own[...], rhs, preferred_element_type=f32)
        res = res[: res.shape[0] // 2] + res[res.shape[0] // 2 :]
        for q in range(2):
            ohat[crop, 2 * pair + q] = res[:, q * LANES : (q + 1) * LANES]
        return 0

    lax.fori_loop(0, crops * depth // 2, own_spectra, 0)
    lag_products(xhat, ohat, crops, depth, ghat)
    lags = jnp.dot(s_lags[...], ghat[...], preferred_element_type=f32)
    stride = K * SUB
    for i in range(K):
        first = row_of["kernel"] + i * stride
        part[first : first + stride, :] = lags[:, i * LANES : (i + 1) * LANES]

    for which, name in enumerate(("in", "out")):
        for block in range(hidden // LANES):
            first = row_of[name] + block * channels
            part[first : first + channels, :] = accw[
                which, 0:channels, block * LANES : (block + 1) * LANES
            ]
    part[row_of["small"] : row_of["small"] + 3, :] = accf[0:3, :]
    for block in range(hidden // LANES):
        row = row_of["in_bias"] + block
        part[row : row + 1, :] = accb[0:1, block * LANES : (block + 1) * LANES]
    part_low[...] = part[...].astype(bf)

    def scatter(offset):
        other, device = peer(offset)
        return pltpu.make_async_remote_copy(
            src_ref=part_low.at[pl.ds(pl.multiple_of(other * chunk, chunk), chunk)],
            dst_ref=inbox.at[offset],
            send_sem=rs_send.at[offset],
            recv_sem=rs_recv.at[offset],
            device_id=device,
            device_id_type=MESH,
        )

    my_rows = pl.ds(pl.multiple_of(me * chunk, chunk), chunk)

    def spread(offset):
        return pltpu.make_async_remote_copy(
            src_ref=mine,
            dst_ref=full.at[my_rows],
            send_sem=ag_send.at[offset],
            recv_sem=ag_recv.at[offset],
            device_id=peer(offset)[1],
            device_id_type=MESH,
        )

    def arrived(offset):
        origin = lax.rem(me + total - offset, total)
        return pltpu.make_async_remote_copy(
            src_ref=mine,
            dst_ref=full.at[pl.ds(pl.multiple_of(origin * chunk, chunk), chunk)],
            send_sem=ag_send.at[offset],
            recv_sem=ag_recv.at[offset],
            device_id=peer(offset)[1],
            device_id_type=MESH,
        )

    def each(fn):
        def step(offset, _):
            fn(offset)
            return 0

        lax.fori_loop(1, total, step, 0)

    each(lambda offset: scatter(offset).start())

    def backward(crop, _):
        halo_s.arrive(crop)
        spectra(s_main, s_side, crop, xs, f_plane, shat, channels)
        conv_products(shat, khat, crop, depth, yhat, True)
        conv = jnp.dot(s_bwd[...], yhat[...], preferred_element_type=f32)
        for d in range(depth):
            total_in = gs[crop, d].astype(f32) + conv[:, d * LANES : (d + 1) * LANES]
            low = total_in.astype(bf)
            gi_ref[crop, d] = to_native(
                [low[n * 2 * SUB : (n + 1) * 2 * SUB] for n in range(voxels // (2 * SUB))],
                channels,
            )
        return 0

    lax.fori_loop(0, crops // 2, backward, 0)

    each(lambda offset: scatter(offset).wait())

    def add(offset, acc):
        return acc + inbox[offset].astype(f32)

    summed = lax.fori_loop(1, total, add, part[my_rows, :])
    mine[...] = summed.astype(bf)
    full[my_rows, :] = mine[...]
    each(lambda offset: spread(offset).start())
    lax.fori_loop(crops // 2, crops, backward, 0)

    def settle(offset):
        spread(offset).wait_send()
        arrived(offset).wait_recv()

    each(settle)
    for crop in range(crops):
        halo_x.finish(crop)
        halo_s.finish(crop)
    red_ref[...] = full[...].astype(f32) * factor
    for name, out_ref in (("in", ginw_ref), ("out", goutw_ref)):
        for block in range(hidden // LANES):
            first = row_of[name] + block * channels
            out_ref[:, block * LANES : (block + 1) * LANES] = red_ref[first : first + channels, :]
    for i in range(K):
        for j in range(K):
            first = row_of["kernel"] + i * stride + j * K
            gk_ref[i, j] = red_ref[first : first + K, 0:channels]
    gb_ref[...] = red_ref[row_of["small"] : row_of["small"] + 1, 0:channels]
    gsmall_ref[...] = red_ref[row_of["small"] : row_of["small"] + SUB, :]


def local(
    counts, volume, grad_out, report, conv_kernel, conv_bias,
    film_weight, film_bias, in_weight, in_bias, out_weight,
):
    crops, slices, lines, merged = volume.shape
    channels = conv_kernel.shape[0]
    hidden = in_weight.shape[1]
    width = merged // channels
    extra = LANES - channels
    smalls = jnp.concatenate(
        [
            jnp.pad(film_bias.reshape(2, channels), ((0, 0), (0, extra))),
            in_bias.reshape(hidden // LANES, LANES),
        ]
    )
    raw_kernel = jnp.transpose(conv_kernel[:, 0], (1, 2, 3, 0))
    total = counts[0] * counts[1] * counts[2]
    blocks = hidden // LANES
    row_of = {"in": 0, "out": blocks * channels, "kernel": 2 * blocks * channels}
    row_of["small"] = row_of["kernel"] + K * K * SUB
    row_of["in_bias"] = row_of["small"] + 3
    row_of["end"] = row_of["in_bias"] + -(-(blocks + 3) // SUB) * SUB
    unit = 16 * total
    all_rows = -(-row_of["end"] // unit) * unit
    chunk = all_rows // total
    bf, f32 = jnp.bfloat16, jnp.float32
    dma = pltpu.SemaphoreType.DMA
    tables = fourier_tables(lines, width)
    names = ("plane", "own", "taps", "forward", "backward", "lags")
    spec = tables["plane"].shape[0] // 2
    planes = slices + 2 * HALF
    voxels = lines * width
    edge_lanes = EDGE * channels
    halves = merged // 2 + 2 * edge_lanes
    main = (crops, planes, lines, merged + 2 * edge_lanes)
    side = (crops, 2, planes, 2 * EDGE, halves)
    edges = (2, crops, slices, 2 * EDGE, merged // 2)
    factor = 1.0 / math.sqrt(crops * slices * voxels * total)
    grad_input, grad_kernel, grad_bias, smalls_out, grad_in_w, grad_out_w = pl.pallas_call(
        functools.partial(kernel, counts, channels, row_of, factor),
        out_shape=(
            jax.ShapeDtypeStruct(volume.shape, bf),
            jax.ShapeDtypeStruct((K, K, K, channels), f32),
            jax.ShapeDtypeStruct((1, channels), f32),
            jax.ShapeDtypeStruct((SUB, LANES), f32),
            jax.ShapeDtypeStruct((channels, hidden), f32),
            jax.ShapeDtypeStruct((channels, hidden), f32),
        ),
        in_specs=[pl.BlockSpec(memory_space=pltpu.VMEM)] * (9 + len(names)),
        out_specs=(pl.BlockSpec(memory_space=pltpu.VMEM),) * 6,
        scratch_shapes=[
            pltpu.VMEM((LANES, hidden), bf),
            pltpu.VMEM((LANES, hidden), bf),
            pltpu.VMEM((all_rows, LANES), f32),
            pltpu.VMEM(main, bf),
            pltpu.VMEM(side, bf),
            pltpu.VMEM(edges, bf),
            pltpu.VMEM(volume.shape, bf),
            pltpu.VMEM(main, bf),
            pltpu.VMEM(side, bf),
            pltpu.VMEM(edges, bf),
            pltpu.VMEM((crops, slices, voxels, LANES), bf),
            pltpu.VMEM((tables["plane"].shape[1], 2 * LANES), bf),
            pltpu.VMEM((crops, slices, voxels, LANES), bf),
            pltpu.VMEM((K * SUB, K * LANES), f32),
            pltpu.VMEM((K, spec, LANES), f32),
            pltpu.VMEM((crops, planes, spec, LANES), f32),
            pltpu.VMEM((crops, planes, spec, LANES), f32),
            pltpu.VMEM((crops, slices, spec, LANES), f32),
            pltpu.VMEM((3 * spec, slices * LANES), bf),
            pltpu.VMEM((3 * spec, K * LANES), bf),
            pltpu.VMEM((slices, voxels, LANES), f32),
            pltpu.VMEM((SUB, LANES), f32),
            pltpu.VMEM((2, LANES, hidden), f32),
            pltpu.VMEM((SUB, hidden), f32),
            pltpu.VMEM((SUB, LANES), f32),
            pltpu.VMEM((all_rows, LANES), f32),
            pltpu.VMEM((all_rows, LANES), bf),
            pltpu.VMEM((total, chunk, LANES), bf),
            pltpu.VMEM((chunk, LANES), bf),
            pltpu.VMEM((all_rows, LANES), bf),
        ]
        + [dma((crops, len(DIRS)))] * 4
        + [dma((total,))] * 4,
        compiler_params=pltpu.CompilerParams(
            collective_id=0, has_side_effects=True, vmem_limit_bytes=56 * 1024 * 1024
        ),
        name="block",
    )(
        volume,
        grad_out,
        raw_kernel,
        conv_bias[None, :],
        report[None, :],
        film_weight.T,
        smalls,
        in_weight,
        out_weight.T,
        *(tables[name] for name in names),
    )
    grad_kernel = jnp.transpose(grad_kernel, (3, 0, 1, 2))[:, None]
    grad_film = smalls_out[1:3, :channels].reshape(2 * channels)
    grad_in_b = smalls_out[3 : 3 + blocks].reshape(hidden)
    return (
        grad_input, grad_kernel, grad_bias[0], grad_film, grad_in_w, grad_in_b, grad_out_w.T
    )


def solution(mesh):
    split = P("groups", "depth", "rows", "cols")
    in_specs = (split, split, P("groups")) + (P(),) * 7
    out_specs = (
        split,
        P("groups", None, None, None, None),
        P("groups"),
        P("groups"),
        P("groups", None),
        P("groups"),
        P("groups", None),
    )
    counts = tuple(mesh.shape[name] for name in ("depth", "rows", "cols"))
    return jax.shard_map(
        functools.partial(local, counts),
        mesh=mesh,
        in_specs=in_specs,
        out_specs=out_specs,
        check_vma=False,
    )
```

```python
import functools
import math

import jax
import jax.numpy as jnp
import numpy as np
from jax import lax
from jax.experimental import pallas as pl
from jax.experimental.pallas import tpu as pltpu
from jax.sharding import PartitionSpec as P

K = 7
HALF = K // 2
LANES = 128
SUB = 8
EDGE = 4
EPSILON = 1e-06
MESH = pl.DeviceIdType.MESH
GELU_C = math.sqrt(2.0 / math.pi)
DIRS = tuple(
    (dz, dx, dc)
    for dz in (-1, 0, 1)
    for dx in (-1, 0, 1)
    for dc in (-1, 0, 1)
    if (dz, dx, dc) != (0, 0, 0)
)


def both(*conds):
    out = conds[0]
    for cond in conds[1:]:
        out = jnp.logical_and(out, cond)
    return out


def split_bf16(array):
    high = array.astype(jnp.bfloat16)
    low = (array - high.astype(np.float64)).astype(jnp.bfloat16)
    return high, low


def fourier_tables(rows, width):
    points_h, points_w = rows + 2 * HALF, width + 2 * HALF
    half_w = points_w // 2 + 1
    freqs = [(a, b) for b in range(half_w) for a in range(points_h)]
    freqs += [None] * (-len(freqs) % SUB)

    def phases(cells):
        table = np.zeros((len(freqs), len(cells)))
        live = np.zeros((len(freqs), len(cells)))
        for f, freq in enumerate(freqs):
            for n, cell in enumerate(cells):
                if freq is not None and cell is not None:
                    turns = (freq[0] * cell[0] % points_h) / points_h
                    turns += (freq[1] * cell[1] % points_w) / points_w
                    table[f, n] = 2.0 * np.pi * turns
                    live[f, n] = 1.0
        return table, live

    def interleave(real, imag):
        tiles = len(freqs) // SUB
        both_parts = np.stack(
            [real.reshape(tiles, SUB, -1), imag.reshape(tiles, SUB, -1)], axis=1
        )
        return both_parts.reshape(2 * len(freqs), -1)

    def analysis(cells, sign):
        angle, live = phases(cells)
        high, low = split_bf16(interleave(np.cos(angle) * live, sign * np.sin(angle) * live))
        return np.concatenate([high, low], axis=0)

    def synthesis(cells):
        angle, live = phases(cells)
        weight = np.array(
            [
                0.0 if f is None else (1.0 if f[1] in (0, points_w // 2) else 2.0)
                for f in freqs
            ]
        )[:, None] / (points_h * points_w)
        table = interleave(np.cos(angle) * weight * live, -np.sin(angle) * weight * live).T
        high, low = split_bf16(table)
        return np.concatenate([high, high, low], axis=1)

    def padded(h, w):
        inside = -HALF <= h < rows + HALF and -HALF <= w < width + HALF
        return (h + HALF, w + HALF) if inside else None

    columns = width + 2 * EDGE
    plane = []
    for s in range(columns // 2):
        for r in range(2 * SUB):
            plane.append(padded(r % SUB, s + columns // 2 * (r // SUB) - EDGE))
    slots = width // 2 + 2 * EDGE
    for s in range(slots):
        for r in range(2 * SUB):
            h = r % EDGE + (-EDGE if r < SUB else rows)
            top = r % SUB < EDGE
            if top:
                col = None if s < EDGE else (s if s < slots - EDGE else s + width // 2)
            else:
                col = None if s >= slots - EDGE else (s if s < EDGE else s + width // 2)
            plane.append(None if col is None else padded(h, col - EDGE))
    own = [
        (r % SUB, s + width // 2 * (r // SUB)) for s in range(width // 2) for r in range(2 * SUB)
    ]
    taps = [(j, k) if k < K else None for j in range(K) for k in range(SUB)]
    lags = [(n // K, n % K) if n < K * K else None for n in range(K * SUB)]
    return {
        "plane": analysis(plane, -1.0),
        "own": analysis(own, -1.0),
        "taps": analysis(taps, 1.0),
        "forward": synthesis(own),
        "backward": synthesis([(h + K - 1, w + K - 1) for h, w in own]),
        "lags": synthesis(lags),
    }


class Halo:
    def __init__(self, own, edges, main, side, sems, where, counts):
        self.own, self.edges, self.main, self.side = own, edges, main, side
        self.send, self.recv = sems
        self.grp, self.z, self.x, self.c = where
        self.nz, self.nx, self.nc = counts
        self.depth, self.lanes = own.shape[1], own.shape[3]
        self.edge_lanes = (self.main.shape[3] - self.lanes) // 2

    def inside(self, dz, dx, dc):
        z, x, c = self.z + dz, self.x + dx, self.c + dc
        return both(z >= 0, z < self.nz, x >= 0, x < self.nx, c >= 0, c < self.nc)

    def copy(self, crop, idx):
        dz, dx, dc = DIRS[idx]
        depth, lanes, edge = self.depth, self.lanes, self.edge_lanes
        src_d = {-1: slice(0, HALF), 0: slice(0, depth), 1: slice(depth - HALF, depth)}[dz]
        dst_d = {
            -1: slice(HALF + depth, 2 * HALF + depth),
            0: slice(HALF, HALF + depth),
            1: slice(0, HALF),
        }[dz]
        every = slice(None)
        full = lanes if dx == 0 else lanes // 2
        src_l = {-1: slice(0, edge), 0: slice(0, full), 1: slice(full - edge, full)}[dc]
        dst_l = {
            -1: slice(edge + full, 2 * edge + full),
            0: slice(edge, edge + full),
            1: slice(0, edge),
        }[dc]
        if dx == 0:
            src = self.own.at[crop, src_d, every, src_l]
            dst = self.main.at[crop, dst_d, every, dst_l]
        else:
            src = self.edges.at[0 if dx < 0 else 1, crop, src_d, every, src_l]
            dst = self.side.at[crop, 1 if dx < 0 else 0, dst_d, every, dst_l]
        return pltpu.make_async_remote_copy(
            src_ref=src,
            dst_ref=dst,
            send_sem=self.send.at[crop, idx],
            recv_sem=self.recv.at[crop, idx],
            device_id=(self.grp, self.z + dz, self.x + dx, self.c + dc),
            device_id_type=MESH,
        )

    def fill_edges(self):
        depth, edge = self.depth, self.edge_lanes

        def clear(cond, *areas):
            @pl.when(cond)
            def _():
                for ref, area in areas:
                    view = ref.at[area]
                    view[...] = jnp.zeros(view.shape, view.dtype)

        every = slice(None)
        low, high = slice(0, HALF), slice(HALF + depth, 2 * HALF + depth)
        main, side = self.main, self.side
        clear(self.z == 0, (main, (every, low)), (side, (every, every, low)))
        clear(self.z == self.nz - 1, (main, (every, high)), (side, (every, every, high)))
        clear(self.x == 0, (side, (every, 0)))
        clear(self.x == self.nx - 1, (side, (every, 1)))
        rest = (every, every, every)
        clear(self.c == 0, (main, rest + (slice(0, edge),)), (side, (every,) + rest + (slice(0, edge),)))
        clear(
            self.c == self.nc - 1,
            (main, rest + (slice(main.shape[3] - edge, main.shape[3]),)),
            (side, (every,) + rest + (slice(side.shape[4] - edge, side.shape[4]),)),
        )

    def cut_edges(self, crop):
        half = self.lanes // 2
        for d in range(self.depth):
            for which, first in enumerate((0, EDGE)):
                for part in range(2):
                    self.edges[which, crop, d, part * EDGE : (part + 1) * EDGE, :] = self.own[
                        crop, d, first : first + EDGE, part * half : (part + 1) * half
                    ]

    def start(self, crop):
        for idx, step in enumerate(DIRS):
            @pl.when(self.inside(*step))
            def _():
                self.copy(crop, idx).start()

    def centre(self, crop):
        depth, lanes, edge = self.depth, self.lanes, self.edge_lanes
        self.main[crop, HALF : HALF + depth, :, edge : edge + lanes] = self.own[crop]

    def arrive(self, crop):
        for idx, (dz, dx, dc) in enumerate(DIRS):
            @pl.when(self.inside(-dz, -dx, -dc))
            def _():
                self.copy(crop, idx).wait_recv()

    def finish(self, crop):
        for idx, step in enumerate(DIRS):
            @pl.when(self.inside(*step))
            def _():
                self.copy(crop, idx).wait_send()


def slot_slices(array, channels):
    return [array[:, s * channels : (s + 1) * channels] for s in range(array.shape[1] // channels)]


def gather_plane(main, side, crop, plane, xs, lane, channels):
    wide = main[crop, plane]
    half = wide.shape[1] // 2
    wide = jnp.concatenate([wide[:, :half], wide[:, half:]], axis=0)
    rim = jnp.concatenate([side[crop, 0, plane], side[crop, 1, plane]], axis=0)
    for n, cell in enumerate(slot_slices(wide, channels) + slot_slices(rim, channels)):
        xs[n * 2 * SUB : (n + 1) * 2 * SUB, lane : lane + channels] = cell


def spectra(main, side, crop, xs, table, out, channels):
    planes = main.shape[1]
    rows = out.shape[2]

    for pair in range(planes // 2):
        for q in range(2):
            gather_plane(main, side, crop, 2 * pair + q, xs.at[pair], q * LANES, channels)
        res = jnp.dot(table[...], xs[pair], preferred_element_type=jnp.float32)
        res = res[:rows] + res[rows:]
        for q in range(2):
            out[crop, 2 * pair + q] = res[:, q * LANES : (q + 1) * LANES]


def store_split(ref, tile, lane, re, im):
    value = jnp.concatenate([re, im], axis=0)
    high = value.astype(jnp.bfloat16)
    low = (value - high.astype(jnp.float32)).astype(jnp.bfloat16)
    rows = ref.shape[0] // 3
    for n, part in enumerate((high, low, high)):
        first = pl.multiple_of(tile * 2 * SUB, 2 * SUB) + n * rows
        ref[pl.ds(first, 2 * SUB), lane : lane + LANES] = part


def tile_of(ref, lead, tile):
    first = pl.multiple_of(tile * 2 * SUB, 2 * SUB)
    return ref[lead + (pl.ds(first, SUB),)], ref[lead + (pl.ds(first + SUB, SUB),)]


def conv_products(xhat, khat, crop, depth, yhat, flip):
    tiles = yhat.shape[0] // (3 * 2 * SUB)

    def step(tile, _):
        taps = [tile_of(khat, (i,), tile) for i in range(K)]
        data = [tile_of(xhat, (crop, p), tile) for p in range(depth + K - 1)]
        for d in range(depth):
            re = im = None
            for i in range(K):
                kr, ki = taps[i]
                xr, xi = data[d + K - 1 - i if flip else d + i]
                if flip:
                    a, b = xr * kr + xi * ki, xi * kr - xr * ki
                else:
                    a, b = xr * kr - xi * ki, xr * ki + xi * kr
                re, im = (a, b) if re is None else (re + a, im + b)
            store_split(yhat, tile, d * LANES, re, im)
        return 0

    lax.fori_loop(0, tiles, step, 0)


def lag_products(xhat, ohat, crops, depth, ghat):
    tiles = ghat.shape[0] // (3 * 2 * SUB)

    def step(tile, _):
        accs = [[None, None] for _ in range(K)]
        for crop in range(crops):
            data = [tile_of(xhat, (crop, p), tile) for p in range(depth + K - 1)]
            slope = [tile_of(ohat, (crop, d), tile) for d in range(depth)]
            for i in range(K):
                for d in range(depth):
                    xr, xi = data[d + i]
                    sr, si = slope[d]
                    a, b = xr * sr + xi * si, xi * sr - xr * si
                    acc = accs[i]
                    accs[i] = [a, b] if acc[0] is None else [acc[0] + a, acc[1] + b]
        for i in range(K):
            store_split(ghat, tile, i * LANES, accs[i][0], accs[i][1])
        return 0

    lax.fori_loop(0, tiles, step, 0)


def to_native(slots, channels):
    line = jnp.concatenate([slot[:, :channels] for slot in slots], axis=1)
    return jnp.concatenate([line[:SUB], line[SUB:]], axis=1)


def kernel(
    counts, channels, row_of,
    *refs,
):
    count = 16
    operands, (gi_hbm, full_hbm), staged, refs = (
        refs[:count], refs[count : count + 2], refs[count + 2 : 2 * count + 2], refs[2 * count + 2 :]
    )
    (
        x_raw, g_raw, kernel_ref, bias_ref, report_ref, fw_ref, fb_ref, ib_ref, inw_raw, outw_raw,
        f_plane, f_own, f_taps, s_fwd, s_bwd, s_lags,
    ) = staged
    (
    gi_ref, full, load_sems, out_sems,
    inw_ref, outw_ref, x_main, x_side, x_edges, s_own, s_main, s_side, s_edges,
    gs, xs, own_rhs, taps_s, khat, xhat, shat, ohat, yhat, ghat, conv_s,
    vec_ref, accw, accb, accf, part, part_low, band_low, inbox_c, inbox, mine,
    x_send, x_recv, sl_send, sl_recv,
    hv_send, hv_recv, rs_send, rs_recv, ag_send, ag_recv, sh_send, sh_recv,
    ) = refs
    nz, nx, nc = counts
    total = nz * nx * nc
    grp, z, x, c = (lax.axis_index(name) for name in ("groups", "depth", "rows", "cols"))
    me = (z * nx + x) * nc + c
    crops, depth = x_raw.shape[:2]
    hidden = inw_raw.shape[1]
    voxels = s_fwd.shape[0]
    bf, f32 = jnp.bfloat16, jnp.float32

    def peer(offset):
        other = lax.rem(me + offset, total)
        return other, (grp, other // (nx * nc), (other // nc) % nx, other % nc)

    loads = [
        pltpu.make_async_copy(src, dst, load_sems.at[n])
        for n, (src, dst) in enumerate(zip(operands, staged))
    ]
    for n in (0, 12, 2, 10, 1, 3, 4, 5, 6, 7, 8, 9, 13, 11, 15, 14):
        loads[n].start()
    barrier = pltpu.get_barrier_semaphore()

    def greet(offset, _):
        pl.semaphore_signal(barrier, inc=1, device_id=peer(offset)[1], device_id_type=MESH)
        return 0

    lax.fori_loop(1, total, greet, 0)
    where = (grp, z, x, c)
    halo_x = Halo(x_raw, x_edges, x_main, x_side, (x_send, x_recv), where, counts)
    halo_s = Halo(s_own, s_edges, s_main, s_side, (sl_send, sl_recv), where, counts)
    loads[0].wait()
    for crop in range(crops):
        halo_x.cut_edges(crop)
    pl.semaphore_wait(barrier, total - 1)
    for crop in range(crops):
        halo_x.start(crop)
    halo_x.fill_edges()
    halo_s.fill_edges()
    for crop in range(crops):
        halo_x.centre(crop)
    for n in (2, 12):
        loads[n].wait()
    spare = LANES - channels
    xs[...] = jnp.zeros_like(xs)
    gs[...] = jnp.zeros_like(gs)
    taps_s[...] = jnp.zeros_like(taps_s)
    for i in range(K):
        for j in range(K):
            taps_s[j * SUB : j * SUB + K, i * LANES : i * LANES + channels] = kernel_ref[
                i, j
            ].astype(f32)
    res = jnp.dot(f_taps[...], taps_s[...].astype(bf), preferred_element_type=f32)
    half = res.shape[0] // 2
    res = res[:half] + res[half:]
    for i in range(K):
        khat[i] = res[:, i * LANES : (i + 1) * LANES]
    for n in (1, 3, 4, 5, 6, 7, 8, 9):
        loads[n].wait()
    for raw, ready in ((inw_raw, inw_ref), (outw_raw, outw_ref)):
        ready[0:channels, :] = raw[...]
        ready[channels:, :] = jnp.zeros((spare, hidden), bf)
    for crop in range(crops):
        for d in range(depth):
            wide = g_raw[crop, d]
            middle = wide.shape[1] // 2
            wide = jnp.concatenate([wide[:, :middle], wide[:, middle:]], axis=0)
            for n, cell in enumerate(slot_slices(wide, channels)):
                first = n * 2 * SUB
                gs[crop, d, first : first + 2 * SUB, 0:channels] = cell
    vec_ref[...] = jnp.zeros_like(vec_ref)
    vec_ref[0:1, 0:channels] = bias_ref[...].reshape(1, channels)
    film = lax.dot_general(
        report_ref[...].astype(f32).reshape(1, report_ref.shape[0]).astype(bf), fw_ref[...],
        (((1,), (1,)), ((), ())), preferred_element_type=f32,
    )
    film = film + fb_ref[...].reshape(1, 2 * channels)
    vec_ref[1:2, 0:channels] = film[:, :channels] + 1.0
    vec_ref[2:3, 0:channels] = film[:, channels:]
    accw[...] = jnp.zeros_like(accw)
    accb[...] = jnp.zeros_like(accb)
    accf[...] = jnp.zeros_like(accf)
    tail = row_of["small"]
    part[tail:, :] = jnp.zeros((part.shape[0] - tail, LANES), f32)

    conv_bias, scale, shift = vec_ref[0:1, :], vec_ref[1:2, :], vec_ref[2:3, :]
    in_bias = ib_ref[...].reshape(1, hidden)
    for n in (10, 13, 11, 15, 14):
        loads[n].wait()
    real = lax.broadcasted_iota(jnp.int32, (1, LANES), 1) < channels

    def mlp(crop, d):
        conv = conv_s[d] + conv_bias
        mean = jnp.sum(conv, axis=1, keepdims=True) * (1.0 / channels)
        centred = jnp.where(real, conv - mean, 0.0)
        variance = jnp.sum(centred * centred, axis=1, keepdims=True) * (1.0 / channels)
        inverse = lax.rsqrt(variance + EPSILON)
        normed = centred * inverse
        hidden_in = (normed * scale + shift).astype(bf)
        grad = gs[crop, d]
        pre = jnp.dot(hidden_in, inw_ref[...], preferred_element_type=f32) + in_bias
        square = pre * pre
        th = jnp.tanh(GELU_C * (pre + 0.044715 * (square * pre)))
        act_low = (0.5 * pre * (1.0 + th)).astype(bf)
        slope_act = 0.5 * (1.0 + th) + 0.5 * pre * (1.0 - th * th) * (
            GELU_C * (1.0 + (3.0 * 0.044715) * square)
        )
        grad_act = jnp.dot(grad, outw_ref[...], preferred_element_type=f32)
        grad_pre = grad_act * slope_act
        grad_low = grad_pre.astype(bf)
        grad_hidden = lax.dot_general(
            grad_low, inw_ref[...], (((1,), (1,)), ((), ())), preferred_element_type=f32
        )
        over_voxels = (((0,), (0,)), ((), ()))
        accw[0] += lax.dot_general(hidden_in, grad_low, over_voxels, preferred_element_type=f32)
        accw[1] += lax.dot_general(grad, act_low, over_voxels, preferred_element_type=f32)
        accb[0:1, :] += jnp.sum(grad_pre, axis=0, keepdims=True)
        accf[1:2, :] += jnp.sum(grad_hidden * normed, axis=0, keepdims=True)
        accf[2:3, :] += jnp.sum(grad_hidden, axis=0, keepdims=True)
        grad_normed = grad_hidden * scale
        mean_g = jnp.sum(grad_normed, axis=1, keepdims=True) * (1.0 / channels)
        mean_gn = jnp.sum(grad_normed * normed, axis=1, keepdims=True) * (1.0 / channels)
        slope = ((grad_normed - mean_g - normed * mean_gn) * inverse).astype(bf)
        accf[0:1, :] += jnp.sum(slope.astype(f32), axis=0, keepdims=True)
        own_rhs[crop, d] = slope
        s_own[crop, d] = to_native(
            [slope[n * 2 * SUB : (n + 1) * 2 * SUB] for n in range(voxels // (2 * SUB))], channels
        )

    def forward(crop, _):
        halo_x.arrive(crop)
        spectra(x_main, x_side, crop, xs, f_plane, xhat, channels)
        conv_products(xhat, khat, crop, depth, yhat, False)
        conv = jnp.dot(s_fwd[...], yhat[...], preferred_element_type=f32)
        for d in range(depth):
            conv_s[d] = conv[:, d * LANES : (d + 1) * LANES]

        def each_plane(d, _):
            mlp(crop, d)
            return 0

        lax.fori_loop(0, depth, each_plane, 0)
        halo_s.cut_edges(crop)
        halo_s.start(crop)
        halo_s.centre(crop)
        return 0

    lax.fori_loop(0, crops, forward, 0)

    def own_spectra(step, _):
        crop, pair = step // (depth // 2), step % (depth // 2)
        rhs = jnp.concatenate([own_rhs[crop, 2 * pair], own_rhs[crop, 2 * pair + 1]], axis=1)
        res = jnp.dot(f_own[...], rhs, preferred_element_type=f32)
        res = res[: res.shape[0] // 2] + res[res.shape[0] // 2 :]
        for q in range(2):
            ohat[crop, 2 * pair + q] = res[:, q * LANES : (q + 1) * LANES]
        return 0

    lax.fori_loop(0, crops * depth // 2, own_spectra, 0)
    lag_products(xhat, ohat, crops, depth, ghat)
    lags = jnp.dot(s_lags[...], ghat[...], preferred_element_type=f32)
    stride = K * SUB
    for i in range(K):
        first = row_of["kernel"] + i * stride
        part[first : first + stride, :] = lags[:, i * LANES : (i + 1) * LANES]

    for which, name in enumerate(("in", "out")):
        for block in range(hidden // LANES):
            first = row_of[name] + block * channels
            part[first : first + channels, :] = accw[
                which, 0:channels, block * LANES : (block + 1) * LANES
            ]
    part[row_of["small"] : row_of["small"] + 3, :] = accf[0:3, :]
    for block in range(hidden // LANES):
        row = row_of["in_bias"] + block
        part[row : row + 1, :] = accb[0:1, block * LANES : (block + 1) * LANES]
    part_low[...] = part[...].astype(bf)

    squad = nz * nx
    seat = z * nx + x
    band = part.shape[0] // nc
    chunk = band // squad

    def aligned(first, size):
        return pl.ds(pl.multiple_of(first, size), size)

    def mate(offset):
        other = lax.rem(c + offset, nc)
        return other, (grp, z, x, other)

    def fellow(offset):
        other = lax.rem(seat + offset, squad)
        return other, (grp, other // nx, other % nx, c)

    def remote(src, dst, send, recv, device):
        return pltpu.make_async_remote_copy(
            src_ref=src, dst_ref=dst, send_sem=send, recv_sem=recv,
            device_id=device, device_id_type=MESH,
        )

    def halve(offset):
        other, device = mate(offset)
        return remote(
            part_low.at[aligned(other * band, band)], inbox_c.at[offset],
            hv_send.at[offset], hv_recv.at[offset], device,
        )

    def scatter(offset):
        other, device = fellow(offset)
        return remote(
            band_low.at[aligned(other * chunk, chunk)], inbox.at[offset],
            rs_send.at[offset], rs_recv.at[offset], device,
        )

    def chunk_of(seat_no, core):
        return aligned(core * band + seat_no * chunk, chunk)

    def spread(offset):
        return remote(
            mine, full.at[chunk_of(seat, c)],
            ag_send.at[offset], ag_recv.at[offset], fellow(offset)[1],
        )

    def arrived(offset):
        origin = lax.rem(seat + squad - offset, squad)
        return remote(
            mine, full.at[chunk_of(origin, c)],
            ag_send.at[offset], ag_recv.at[offset], fellow(offset)[1],
        )

    def share(offset, step):
        origin = lax.rem(seat + squad - offset, squad)
        rows = full.at[chunk_of(origin, c)]
        return remote(rows, rows, sh_send.at[step, offset], sh_recv.at[step, offset], mate(step)[1])

    def shared(offset, step):
        core = lax.rem(c + nc - step, nc)
        origin = lax.rem(seat + squad - offset, squad)
        rows = full.at[chunk_of(origin, core)]
        return remote(rows, rows, sh_send.at[step, offset], sh_recv.at[step, offset], mate(step)[1])

    def each(first, last, fn):
        def step(offset, _):
            fn(offset)
            return 0

        lax.fori_loop(first, last, step, 0)

    def slope_spectra(crop):
        halo_s.arrive(crop)
        spectra(s_main, s_side, crop, xs, f_plane, shat, channels)

    def backward(crop):
        conv_products(shat, khat, crop, depth, yhat, True)
        conv = jnp.dot(s_bwd[...], yhat[...], preferred_element_type=f32)
        for d in range(depth):
            total_in = gs[crop, d].astype(f32) + conv[:, d * LANES : (d + 1) * LANES]
            low = total_in.astype(bf)
            gi_ref[crop, d] = to_native(
                [low[n * 2 * SUB : (n + 1) * 2 * SUB] for n in range(voxels // (2 * SUB))],
                channels,
            )

    def gi_out(crop):
        return pltpu.make_async_copy(gi_ref.at[crop], gi_hbm.at[crop], out_sems.at[crop])

    def start_halves():
        each(1, nc, lambda offset: halve(offset).start())

    def start_scatter():
        each(1, nc, lambda offset: halve(offset).wait())
        my_band = aligned(c * band, band)
        acc = part[my_band, :]
        for offset in range(1, nc):
            acc = acc + inbox_c[offset].astype(f32)
        part[my_band, :] = acc
        band_low[...] = acc.astype(bf)
        each(1, squad, lambda offset: scatter(offset).start())

    def start_spread():
        each(1, squad, lambda offset: scatter(offset).wait())
        acc = part[chunk_of(seat, c), :]
        for offset in range(1, squad):
            acc = acc + inbox[offset].astype(f32)
        mine[...] = acc.astype(bf)
        full[chunk_of(seat, c), :] = mine[...]
        each(1, squad, lambda offset: spread(offset).start())
        each(1, nc, lambda step: share(0, step).start())

    def settle():
        def pass_on(offset):
            spread(offset).wait_send()
            arrived(offset).wait_recv()
            each(1, nc, lambda step: share(offset, step).start())

        each(1, squad, pass_on)

        def close(offset):
            def one(step):
                share(offset, step).wait_send()
                shared(offset, step).wait_recv()

            each(1, nc, one)

        each(0, squad, close)

    start_halves()
    slope_spectra(0)
    start_scatter()
    for crop in range(crops):
        backward(crop)
        gi_out(crop).start()
        if crop == 0:
            start_spread()
        if crop + 1 < crops:
            slope_spectra(crop + 1)
    settle()
    full_out = pltpu.make_async_copy(full, full_hbm, out_sems.at[crops])
    full_out.start()
    for crop in range(crops):
        halo_x.finish(crop)
        halo_s.finish(crop)
        gi_out(crop).wait()
    full_out.wait()


def finish_kernel(
    channels, row_of, factor, gi_in, full_in, gi_ref, gk_ref, gb_ref, gf_ref, ginw_ref, gib_ref, goutw_ref, gi_buf, full, red, sems
):
    load = pltpu.make_async_copy(gi_in, gi_buf, sems.at[0])
    load.start()
    fetch = pltpu.make_async_copy(full_in, full, sems.at[1])
    fetch.start()
    load.wait()
    pass_through = pltpu.make_async_copy(gi_buf, gi_ref, sems.at[2])
    pass_through.start()
    fetch.wait()
    hidden = ginw_ref.shape[1]
    red[...] = full[...].astype(jnp.float32) * factor
    for name, out_ref in (("in", ginw_ref), ("out", goutw_ref)):
        for block in range(hidden // LANES):
            first = row_of[name] + block * channels
            out_ref[:, block * LANES : (block + 1) * LANES] = red[first : first + channels, :]
    for i in range(K):
        for j in range(K):
            first = row_of["kernel"] + i * K * SUB + j * K
            gk_ref[i, j] = red[first : first + K, 0:channels].reshape(K, 1, channels)
    small = row_of["small"]
    gb_ref[...] = red[small : small + 1, 0:channels].reshape(channels)
    film = [red[small + n : small + n + 1, 0:channels] for n in (1, 2)]
    gf_ref[...] = jnp.concatenate(film, axis=1).reshape(2 * channels)
    rows = [red[small + 3 + n : small + 4 + n, :] for n in range(hidden // LANES)]
    gib_ref[...] = jnp.concatenate(rows, axis=1).reshape(hidden)
    pass_through.wait()


def local(
    counts, volume, grad_out, report, conv_kernel, conv_bias,
    film_weight, film_bias, in_weight, in_bias, out_weight,
):
    crops, slices, lines, merged = volume.shape
    channels = conv_kernel.shape[0]
    hidden = in_weight.shape[1]
    width = merged // channels
    raw_kernel = jnp.transpose(conv_kernel[:, 0], (1, 2, 3, 0))
    total = counts[0] * counts[1] * counts[2]
    blocks = hidden // LANES
    row_of = {"in": 0, "out": blocks * channels, "kernel": 2 * blocks * channels}
    row_of["small"] = row_of["kernel"] + K * K * SUB
    row_of["in_bias"] = row_of["small"] + 3
    row_of["end"] = row_of["in_bias"] + -(-(blocks + 3) // SUB) * SUB
    unit = 16 * total
    all_rows = -(-row_of["end"] // unit) * unit
    chunk = all_rows // total
    cores, squad = counts[2], counts[0] * counts[1]
    bf, f32 = jnp.bfloat16, jnp.float32
    dma = pltpu.SemaphoreType.DMA
    tables = fourier_tables(lines, width)
    names = ("plane", "own", "taps", "forward", "backward", "lags")
    spec = tables["plane"].shape[0] // 2
    planes = slices + 2 * HALF
    voxels = lines * width
    edge_lanes = EDGE * channels
    halves = merged // 2 + 2 * edge_lanes
    main = (crops, planes, lines, merged + 2 * edge_lanes)
    side = (crops, 2, planes, 2 * EDGE, halves)
    edges = (2, crops, slices, 2 * EDGE, merged // 2)
    factor = 1.0 / math.sqrt(crops * slices * voxels * total)
    operands = (
        volume,
        grad_out,
        raw_kernel,
        conv_bias,
        report,
        film_weight.T,
        film_bias,
        in_bias,
        in_weight,
        out_weight.T,
        *(tables[name] for name in names),
    )
    gathered = pl.pallas_call(
        functools.partial(kernel, counts, channels, row_of),
        out_shape=(
            jax.ShapeDtypeStruct(volume.shape, bf),
            jax.ShapeDtypeStruct((all_rows, LANES), bf),
        ),
        in_specs=[pl.BlockSpec(memory_space=pltpu.HBM)] * len(operands),
        out_specs=(pl.BlockSpec(memory_space=pltpu.HBM),) * 2,
        scratch_shapes=[pltpu.VMEM(a.shape, a.dtype) for a in operands]
        + [
            pltpu.VMEM(volume.shape, bf),
            pltpu.VMEM((all_rows, LANES), bf),
            dma((len(operands),)),
            dma((crops + 1,)),
            pltpu.VMEM((LANES, hidden), bf),
            pltpu.VMEM((LANES, hidden), bf),
            pltpu.VMEM(main, bf),
            pltpu.VMEM(side, bf),
            pltpu.VMEM(edges, bf),
            pltpu.VMEM(volume.shape, bf),
            pltpu.VMEM(main, bf),
            pltpu.VMEM(side, bf),
            pltpu.VMEM(edges, bf),
            pltpu.VMEM((crops, slices, voxels, LANES), bf),
            pltpu.VMEM((planes // 2, tables["plane"].shape[1], 2 * LANES), bf),
            pltpu.VMEM((crops, slices, voxels, LANES), bf),
            pltpu.VMEM((K * SUB, K * LANES), f32),
            pltpu.VMEM((K, spec, LANES), f32),
            pltpu.VMEM((crops, planes, spec, LANES), f32),
            pltpu.VMEM((crops, planes, spec, LANES), f32),
            pltpu.VMEM((crops, slices, spec, LANES), f32),
            pltpu.VMEM((3 * spec, slices * LANES), bf),
            pltpu.VMEM((3 * spec, K * LANES), bf),
            pltpu.VMEM((slices, voxels, LANES), f32),
            pltpu.VMEM((SUB, LANES), f32),
            pltpu.VMEM((2, LANES, hidden), f32),
            pltpu.VMEM((SUB, hidden), f32),
            pltpu.VMEM((SUB, LANES), f32),
            pltpu.VMEM((all_rows, LANES), f32),
            pltpu.VMEM((all_rows, LANES), bf),
            pltpu.VMEM((all_rows // cores, LANES), bf),
            pltpu.VMEM((cores, all_rows // cores, LANES), bf),
            pltpu.VMEM((squad, chunk, LANES), bf),
            pltpu.VMEM((chunk, LANES), bf),
        ]
        + [dma((crops, len(DIRS)))] * 4
        + [dma((cores,))] * 2
        + [dma((squad,))] * 4
        + [dma((cores, squad))] * 2,
        compiler_params=pltpu.CompilerParams(
            collective_id=0, has_side_effects=True, vmem_limit_bytes=60 * 1024 * 1024
        ),
        name="block",
    )(*operands)
    grad_input, grad_kernel, grad_bias, grad_film, grad_in_w, grad_in_b, grad_out_w = pl.pallas_call(
        functools.partial(finish_kernel, channels, row_of, factor),
        out_shape=(
            jax.ShapeDtypeStruct(volume.shape, bf),
            jax.ShapeDtypeStruct((K, K, K, 1, channels), f32),
            jax.ShapeDtypeStruct((channels,), f32),
            jax.ShapeDtypeStruct((2 * channels,), f32),
            jax.ShapeDtypeStruct((channels, hidden), f32),
            jax.ShapeDtypeStruct((hidden,), f32),
            jax.ShapeDtypeStruct((channels, hidden), f32),
        ),
        in_specs=[pl.BlockSpec(memory_space=pltpu.HBM)] * 2,
        out_specs=(pl.BlockSpec(memory_space=pltpu.HBM),) + (pl.BlockSpec(memory_space=pltpu.VMEM),) * 6,
        scratch_shapes=[
            pltpu.VMEM(volume.shape, bf),
            pltpu.VMEM((all_rows, LANES), bf),
            pltpu.VMEM((all_rows, LANES), f32),
            dma((3,)),
        ],
        compiler_params=pltpu.CompilerParams(vmem_limit_bytes=60 * 1024 * 1024),
        name="finish",
    )(*gathered)
    grad_kernel = jnp.transpose(grad_kernel, (4, 3, 0, 1, 2))
    return (
        grad_input, grad_kernel, grad_bias, grad_film, grad_in_w, grad_in_b, grad_out_w.T
    )


def solution(mesh):
    split = P("groups", "depth", "rows", "cols")
    in_specs = (split, split, P("groups")) + (P(),) * 7
    out_specs = (
        split,
        P("groups", None, None, None, None),
        P("groups"),
        P("groups"),
        P("groups", None),
        P("groups"),
        P("groups", None),
    )
    counts = tuple(mesh.shape[name] for name in ("depth", "rows", "cols"))
    return jax.shard_map(
        functools.partial(local, counts),
        mesh=mesh,
        in_specs=in_specs,
        out_specs=out_specs,
        check_vma=False,
    )
```

```python
import functools
import math

import jax
import jax.numpy as jnp
import numpy as np
from jax import lax
from jax.experimental import pallas as pl
from jax.experimental.pallas import tpu as pltpu
from jax.sharding import PartitionSpec as P

K = 7
HALF = K // 2
LANES = 128
SUB = 8
EDGE = 4
EPSILON = 1e-06
MESH = pl.DeviceIdType.MESH
GELU_C = math.sqrt(2.0 / math.pi)
DIRS = tuple(
    (dz, dx, dc)
    for dz in (-1, 0, 1)
    for dx in (-1, 0, 1)
    for dc in (-1, 0, 1)
    if (dz, dx, dc) != (0, 0, 0)
)


def both(*conds):
    out = conds[0]
    for cond in conds[1:]:
        out = jnp.logical_and(out, cond)
    return out


def split_bf16(array):
    high = array.astype(jnp.bfloat16)
    low = (array - high.astype(np.float64)).astype(jnp.bfloat16)
    return high, low


def fourier_tables(rows, width):
    points_h, points_w = rows + 2 * HALF, width + 2 * HALF
    half_w = points_w // 2 + 1
    freqs = [(a, b) for b in range(half_w) for a in range(points_h)]
    freqs += [None] * (-len(freqs) % SUB)

    def phases(cells):
        table = np.zeros((len(freqs), len(cells)))
        live = np.zeros((len(freqs), len(cells)))
        for f, freq in enumerate(freqs):
            for n, cell in enumerate(cells):
                if freq is not None and cell is not None:
                    turns = (freq[0] * cell[0] % points_h) / points_h
                    turns += (freq[1] * cell[1] % points_w) / points_w
                    table[f, n] = 2.0 * np.pi * turns
                    live[f, n] = 1.0
        return table, live

    def interleave(real, imag):
        tiles = len(freqs) // SUB
        both_parts = np.stack(
            [real.reshape(tiles, SUB, -1), imag.reshape(tiles, SUB, -1)], axis=1
        )
        return both_parts.reshape(2 * len(freqs), -1)

    def analysis(cells, sign):
        angle, live = phases(cells)
        high, low = split_bf16(interleave(np.cos(angle) * live, sign * np.sin(angle) * live))
        return np.concatenate([high, low], axis=0)

    def synthesis(cells):
        angle, live = phases(cells)
        weight = np.array(
            [
                0.0 if f is None else (1.0 if f[1] in (0, points_w // 2) else 2.0)
                for f in freqs
            ]
        )[:, None] / (points_h * points_w)
        table = interleave(np.cos(angle) * weight * live, -np.sin(angle) * weight * live).T
        high, low = split_bf16(table)
        return np.concatenate([high, high, low], axis=1)

    def padded(h, w):
        inside = -HALF <= h < rows + HALF and -HALF <= w < width + HALF
        return (h + HALF, w + HALF) if inside else None

    columns = width + 2 * EDGE
    plane = []
    for s in range(columns // 2):
        for r in range(2 * SUB):
            plane.append(padded(r % SUB, s + columns // 2 * (r // SUB) - EDGE))
    slots = width // 2 + 2 * EDGE
    for s in range(slots):
        for r in range(2 * SUB):
            h = r % EDGE + (-EDGE if r < SUB else rows)
            top = r % SUB < EDGE
            if top:
                col = None if s < EDGE else (s if s < slots - EDGE else s + width // 2)
            else:
                col = None if s >= slots - EDGE else (s if s < EDGE else s + width // 2)
            plane.append(None if col is None else padded(h, col - EDGE))
    own = [
        (r % SUB, s + width // 2 * (r // SUB)) for s in range(width // 2) for r in range(2 * SUB)
    ]
    taps = [(j, k) if k < K else None for j in range(K) for k in range(SUB)]
    lags = [(n // K, n % K) if n < K * K else None for n in range(K * SUB)]
    return {
        "plane": analysis(plane, -1.0),
        "own": analysis(own, -1.0),
        "taps": analysis(taps, 1.0),
        "forward": synthesis(own),
        "backward": synthesis([(h + K - 1, w + K - 1) for h, w in own]),
        "lags": synthesis(lags),
    }


class Halo:
    def __init__(self, own, edges, main, side, sems, where, counts):
        self.own, self.edges, self.main, self.side = own, edges, main, side
        self.send, self.recv = sems
        self.grp, self.z, self.x, self.c = where
        self.nz, self.nx, self.nc = counts
        self.depth, self.lanes = own.shape[1], own.shape[3]
        self.edge_lanes = (self.main.shape[3] - self.lanes) // 2

    def inside(self, dz, dx, dc):
        z, x, c = self.z + dz, self.x + dx, self.c + dc
        return both(z >= 0, z < self.nz, x >= 0, x < self.nx, c >= 0, c < self.nc)

    def copy(self, crop, idx):
        dz, dx, dc = DIRS[idx]
        depth, lanes, edge = self.depth, self.lanes, self.edge_lanes
        src_d = {-1: slice(0, HALF), 0: slice(0, depth), 1: slice(depth - HALF, depth)}[dz]
        dst_d = {
            -1: slice(HALF + depth, 2 * HALF + depth),
            0: slice(HALF, HALF + depth),
            1: slice(0, HALF),
        }[dz]
        every = slice(None)
        full = lanes if dx == 0 else lanes // 2
        src_l = {-1: slice(0, edge), 0: slice(0, full), 1: slice(full - edge, full)}[dc]
        dst_l = {
            -1: slice(edge + full, 2 * edge + full),
            0: slice(edge, edge + full),
            1: slice(0, edge),
        }[dc]
        if dx == 0:
            src = self.own.at[crop, src_d, every, src_l]
            dst = self.main.at[crop, dst_d, every, dst_l]
        else:
            src = self.edges.at[0 if dx < 0 else 1, crop, src_d, every, src_l]
            dst = self.side.at[crop, 1 if dx < 0 else 0, dst_d, every, dst_l]
        return pltpu.make_async_remote_copy(
            src_ref=src,
            dst_ref=dst,
            send_sem=self.send.at[crop, idx],
            recv_sem=self.recv.at[crop, idx],
            device_id=(self.grp, self.z + dz, self.x + dx, self.c + dc),
            device_id_type=MESH,
        )

    def fill_edges(self):
        depth, edge = self.depth, self.edge_lanes

        def clear(cond, *areas):
            @pl.when(cond)
            def _():
                for ref, area in areas:
                    view = ref.at[area]
                    view[...] = jnp.zeros(view.shape, view.dtype)

        every = slice(None)
        low, high = slice(0, HALF), slice(HALF + depth, 2 * HALF + depth)
        main, side = self.main, self.side
        clear(self.z == 0, (main, (every, low)), (side, (every, every, low)))
        clear(self.z == self.nz - 1, (main, (every, high)), (side, (every, every, high)))
        clear(self.x == 0, (side, (every, 0)))
        clear(self.x == self.nx - 1, (side, (every, 1)))
        rest = (every, every, every)
        clear(self.c == 0, (main, rest + (slice(0, edge),)), (side, (every,) + rest + (slice(0, edge),)))
        clear(
            self.c == self.nc - 1,
            (main, rest + (slice(main.shape[3] - edge, main.shape[3]),)),
            (side, (every,) + rest + (slice(side.shape[4] - edge, side.shape[4]),)),
        )

    def cut_edges(self, crop):
        half = self.lanes // 2
        for d in range(self.depth):
            for which, first in enumerate((0, EDGE)):
                for part in range(2):
                    self.edges[which, crop, d, part * EDGE : (part + 1) * EDGE, :] = self.own[
                        crop, d, first : first + EDGE, part * half : (part + 1) * half
                    ]

    def start(self, crop, inner):
        for idx, step in enumerate(DIRS):
            if inner != (step[0] == 0):
                continue

            @pl.when(self.inside(*step))
            def _():
                self.copy(crop, idx).start()

    def centre(self, crop):
        depth, lanes, edge = self.depth, self.lanes, self.edge_lanes
        self.main[crop, HALF : HALF + depth, :, edge : edge + lanes] = self.own[crop]

    def arrive(self, crop, inner):
        for idx, (dz, dx, dc) in enumerate(DIRS):
            if inner != (dz == 0):
                continue

            @pl.when(self.inside(-dz, -dx, -dc))
            def _():
                self.copy(crop, idx).wait_recv()

    def finish(self, crop):
        for idx, step in enumerate(DIRS):
            @pl.when(self.inside(*step))
            def _():
                self.copy(crop, idx).wait_send()


def wrap(index, extent):
    return jnp.where(index >= extent, index - extent, index)


def digits(offset, extent):
    if isinstance(offset, int):
        return divmod(offset, extent)
    return offset // extent, lax.rem(offset, extent)


def each(first, last, fn):
    if last - first <= 2 * SUB:
        for offset in range(first, last):
            fn(offset)
        return

    def step(offset, _):
        fn(offset)
        return 0

    lax.fori_loop(first, last, step, 0)


class Reduction:
    def __init__(self, part, bufs, sems, full, where, counts):
        self.part, self.full = part, full
        self.low, self.band_low, self.inbox_c, self.inbox, self.mine = bufs
        self.hv, self.rs, self.ag, self.sh = sems
        self.grp, self.z, self.x, self.c = where
        self.nz, self.nx, self.nc = counts
        self.squad = self.nz * self.nx
        self.seat = self.z * self.nx + self.x
        self.band = part.shape[0] // self.nc
        self.chunk = self.band // self.squad

    def mate(self, offset):
        other = wrap(self.c + offset, self.nc)
        return other, (self.grp, self.z, self.x, other)

    def fellow(self, offset):
        dz, dx = digits(offset, self.nx)
        other_z, other_x = wrap(self.z + dz, self.nz), wrap(self.x + dx, self.nx)
        return other_z * self.nx + other_x, (self.grp, other_z, other_x, self.c)

    def remote(self, src, dst, sems, idx, device):
        return pltpu.make_async_remote_copy(
            src_ref=src, dst_ref=dst, send_sem=sems[0].at[idx], recv_sem=sems[1].at[idx],
            device_id=device, device_id_type=MESH,
        )

    def rows(self, seat, core):
        return pl.ds(core * self.band + seat * self.chunk, self.chunk)

    def origin(self, offset):
        dz, dx = digits(offset, self.nx)
        from_z = wrap(self.z + self.nz - dz, self.nz)
        return from_z * self.nx + wrap(self.x + self.nx - dx, self.nx)

    def halve(self, offset):
        other, device = self.mate(offset)
        src = self.low.at[pl.ds(other * self.band, self.band)]
        return self.remote(src, self.inbox_c.at[offset], self.hv, offset, device)

    def scatter(self, offset):
        other, device = self.fellow(offset)
        src = self.band_low.at[pl.ds(other * self.chunk, self.chunk)]
        return self.remote(src, self.inbox.at[offset], self.rs, offset, device)

    def spread(self, offset, seat):
        dst = self.full.at[self.rows(seat, self.c)]
        return self.remote(self.mine, dst, self.ag, offset, self.fellow(offset)[1])

    def share(self, offset, step, core):
        view = self.full.at[self.rows(self.origin(offset), core)]
        sems = [sem.at[step] for sem in self.sh]
        return self.remote(view, view, sems, offset, self.mate(step)[1])

    def start_halves(self):
        self.low[...] = self.part[...].astype(jnp.bfloat16)
        each(1, self.nc, lambda offset: self.halve(offset).start())

    def start_scatter(self):
        each(1, self.nc, lambda offset: self.halve(offset).wait())
        band = pl.ds(self.c * self.band, self.band)
        acc = self.part[band]
        for offset in range(1, self.nc):
            acc = acc + self.inbox_c[offset].astype(jnp.float32)
        self.part[band] = acc
        self.band_low[...] = acc.astype(jnp.bfloat16)
        each(1, self.squad, lambda offset: self.scatter(offset).start())

    def start_spread(self):
        each(1, self.squad, lambda offset: self.scatter(offset).wait())

        def add(offset, acc):
            return acc + self.inbox[offset].astype(jnp.float32)

        acc = self.part[self.rows(self.seat, self.c)]
        if self.squad <= 2 * SUB:
            for offset in range(1, self.squad):
                acc = add(offset, acc)
        else:
            acc = lax.fori_loop(1, self.squad, add, acc)
        self.mine[...] = acc.astype(jnp.bfloat16)
        self.full[self.rows(self.seat, self.c)] = self.mine[...]
        each(1, self.squad, lambda offset: self.spread(offset, self.seat).start())
        each(1, self.nc, lambda step: self.share(0, step, self.c).start())

    def start_share(self):
        def pass_on(offset):
            self.spread(offset, self.origin(offset)).wait_recv()
            each(1, self.nc, lambda step: self.share(offset, step, self.c).start())

        each(1, self.squad, pass_on)

    def settle(self):
        each(1, self.squad, lambda offset: self.spread(offset, self.seat).wait_send())

        def close(offset):
            def one(step):
                self.share(offset, step, self.c).wait_send()
                core = wrap(self.c + self.nc - step, self.nc)
                self.share(offset, step, core).wait_recv()

            each(1, self.nc, one)

        each(0, self.squad, close)


def slot_slices(array, channels):
    return [array[:, s * channels : (s + 1) * channels] for s in range(array.shape[1] // channels)]


def gather_plane(main, side, crop, plane, xs, lane, channels):
    wide = main[crop, plane]
    half = wide.shape[1] // 2
    wide = jnp.concatenate([wide[:, :half], wide[:, half:]], axis=0)
    rim = jnp.concatenate([side[crop, 0, plane], side[crop, 1, plane]], axis=0)
    for n, cell in enumerate(slot_slices(wide, channels) + slot_slices(rim, channels)):
        xs[n * 2 * SUB : (n + 1) * 2 * SUB, lane : lane + channels] = cell


def spectra(halo, crop, xs, table, out, channels, then=None):
    depth, rows = halo.depth, out.shape[2]
    own = list(range(HALF, HALF + depth))
    order = own + [p for p in range(depth + 2 * HALF) if p not in own]
    halo.arrive(crop, True)
    if then is not None:
        then()
    for pair in range(len(order) // 2):
        planes = order[2 * pair : 2 * pair + 2]
        if pair == depth // 2:
            halo.arrive(crop, False)
        for q, plane in enumerate(planes):
            gather_plane(halo.main, halo.side, crop, plane, xs.at[pair], q * LANES, channels)
        res = jnp.dot(table[...], xs[pair], preferred_element_type=jnp.float32)
        res = res[:rows] + res[rows:]
        for q, plane in enumerate(planes):
            out[crop, plane] = res[:, q * LANES : (q + 1) * LANES]


def store_split(ref, tile, lane, re, im):
    value = jnp.concatenate([re, im], axis=0)
    high = value.astype(jnp.bfloat16)
    low = (value - high.astype(jnp.float32)).astype(jnp.bfloat16)
    rows = ref.shape[0] // 3
    for n, part in enumerate((high, low, high)):
        first = pl.multiple_of(tile * 2 * SUB, 2 * SUB) + n * rows
        ref[pl.ds(first, 2 * SUB), lane : lane + LANES] = part


def tile_of(ref, lead, tile):
    first = pl.multiple_of(tile * 2 * SUB, 2 * SUB)
    return ref[lead + (pl.ds(first, SUB),)], ref[lead + (pl.ds(first + SUB, SUB),)]


def conv_products(xhat, khat, crop, depth, yhat, flip):
    tiles = yhat.shape[0] // (3 * 2 * SUB)

    def step(tile, _):
        taps = [tile_of(khat, (i,), tile) for i in range(K)]
        data = [tile_of(xhat, (crop, p), tile) for p in range(depth + K - 1)]
        for d in range(depth):
            re = im = None
            for i in range(K):
                kr, ki = taps[i]
                xr, xi = data[d + K - 1 - i if flip else d + i]
                if flip:
                    a, b = xr * kr + xi * ki, xi * kr - xr * ki
                else:
                    a, b = xr * kr - xi * ki, xr * ki + xi * kr
                re, im = (a, b) if re is None else (re + a, im + b)
            store_split(yhat, tile, d * LANES, re, im)
        return 0

    lax.fori_loop(0, tiles, step, 0)


def lag_products(xhat, ohat, crops, depth, ghat):
    tiles = ghat.shape[0] // (3 * 2 * SUB)

    def step(tile, _):
        accs = [[None, None] for _ in range(K)]
        for crop in range(crops):
            data = [tile_of(xhat, (crop, p), tile) for p in range(depth + K - 1)]
            slope = [tile_of(ohat, (crop, d), tile) for d in range(depth)]
            for i in range(K):
                for d in range(depth):
                    xr, xi = data[d + i]
                    sr, si = slope[d]
                    a, b = xr * sr + xi * si, xi * sr - xr * si
                    acc = accs[i]
                    accs[i] = [a, b] if acc[0] is None else [acc[0] + a, acc[1] + b]
        for i in range(K):
            store_split(ghat, tile, i * LANES, accs[i][0], accs[i][1])
        return 0

    lax.fori_loop(0, tiles, step, 0)


def to_native(slots, channels):
    line = jnp.concatenate([slot[:, :channels] for slot in slots], axis=1)
    return jnp.concatenate([line[:SUB], line[SUB:]], axis=1)


def kernel(
    counts, channels, row_of,
    *refs,
):
    count = 16
    operands, (gi_hbm, full_hbm), staged, refs = (
        refs[:count], refs[count : count + 2], refs[count + 2 : 2 * count + 2], refs[2 * count + 2 :]
    )
    (
        x_raw, g_raw, kernel_ref, bias_ref, report_ref, fw_ref, fb_ref, ib_ref, inw_raw, outw_raw,
        f_plane, f_own, f_taps, s_fwd, s_bwd, s_lags,
    ) = staged
    (
    gi_ref, full, load_sems, out_sems,
    inw_ref, outw_ref, x_main, x_side, x_edges, s_own, s_main, s_side, s_edges,
    gs, xs, own_rhs, taps_s, khat, xhat, shat, ohat, yhat, ghat, conv_s,
    vec_ref, norm_s, inv_s, hid_s, pre_s, act_s, act_low, gpre_low, accb, accf, part, part_low, band_low, inbox_c, inbox, mine, taps_part,
    x_send, x_recv, sl_send, sl_recv,
    hv_send, hv_recv, rs_send, rs_recv, ag_send, ag_recv, sh_send, sh_recv,
    ) = refs
    nz, nx, nc = counts
    total = nz * nx * nc
    grp, z, x, c = (lax.axis_index(name) for name in ("groups", "depth", "rows", "cols"))
    crops, depth = x_raw.shape[:2]
    hidden = inw_raw.shape[1]
    voxels = s_fwd.shape[0]
    bf, f32 = jnp.bfloat16, jnp.float32

    def peer(offset):
        rest, dc = digits(offset, nc)
        dz, dx = digits(rest, nx)
        return grp, wrap(z + dz, nz), wrap(x + dx, nx), wrap(c + dc, nc)

    loads = [
        pltpu.make_async_copy(src, dst, load_sems.at[n])
        for n, (src, dst) in enumerate(zip(operands, staged))
    ]
    for n in (0, 12, 2, 10, 1, 3, 4, 5, 6, 7, 8, 9, 13, 11, 15, 14):
        loads[n].start()
    barrier = pltpu.get_barrier_semaphore()

    each(
        1, total,
        lambda offset: pl.semaphore_signal(
            barrier, inc=1, device_id=peer(offset), device_id_type=MESH
        ),
    )
    where = (grp, z, x, c)
    halo_x = Halo(x_raw, x_edges, x_main, x_side, (x_send, x_recv), where, counts)
    halo_s = Halo(s_own, s_edges, s_main, s_side, (sl_send, sl_recv), where, counts)
    loads[0].wait()
    for crop in range(crops):
        halo_x.cut_edges(crop)
    pl.semaphore_wait(barrier, total - 1)
    halo_x.start(0, True)
    halo_x.start(0, False)
    halo_x.fill_edges()
    halo_s.fill_edges()
    for crop in range(crops):
        halo_x.centre(crop)
    for n in (2, 12):
        loads[n].wait()
    spare = LANES - channels
    xs[...] = jnp.zeros_like(xs)
    gs[...] = jnp.zeros_like(gs)
    taps_s[...] = jnp.zeros_like(taps_s)
    for i in range(K):
        for j in range(K):
            taps_s[j * SUB : j * SUB + K, i * LANES : i * LANES + channels] = kernel_ref[
                i, j
            ].astype(f32)
    res = jnp.dot(f_taps[...], taps_s[...].astype(bf), preferred_element_type=f32)
    half = res.shape[0] // 2
    res = res[:half] + res[half:]
    for i in range(K):
        khat[i] = res[:, i * LANES : (i + 1) * LANES]
    for n in (1, 3, 4, 5, 6, 7, 8, 9):
        loads[n].wait()
    for raw, ready in ((inw_raw, inw_ref), (outw_raw, outw_ref)):
        ready[0:channels, :] = raw[...]
        ready[channels:, :] = jnp.zeros((spare, hidden), bf)
    for crop in range(crops):
        for d in range(depth):
            wide = g_raw[crop, d]
            middle = wide.shape[1] // 2
            wide = jnp.concatenate([wide[:, :middle], wide[:, middle:]], axis=0)
            for n, cell in enumerate(slot_slices(wide, channels)):
                first = n * 2 * SUB
                gs[crop, d, first : first + 2 * SUB, 0:channels] = cell
    vec_ref[...] = jnp.zeros_like(vec_ref)
    vec_ref[0:1, 0:channels] = bias_ref[...].reshape(1, channels)
    film = lax.dot_general(
        report_ref[...].astype(f32).reshape(1, report_ref.shape[0]).astype(bf), fw_ref[...],
        (((1,), (1,)), ((), ())), preferred_element_type=f32,
    )
    film = film + fb_ref[...].reshape(1, 2 * channels)
    vec_ref[1:2, 0:channels] = film[:, :channels] + 1.0
    vec_ref[2:3, 0:channels] = film[:, channels:]
    accb[...] = jnp.zeros_like(accb)
    accf[...] = jnp.zeros_like(accf)
    tail = row_of["small"] // SUB
    part[tail:] = jnp.zeros((part.shape[0] - tail, SUB, LANES), f32)
    taps_part[...] = jnp.zeros_like(taps_part)

    conv_bias, scale, shift = vec_ref[0:1, :], vec_ref[1:2, :], vec_ref[2:3, :]
    in_bias = ib_ref[...].reshape(1, hidden)
    for n in (10, 13, 11, 15, 14):
        loads[n].wait()
    real = lax.broadcasted_iota(jnp.int32, (1, LANES), 1) < channels

    inner = GELU_C
    outer = GELU_C * 0.044715

    def normalise(crop, d):
        conv = conv_s[d] + conv_bias
        mean = jnp.sum(conv, axis=1, keepdims=True) * (1.0 / channels)
        centred = jnp.where(real, conv - mean, 0.0)
        variance = jnp.sum(centred * centred, axis=1, keepdims=True) * (1.0 / channels)
        inverse = lax.rsqrt(variance + EPSILON)
        normed = centred * inverse
        first = d * voxels
        norm_s[first : first + voxels] = normed
        inv_s[first : first + voxels] = jnp.broadcast_to(inverse, (voxels, LANES))
        hid_s[crop, first : first + voxels] = (normed * scale + shift).astype(bf)

    def activate(crop, d):
        rows = slice(d * voxels, (d + 1) * voxels)
        pre_s[...] = jnp.dot(hid_s[crop, rows], inw_ref[...], preferred_element_type=f32)
        act_s[...] = jnp.dot(gs[crop, d], outw_ref[...], preferred_element_type=f32)
        sums = jnp.zeros((2 * SUB, hidden), f32)
        for n in range(voxels // (2 * SUB)):
            part_rows = slice(n * 2 * SUB, (n + 1) * 2 * SUB)
            out_rows = slice(d * voxels + n * 2 * SUB, d * voxels + (n + 1) * 2 * SUB)
            pre = pre_s[part_rows] + in_bias
            square = pre * pre
            half = 0.5 * jnp.tanh(pre * (inner + outer * square)) + 0.5
            act = pre * half
            act_low[crop, out_rows] = act.astype(bf)
            slope_act = half + act * (1.0 - half) * (2.0 * inner + (6.0 * outer) * square)
            grad_pre = act_s[part_rows] * slope_act
            gpre_low[crop, out_rows] = grad_pre.astype(bf)
            sums = sums + grad_pre
        accb[...] += sums[:SUB] + sums[SUB:]

    def settle_slope(crop, d):
        rows = slice(d * voxels, (d + 1) * voxels)
        grad_hidden = lax.dot_general(
            gpre_low[crop, rows], inw_ref[...], (((1,), (1,)), ((), ())),
            preferred_element_type=f32,
        )
        normed = norm_s[rows]
        product = grad_hidden * normed
        accf[1] += jnp.sum(product.reshape(voxels // SUB, SUB, LANES), axis=0)
        accf[2] += jnp.sum(grad_hidden.reshape(voxels // SUB, SUB, LANES), axis=0)
        mean_g = jnp.sum(grad_hidden * scale, axis=1, keepdims=True) * (1.0 / channels)
        mean_gn = jnp.sum(product * scale, axis=1, keepdims=True) * (1.0 / channels)
        slope = (grad_hidden * scale - mean_g - normed * mean_gn) * inv_s[rows]
        slope = slope.astype(bf)
        accf[0] += jnp.sum(slope.astype(f32).reshape(voxels // SUB, SUB, LANES), axis=0)
        own_rhs[crop, d] = slope
        s_own[crop, d] = to_native(
            [slope[n * 2 * SUB : (n + 1) * 2 * SUB] for n in range(voxels // (2 * SUB))], channels
        )

    def mlp(crop):
        for stage in (normalise, activate, settle_slope):
            for d in range(depth):
                stage(crop, d)

    def forward(crop, _):
        def next_crop():
            @pl.when(crop + 1 < crops)
            def _():
                halo_x.start(crop + 1, True)
                halo_x.start(crop + 1, False)

        spectra(halo_x, crop, xs, f_plane, xhat, channels, next_crop)
        conv_products(xhat, khat, crop, depth, yhat, False)
        conv = jnp.dot(s_fwd[...], yhat[...], preferred_element_type=f32)
        for d in range(depth):
            conv_s[d] = conv[:, d * LANES : (d + 1) * LANES]

        mlp(crop)
        halo_s.cut_edges(crop)
        halo_s.start(crop, True)
        halo_s.start(crop, False)
        halo_s.centre(crop)
        return 0

    lax.fori_loop(0, crops, forward, 0)

    def own_spectra(step, _):
        crop, pair = step // (depth // 2), step % (depth // 2)
        rhs = jnp.concatenate([own_rhs[crop, 2 * pair], own_rhs[crop, 2 * pair + 1]], axis=1)
        res = jnp.dot(f_own[...], rhs, preferred_element_type=f32)
        res = res[: res.shape[0] // 2] + res[res.shape[0] // 2 :]
        for q in range(2):
            ohat[crop, 2 * pair + q] = res[:, q * LANES : (q + 1) * LANES]
        return 0

    bufs = (part_low, band_low, inbox_c, inbox, mine)
    first_sems = ((hv_send, hv_recv), (rs_send, rs_recv), (ag_send, ag_recv), (sh_send, sh_recv))
    dense = Reduction(part, bufs, first_sems, full, where, counts)
    def slope_spectra(crop):
        spectra(halo_s, crop, xs, f_plane, shat, channels)

    def backward(crop):
        conv_products(shat, khat, crop, depth, yhat, True)
        conv = jnp.dot(s_bwd[...], yhat[...], preferred_element_type=f32)
        for d in range(depth):
            total_in = gs[crop, d].astype(f32) + conv[:, d * LANES : (d + 1) * LANES]
            low = total_in.astype(bf)
            gi_ref[crop, d] = to_native(
                [low[n * 2 * SUB : (n + 1) * 2 * SUB] for n in range(voxels // (2 * SUB))],
                channels,
            )

    def gi_out(crop):
        return pltpu.make_async_copy(gi_ref.at[crop], gi_hbm.at[crop], out_sems.at[crop])

    over_voxels = (((0,), (0,)), ((), ()))
    everything = crops * depth * voxels
    for name, left, right in (
        ("in", hid_s[...].reshape(everything, LANES), gpre_low[...].reshape(everything, hidden)),
        ("out", gs[...].reshape(everything, LANES), act_low[...].reshape(everything, hidden)),
    ):
        grads = lax.dot_general(left, right, over_voxels, preferred_element_type=f32)
        for block in range(hidden // LANES):
            first = row_of[name] + block * channels
            piece = grads[0:channels, block * LANES : (block + 1) * LANES]
            part[first // SUB : (first + channels) // SUB] = piece.reshape(
                channels // SUB, SUB, LANES
            )
    for n in range(3):
        row = row_of["small"] + n
        part[row // SUB, row % SUB : row % SUB + 1, :] = jnp.sum(accf[n], axis=0, keepdims=True)
    for block in range(hidden // LANES):
        row = row_of["in_bias"] + block
        part[row // SUB, row % SUB : row % SUB + 1, :] = jnp.sum(
            accb[:, block * LANES : (block + 1) * LANES], axis=0, keepdims=True
        )
    lax.fori_loop(0, crops * depth // 2, own_spectra, 0)
    lag_products(xhat, ohat, crops, depth, ghat)
    lags = jnp.dot(s_lags[...], ghat[...], preferred_element_type=f32)
    for i in range(K):
        rows_i = lags[0 : K * K, i * LANES : (i + 1) * LANES]
        taps_part[i * K * K : (i + 1) * K * K, :] = rows_i
    first_tap = row_of["kernel"] // SUB
    part[first_tap : first_tap + taps_part.shape[0] // SUB] = taps_part[...].reshape(
        taps_part.shape[0] // SUB, SUB, LANES
    )
    dense.start_halves()
    slope_spectra(0)
    dense.start_scatter()
    backward(0)
    gi_out(0).start()
    dense.start_spread()
    for crop in range(1, crops):
        slope_spectra(crop)
        backward(crop)
        gi_out(crop).start()
    dense.start_share()
    dense.settle()
    full_out = pltpu.make_async_copy(full, full_hbm, out_sems.at[crops])
    full_out.start()
    for crop in range(crops):
        halo_x.finish(crop)
        halo_s.finish(crop)
        gi_out(crop).wait()
    full_out.wait()


def finish_kernel(
    channels, row_of, factor,
    gi_in, dense_in,
    gi_ref, gk_ref, gb_ref, gf_ref, ginw_ref, gib_ref, goutw_ref,
    gi_buf, dense, red, sems,
):
    load = pltpu.make_async_copy(gi_in, gi_buf, sems.at[0])
    fetch = pltpu.make_async_copy(dense_in, dense, sems.at[1])
    for copy in (load, fetch):
        copy.start()
    load.wait()
    pass_through = pltpu.make_async_copy(gi_buf, gi_ref, sems.at[2])
    pass_through.start()
    fetch.wait()
    hidden = ginw_ref.shape[1]
    for name, out_ref in (("in", ginw_ref), ("out", goutw_ref)):
        for block in range(hidden // LANES):
            first = (row_of[name] + block * channels) // SUB
            piece = dense[first : first + channels // SUB].astype(jnp.float32) * factor
            out_ref[:, block * LANES : (block + 1) * LANES] = piece.reshape(channels, LANES)
    small = row_of["small"] // SUB
    rows = dense[small].astype(jnp.float32) * factor
    gb_ref[...] = rows[0:1, 0:channels].reshape(channels)
    film = [rows[n : n + 1, 0:channels] for n in (1, 2)]
    gf_ref[...] = jnp.concatenate(film, axis=1).reshape(2 * channels)
    lines = [rows[3 + n : 4 + n, :] for n in range(hidden // LANES)]
    gib_ref[...] = jnp.concatenate(lines, axis=1).reshape(hidden)
    first_tap = row_of["kernel"] // SUB
    taps = dense[first_tap : first_tap + red.shape[0] // SUB].astype(jnp.float32)
    red[...] = taps.reshape(red.shape) * factor
    for i in range(K):
        for j in range(K):
            first = (i * K + j) * K
            gk_ref[i, j] = red[first : first + K, 0:channels].reshape(K, 1, channels)
    pass_through.wait()


def local(
    counts, volume, grad_out, report, conv_kernel, conv_bias,
    film_weight, film_bias, in_weight, in_bias, out_weight,
):
    crops, slices, lines, merged = volume.shape
    channels = conv_kernel.shape[0]
    hidden = in_weight.shape[1]
    width = merged // channels
    raw_kernel = jnp.transpose(conv_kernel[:, 0], (1, 2, 3, 0))
    total = counts[0] * counts[1] * counts[2]
    blocks = hidden // LANES
    row_of = {"in": 0, "out": blocks * channels, "small": 2 * blocks * channels}
    row_of["in_bias"] = row_of["small"] + 3
    cores, squad = counts[2], counts[0] * counts[1]
    row_of["kernel"] = -(-(row_of["in_bias"] + blocks) // SUB) * SUB
    taps_rows = -(-K * K * K // SUB) * SUB
    dense_tiles = -(-(row_of["kernel"] + taps_rows) // (SUB * total)) * total
    bf, f32 = jnp.bfloat16, jnp.float32
    dma = pltpu.SemaphoreType.DMA
    tables = fourier_tables(lines, width)
    names = ("plane", "own", "taps", "forward", "backward", "lags")
    spec = tables["plane"].shape[0] // 2
    planes = slices + 2 * HALF
    voxels = lines * width
    edge_lanes = EDGE * channels
    halves = merged // 2 + 2 * edge_lanes
    main = (crops, planes, lines, merged + 2 * edge_lanes)
    side = (crops, 2, planes, 2 * EDGE, halves)
    edges = (2, crops, slices, 2 * EDGE, merged // 2)
    factor = 1.0 / math.sqrt(crops * slices * voxels * total)
    def reduce_buffers(tiles):
        band, chunk = tiles // cores, tiles // total
        return [
            pltpu.VMEM((tiles, SUB, LANES), f32),
            pltpu.VMEM((tiles, SUB, LANES), bf),
            pltpu.VMEM((band, SUB, LANES), bf),
            pltpu.VMEM((cores, band, SUB, LANES), bf),
            pltpu.VMEM((squad, chunk, SUB, LANES), bf),
            pltpu.VMEM((chunk, SUB, LANES), bf),
        ]

    operands = (
        volume,
        grad_out,
        raw_kernel,
        conv_bias,
        report,
        film_weight.T,
        film_bias,
        in_bias,
        in_weight,
        out_weight.T,
        *(tables[name] for name in names),
    )
    gathered = pl.pallas_call(
        functools.partial(kernel, counts, channels, row_of),
        out_shape=(
            jax.ShapeDtypeStruct(volume.shape, bf),
            jax.ShapeDtypeStruct((dense_tiles, SUB, LANES), bf),
        ),
        in_specs=[pl.BlockSpec(memory_space=pltpu.HBM)] * len(operands),
        out_specs=(pl.BlockSpec(memory_space=pltpu.HBM),) * 2,
        scratch_shapes=[pltpu.VMEM(a.shape, a.dtype) for a in operands]
        + [
            pltpu.VMEM(volume.shape, bf),
            pltpu.VMEM((dense_tiles, SUB, LANES), bf),
            dma((len(operands),)),
            dma((crops + 1,)),
            pltpu.VMEM((LANES, hidden), bf),
            pltpu.VMEM((LANES, hidden), bf),
            pltpu.VMEM(main, bf),
            pltpu.VMEM(side, bf),
            pltpu.VMEM(edges, bf),
            pltpu.VMEM(volume.shape, bf),
            pltpu.VMEM(main, bf),
            pltpu.VMEM(side, bf),
            pltpu.VMEM(edges, bf),
            pltpu.VMEM((crops, slices, voxels, LANES), bf),
            pltpu.VMEM((planes // 2, tables["plane"].shape[1], 2 * LANES), bf),
            pltpu.VMEM((crops, slices, voxels, LANES), bf),
            pltpu.VMEM((K * SUB, K * LANES), f32),
            pltpu.VMEM((K, spec, LANES), f32),
            pltpu.VMEM((crops, planes, spec, LANES), f32),
            pltpu.VMEM((crops, planes, spec, LANES), f32),
            pltpu.VMEM((crops, slices, spec, LANES), f32),
            pltpu.VMEM((3 * spec, slices * LANES), bf),
            pltpu.VMEM((3 * spec, K * LANES), bf),
            pltpu.VMEM((slices, voxels, LANES), f32),
            pltpu.VMEM((SUB, LANES), f32),
            pltpu.VMEM((slices * voxels, LANES), f32),
            pltpu.VMEM((slices * voxels, LANES), f32),
            pltpu.VMEM((crops, slices * voxels, LANES), bf),
            pltpu.VMEM((voxels, hidden), f32),
            pltpu.VMEM((voxels, hidden), f32),
            pltpu.VMEM((crops, slices * voxels, hidden), bf),
            pltpu.VMEM((crops, slices * voxels, hidden), bf),
            pltpu.VMEM((SUB, hidden), f32),
            pltpu.VMEM((3, SUB, LANES), f32),
            *reduce_buffers(dense_tiles),
            pltpu.VMEM((taps_rows, LANES), f32),
        ]
        + [dma((crops, len(DIRS)))] * 4
        + [dma((cores,))] * 2 + [dma((squad,))] * 4 + [dma((cores, squad))] * 2,
        compiler_params=pltpu.CompilerParams(
            collective_id=0, has_side_effects=True, vmem_limit_bytes=60 * 1024 * 1024
        ),
        name="block",
    )(*operands)
    grad_input, grad_kernel, grad_bias, grad_film, grad_in_w, grad_in_b, grad_out_w = pl.pallas_call(
        functools.partial(finish_kernel, channels, row_of, factor),
        out_shape=(
            jax.ShapeDtypeStruct(volume.shape, bf),
            jax.ShapeDtypeStruct((K, K, K, 1, channels), f32),
            jax.ShapeDtypeStruct((channels,), f32),
            jax.ShapeDtypeStruct((2 * channels,), f32),
            jax.ShapeDtypeStruct((channels, hidden), f32),
            jax.ShapeDtypeStruct((hidden,), f32),
            jax.ShapeDtypeStruct((channels, hidden), f32),
        ),
        in_specs=[pl.BlockSpec(memory_space=pltpu.HBM)] * 2,
        out_specs=(pl.BlockSpec(memory_space=pltpu.HBM),) + (pl.BlockSpec(memory_space=pltpu.VMEM),) * 6,
        scratch_shapes=[
            pltpu.VMEM(volume.shape, bf),
            pltpu.VMEM((dense_tiles, SUB, LANES), bf),
            pltpu.VMEM((taps_rows, LANES), f32),
            dma((3,)),
        ],
        compiler_params=pltpu.CompilerParams(vmem_limit_bytes=60 * 1024 * 1024),
        name="finish",
    )(*gathered)
    grad_kernel = jnp.transpose(grad_kernel, (4, 3, 0, 1, 2))
    return (
        grad_input, grad_kernel, grad_bias, grad_film, grad_in_w, grad_in_b, grad_out_w.T
    )


def solution(mesh):
    split = P("groups", "depth", "rows", "cols")
    in_specs = (split, split, P("groups")) + (P(),) * 7
    out_specs = (
        split,
        P("groups", None, None, None, None),
        P("groups"),
        P("groups"),
        P("groups", None),
        P("groups"),
        P("groups", None),
    )
    counts = tuple(mesh.shape[name] for name in ("depth", "rows", "cols"))
    return jax.shard_map(
        functools.partial(local, counts),
        mesh=mesh,
        in_specs=in_specs,
        out_specs=out_specs,
        check_vma=False,
    )
```

```python
import functools
import math

import jax
import jax.numpy as jnp
import numpy as np
from jax import lax
from jax.experimental import pallas as pl
from jax.experimental.pallas import tpu as pltpu
from jax.sharding import PartitionSpec as P

K = 7
HALF = K // 2
LANES = 128
SUB = 8
EDGE = 4
EPSILON = 1e-06
MESH = pl.DeviceIdType.MESH
GELU_C = math.sqrt(2.0 / math.pi)
DIRS = tuple(
    (dz, dx, dc)
    for dz in (-1, 0, 1)
    for dx in (-1, 0, 1)
    for dc in (-1, 0, 1)
    if (dz, dx, dc) != (0, 0, 0)
)


def both(*conds):
    out = conds[0]
    for cond in conds[1:]:
        out = jnp.logical_and(out, cond)
    return out


def split_bf16(array):
    high = array.astype(jnp.bfloat16)
    low = (array - high.astype(np.float64)).astype(jnp.bfloat16)
    return high, low


def fourier_tables(rows, width):
    points_h, points_w = rows + 2 * HALF, width + 2 * HALF
    half_w = points_w // 2 + 1
    ends = (0, points_w // 2)
    freqs = [
        (a, b)
        for b in range(half_w)
        for a in range(points_h // 2 + 1 if b in ends else points_h)
    ]
    freqs += [None] * (-len(freqs) % SUB)

    def phases(cells):
        table = np.zeros((len(freqs), len(cells)))
        live = np.zeros((len(freqs), len(cells)))
        for f, freq in enumerate(freqs):
            for n, cell in enumerate(cells):
                if freq is not None and cell is not None:
                    turns = (freq[0] * cell[0] % points_h) / points_h
                    turns += (freq[1] * cell[1] % points_w) / points_w
                    table[f, n] = 2.0 * np.pi * turns
                    live[f, n] = 1.0
        return table, live

    def interleave(real, imag):
        tiles = len(freqs) // SUB
        both_parts = np.stack(
            [real.reshape(tiles, SUB, -1), imag.reshape(tiles, SUB, -1)], axis=1
        )
        return both_parts.reshape(2 * len(freqs), -1)

    def analysis(cells, sign):
        angle, live = phases(cells)
        high, low = split_bf16(interleave(np.cos(angle) * live, sign * np.sin(angle) * live))
        return np.concatenate([high, low], axis=0)

    def synthesis(cells):
        angle, live = phases(cells)
        lone = [f is not None and f[1] in ends and f[0] in (0, points_h // 2) for f in freqs]
        weight = np.where(np.array(lone), 1.0, 2.0)[:, None] / (points_h * points_w)
        table = interleave(np.cos(angle) * weight * live, -np.sin(angle) * weight * live).T
        high, low = split_bf16(table)
        return np.concatenate([high, high, low], axis=1)

    def padded(h, w):
        inside = -HALF <= h < rows + HALF and -HALF <= w < width + HALF
        return (h + HALF, w + HALF) if inside else None

    columns = width + 2 * EDGE
    plane = []
    for s in range(columns // 2):
        for r in range(2 * SUB):
            plane.append(padded(r % SUB, s + columns // 2 * (r // SUB) - EDGE))
    slots = width // 2 + 2 * EDGE
    for s in range(slots):
        for r in range(2 * SUB):
            h = r % EDGE + (-EDGE if r < SUB else rows)
            top = r % SUB < EDGE
            if top:
                col = None if s < EDGE else (s if s < slots - EDGE else s + width // 2)
            else:
                col = None if s >= slots - EDGE else (s if s < EDGE else s + width // 2)
            plane.append(None if col is None else padded(h, col - EDGE))
    own = [
        (r % SUB, s + width // 2 * (r // SUB)) for s in range(width // 2) for r in range(2 * SUB)
    ]
    taps = [(j, k) if k < K else None for j in range(K) for k in range(SUB)]
    lags = [(n // K, n % K) if n < K * K else None for n in range(K * SUB)]
    return {
        "plane": analysis(plane, -1.0),
        "own": analysis(own, -1.0),
        "taps": analysis(taps, 1.0),
        "forward": synthesis(own),
        "backward": synthesis([(h + K - 1, w + K - 1) for h, w in own]),
        "lags": synthesis(lags),
    }


class Halo:
    def __init__(self, own, edges, main, side, sems, where, counts):
        self.own, self.edges, self.main, self.side = own, edges, main, side
        self.send, self.recv = sems
        self.grp, self.z, self.x, self.c = where
        self.nz, self.nx, self.nc = counts
        self.depth, self.lanes = own.shape[1], own.shape[3]
        self.edge_lanes = (self.main.shape[3] - self.lanes) // 2

    def inside(self, dz, dx, dc):
        z, x, c = self.z + dz, self.x + dx, self.c + dc
        return both(z >= 0, z < self.nz, x >= 0, x < self.nx, c >= 0, c < self.nc)

    def copy(self, crop, idx):
        dz, dx, dc = DIRS[idx]
        depth, lanes, edge = self.depth, self.lanes, self.edge_lanes
        src_d = {-1: slice(0, HALF), 0: slice(0, depth), 1: slice(depth - HALF, depth)}[dz]
        dst_d = {
            -1: slice(HALF + depth, 2 * HALF + depth),
            0: slice(HALF, HALF + depth),
            1: slice(0, HALF),
        }[dz]
        every = slice(None)
        full = lanes if dx == 0 else lanes // 2
        src_l = {-1: slice(0, edge), 0: slice(0, full), 1: slice(full - edge, full)}[dc]
        dst_l = {
            -1: slice(edge + full, 2 * edge + full),
            0: slice(edge, edge + full),
            1: slice(0, edge),
        }[dc]
        if dx == 0:
            src = self.own.at[crop, src_d, every, src_l]
            dst = self.main.at[crop, dst_d, every, dst_l]
        else:
            src = self.edges.at[0 if dx < 0 else 1, crop, src_d, every, src_l]
            dst = self.side.at[crop, 1 if dx < 0 else 0, dst_d, every, dst_l]
        return pltpu.make_async_remote_copy(
            src_ref=src,
            dst_ref=dst,
            send_sem=self.send.at[crop, idx],
            recv_sem=self.recv.at[crop, idx],
            device_id=(self.grp, self.z + dz, self.x + dx, self.c + dc),
            device_id_type=MESH,
        )

    def fill_edges(self):
        depth, edge = self.depth, self.edge_lanes

        def clear(cond, *areas):
            @pl.when(cond)
            def _():
                for ref, area in areas:
                    view = ref.at[area]
                    view[...] = jnp.zeros(view.shape, view.dtype)

        every = slice(None)
        low, high = slice(0, HALF), slice(HALF + depth, 2 * HALF + depth)
        main, side = self.main, self.side
        clear(self.z == 0, (main, (every, low)), (side, (every, every, low)))
        clear(self.z == self.nz - 1, (main, (every, high)), (side, (every, every, high)))
        clear(self.x == 0, (side, (every, 0)))
        clear(self.x == self.nx - 1, (side, (every, 1)))
        rest = (every, every, every)
        clear(self.c == 0, (main, rest + (slice(0, edge),)), (side, (every,) + rest + (slice(0, edge),)))
        clear(
            self.c == self.nc - 1,
            (main, rest + (slice(main.shape[3] - edge, main.shape[3]),)),
            (side, (every,) + rest + (slice(side.shape[4] - edge, side.shape[4]),)),
        )

    def cut_edges(self, crop):
        half = self.lanes // 2
        for d in range(self.depth):
            for which, first in enumerate((0, EDGE)):
                for part in range(2):
                    self.edges[which, crop, d, part * EDGE : (part + 1) * EDGE, :] = self.own[
                        crop, d, first : first + EDGE, part * half : (part + 1) * half
                    ]

    def start(self, crop, inner):
        for idx, step in enumerate(DIRS):
            if inner != (step[0] == 0):
                continue

            @pl.when(self.inside(*step))
            def _():
                self.copy(crop, idx).start()

    def centre(self, crop):
        depth, lanes, edge = self.depth, self.lanes, self.edge_lanes
        self.main[crop, HALF : HALF + depth, :, edge : edge + lanes] = self.own[crop]

    def arrive(self, crop, inner):
        for idx, (dz, dx, dc) in enumerate(DIRS):
            if inner != (dz == 0):
                continue

            @pl.when(self.inside(-dz, -dx, -dc))
            def _():
                self.copy(crop, idx).wait_recv()

    def finish(self, crop):
        for idx, step in enumerate(DIRS):
            @pl.when(self.inside(*step))
            def _():
                self.copy(crop, idx).wait_send()


def wrap(index, extent):
    return jnp.where(index >= extent, index - extent, index)


def digits(offset, extent):
    if isinstance(offset, int):
        return divmod(offset, extent)
    return offset // extent, lax.rem(offset, extent)


def each(first, last, fn):
    if last - first <= 2 * SUB:
        for offset in range(first, last):
            fn(offset)
        return

    def step(offset, _):
        fn(offset)
        return 0

    lax.fori_loop(first, last, step, 0)


class Reduction:
    def __init__(self, part, bufs, sems, full, out, out_sem, where, counts):
        self.part, self.full, self.out, self.out_sem = part, full, out, out_sem
        self.low, self.band_low, self.inbox_c, self.inbox, self.mine = bufs
        self.hv, self.rs, self.ag, self.sh = sems
        self.grp, self.z, self.x, self.c = where
        self.nz, self.nx, self.nc = counts
        self.squad = self.nz * self.nx
        self.seat = self.z * self.nx + self.x
        self.band = part.shape[0] // self.nc
        self.chunk = self.band // self.squad

    def mate(self, offset):
        other = wrap(self.c + offset, self.nc)
        return other, (self.grp, self.z, self.x, other)

    def fellow(self, offset):
        dz, dx = digits(offset, self.nx)
        other_z, other_x = wrap(self.z + dz, self.nz), wrap(self.x + dx, self.nx)
        return other_z * self.nx + other_x, (self.grp, other_z, other_x, self.c)

    def remote(self, src, dst, sems, idx, device):
        return pltpu.make_async_remote_copy(
            src_ref=src, dst_ref=dst, send_sem=sems[0].at[idx], recv_sem=sems[1].at[idx],
            device_id=device, device_id_type=MESH,
        )

    def rows(self, seat, core):
        return pl.ds(core * self.band + seat * self.chunk, self.chunk)

    def origin(self, offset):
        dz, dx = digits(offset, self.nx)
        from_z = wrap(self.z + self.nz - dz, self.nz)
        return from_z * self.nx + wrap(self.x + self.nx - dx, self.nx)

    def halve(self, offset):
        other, device = self.mate(offset)
        src = self.low.at[pl.ds(other * self.band, self.band)]
        return self.remote(src, self.inbox_c.at[offset], self.hv, offset, device)

    def scatter(self, offset):
        other, device = self.fellow(offset)
        src = self.band_low.at[pl.ds(other * self.chunk, self.chunk)]
        return self.remote(src, self.inbox.at[offset], self.rs, offset, device)

    def spread(self, offset, seat):
        dst = self.full.at[self.rows(seat, self.c)]
        return self.remote(self.mine, dst, self.ag, offset, self.fellow(offset)[1])

    def share(self, offset, step, core):
        rows = self.rows(self.origin(offset), core)
        sems = [sem.at[step] for sem in self.sh]
        return self.remote(
            self.full.at[rows], self.out.at[rows], sems, offset, self.mate(step)[1]
        )

    def write_band(self):
        band = pl.ds(self.c * self.band, self.band)
        return pltpu.make_async_copy(self.full.at[band], self.out.at[band], self.out_sem)

    def start_halves(self):
        self.low[...] = self.part[...].astype(jnp.bfloat16)
        each(1, self.nc, lambda offset: self.halve(offset).start())

    def start_scatter(self):
        each(1, self.nc, lambda offset: self.halve(offset).wait())
        band = pl.ds(self.c * self.band, self.band)
        acc = self.part[band]
        for offset in range(1, self.nc):
            acc = acc + self.inbox_c[offset].astype(jnp.float32)
        self.part[band] = acc
        self.band_low[...] = acc.astype(jnp.bfloat16)
        each(1, self.squad, lambda offset: self.scatter(offset).start())

    def start_spread(self):
        each(1, self.squad, lambda offset: self.scatter(offset).wait())

        def add(offset, acc):
            return acc + self.inbox[offset].astype(jnp.float32)

        acc = self.part[self.rows(self.seat, self.c)]
        if self.squad <= 2 * SUB:
            for offset in range(1, self.squad):
                acc = add(offset, acc)
        else:
            acc = lax.fori_loop(1, self.squad, add, acc)
        self.mine[...] = acc.astype(jnp.bfloat16)
        self.full[self.rows(self.seat, self.c)] = self.mine[...]
        each(1, self.squad, lambda offset: self.spread(offset, self.seat).start())
        each(1, self.nc, lambda step: self.share(0, step, self.c).start())

    def start_share(self):
        def pass_on(offset):
            self.spread(offset, self.origin(offset)).wait_recv()
            each(1, self.nc, lambda step: self.share(offset, step, self.c).start())

        each(1, self.squad, pass_on)
        self.write_band().start()

    def settle(self):
        each(1, self.squad, lambda offset: self.spread(offset, self.seat).wait_send())

        def close(offset):
            def one(step):
                self.share(offset, step, self.c).wait_send()
                core = wrap(self.c + self.nc - step, self.nc)
                self.share(offset, step, core).wait_recv()

            each(1, self.nc, one)

        each(0, self.squad, close)
        self.write_band().wait()


def slot_slices(array, channels):
    return [array[:, s * channels : (s + 1) * channels] for s in range(array.shape[1] // channels)]


def gather_plane(main, side, crop, plane, xs, lane, channels):
    wide = main[crop, plane]
    half = wide.shape[1] // 2
    wide = jnp.concatenate([wide[:, :half], wide[:, half:]], axis=0)
    rim = jnp.concatenate([side[crop, 0, plane], side[crop, 1, plane]], axis=0)
    for n, cell in enumerate(slot_slices(wide, channels) + slot_slices(rim, channels)):
        xs[n * 2 * SUB : (n + 1) * 2 * SUB, lane : lane + channels] = cell


def spectra(halo, crop, xs, table, out, channels, then=None, arrived=False):
    depth, rows = halo.depth, out.shape[2]
    own = list(range(HALF, HALF + depth))
    order = own + [p for p in range(depth + 2 * HALF) if p not in own]
    if not arrived:
        halo.arrive(crop, True)
    for pair in range(len(order) // 2):
        planes = order[2 * pair : 2 * pair + 2]
        if pair == depth // 2:
            if then is not None:
                then()
            halo.arrive(crop, False)
        for q, plane in enumerate(planes):
            gather_plane(halo.main, halo.side, crop, plane, xs.at[pair], q * LANES, channels)
        res = jnp.dot(table[...], xs[pair], preferred_element_type=jnp.float32)
        res = res[:rows] + res[rows:]
        for q, plane in enumerate(planes):
            out[crop, plane] = res[:, q * LANES : (q + 1) * LANES]


def store_split(ref, tile, lane, re, im):
    value = jnp.concatenate([re, im], axis=0)
    high = value.astype(jnp.bfloat16)
    low = (value - high.astype(jnp.float32)).astype(jnp.bfloat16)
    rows = ref.shape[0] // 3
    for n, part in enumerate((high, low, high)):
        first = pl.multiple_of(tile * 2 * SUB, 2 * SUB) + n * rows
        ref[pl.ds(first, 2 * SUB), lane : lane + LANES] = part


def tile_of(ref, lead, tile):
    first = pl.multiple_of(tile * 2 * SUB, 2 * SUB)
    return ref[lead + (pl.ds(first, SUB),)], ref[lead + (pl.ds(first + SUB, SUB),)]


def conv_products(xhat, khat, crop, depth, yhat, flip):
    tiles = yhat.shape[0] // (3 * 2 * SUB)

    def step(tile, _):
        taps = [tile_of(khat, (i,), tile) for i in range(K)]
        data = [tile_of(xhat, (crop, p), tile) for p in range(depth + K - 1)]
        for d in range(depth):
            re = im = None
            for i in range(K):
                kr, ki = taps[i]
                xr, xi = data[d + K - 1 - i if flip else d + i]
                if flip:
                    a, b = xr * kr + xi * ki, xi * kr - xr * ki
                else:
                    a, b = xr * kr - xi * ki, xr * ki + xi * kr
                re, im = (a, b) if re is None else (re + a, im + b)
            store_split(yhat, tile, d * LANES, re, im)
        return 0

    lax.fori_loop(0, tiles, step, 0)


def lag_products(xhat, ohat, crops, depth, ghat):
    tiles = ghat.shape[0] // (3 * 2 * SUB)

    def step(tile, _):
        accs = [[None, None] for _ in range(K)]
        for crop in range(crops):
            data = [tile_of(xhat, (crop, p), tile) for p in range(depth + K - 1)]
            slope = [tile_of(ohat, (crop, d), tile) for d in range(depth)]
            for i in range(K):
                for d in range(depth):
                    xr, xi = data[d + i]
                    sr, si = slope[d]
                    a, b = xr * sr + xi * si, xi * sr - xr * si
                    acc = accs[i]
                    accs[i] = [a, b] if acc[0] is None else [acc[0] + a, acc[1] + b]
        for i in range(K):
            store_split(ghat, tile, i * LANES, accs[i][0], accs[i][1])
        return 0

    lax.fori_loop(0, tiles, step, 0)


def to_native(slots, channels):
    line = jnp.concatenate([slot[:, :channels] for slot in slots], axis=1)
    return jnp.concatenate([line[:SUB], line[SUB:]], axis=1)


def kernel(
    counts, channels, row_of,
    *refs,
):
    count = 16
    operands, (gi_hbm, full_hbm), staged, refs = (
        refs[:count], refs[count : count + 2], refs[count + 2 : 2 * count + 2], refs[2 * count + 2 :]
    )
    (
        x_raw, g_raw, kernel_ref, bias_ref, report_ref, fw_ref, fb_ref, ib_ref, inw_raw, outw_raw,
        f_plane, f_own, f_taps, s_fwd, s_bwd, s_lags,
    ) = staged
    (
    gi_ref, full, load_sems, out_sems,
    inw_ref, outw_ref, x_main, x_side, x_edges, s_own, s_main, s_side, s_edges,
    gs, xs, own_rhs, taps_s, khat, xhat, shat, ohat, yhat, ghat, conv_s,
    vec_ref, norm_s, inv_s, hid_s, pre_s, act_s, act_low, gpre_low, accb, accf, part, part_low, band_low, inbox_c, inbox, mine, taps_part,
    x_send, x_recv, sl_send, sl_recv,
    hv_send, hv_recv, rs_send, rs_recv, ag_send, ag_recv, sh_send, sh_recv,
    ) = refs
    nz, nx, nc = counts
    total = nz * nx * nc
    grp, z, x, c = (lax.axis_index(name) for name in ("groups", "depth", "rows", "cols"))
    crops, depth = x_raw.shape[:2]
    hidden = inw_raw.shape[1]
    voxels = s_fwd.shape[0]
    bf, f32 = jnp.bfloat16, jnp.float32

    def peer(offset):
        rest, dc = digits(offset, nc)
        dz, dx = digits(rest, nx)
        return grp, wrap(z + dz, nz), wrap(x + dx, nx), wrap(c + dc, nc)

    loads = [
        pltpu.make_async_copy(src, dst, load_sems.at[n])
        for n, (src, dst) in enumerate(zip(operands, staged))
    ]
    for n in (0, 12, 2, 10, 1, 3, 4, 5, 6, 7, 8, 9, 13, 11, 15, 14):
        loads[n].start()
    barrier = pltpu.get_barrier_semaphore()

    each(
        1, total,
        lambda offset: pl.semaphore_signal(
            barrier, inc=1, device_id=peer(offset), device_id_type=MESH
        ),
    )
    where = (grp, z, x, c)
    halo_x = Halo(x_raw, x_edges, x_main, x_side, (x_send, x_recv), where, counts)
    halo_s = Halo(s_own, s_edges, s_main, s_side, (sl_send, sl_recv), where, counts)
    loads[0].wait()
    for crop in range(crops):
        halo_x.cut_edges(crop)
    pl.semaphore_wait(barrier, total - 1)
    halo_x.start(0, True)
    halo_x.start(0, False)
    halo_x.fill_edges()
    halo_s.fill_edges()
    for crop in range(crops):
        halo_x.centre(crop)
    for n in (2, 12):
        loads[n].wait()
    spare = LANES - channels
    xs[...] = jnp.zeros_like(xs)
    gs[...] = jnp.zeros_like(gs)
    taps_s[...] = jnp.zeros_like(taps_s)
    for i in range(K):
        for j in range(K):
            taps_s[j * SUB : j * SUB + K, i * LANES : i * LANES + channels] = kernel_ref[
                i, j
            ].astype(f32)
    res = jnp.dot(f_taps[...], taps_s[...].astype(bf), preferred_element_type=f32)
    half = res.shape[0] // 2
    res = res[:half] + res[half:]
    for i in range(K):
        khat[i] = res[:, i * LANES : (i + 1) * LANES]
    for n in (1, 3, 4, 5, 6, 7, 8, 9):
        loads[n].wait()
    for raw, ready in ((inw_raw, inw_ref), (outw_raw, outw_ref)):
        ready[0:channels, :] = raw[...]
        ready[channels:, :] = jnp.zeros((spare, hidden), bf)
    for crop in range(crops):
        for d in range(depth):
            wide = g_raw[crop, d]
            middle = wide.shape[1] // 2
            wide = jnp.concatenate([wide[:, :middle], wide[:, middle:]], axis=0)
            for n, cell in enumerate(slot_slices(wide, channels)):
                first = n * 2 * SUB
                gs[crop, d, first : first + 2 * SUB, 0:channels] = cell
    vec_ref[...] = jnp.zeros_like(vec_ref)
    vec_ref[0:1, 0:channels] = bias_ref[...].reshape(1, channels)
    film = lax.dot_general(
        report_ref[...].astype(f32).reshape(1, report_ref.shape[0]).astype(bf), fw_ref[...],
        (((1,), (1,)), ((), ())), preferred_element_type=f32,
    )
    film = film + fb_ref[...].reshape(1, 2 * channels)
    vec_ref[1:2, 0:channels] = film[:, :channels] + 1.0
    vec_ref[2:3, 0:channels] = film[:, channels:]
    accb[...] = jnp.zeros_like(accb)
    accf[...] = jnp.zeros_like(accf)
    tail = row_of["small"] // SUB
    part[tail:] = jnp.zeros((part.shape[0] - tail, SUB, LANES), f32)
    taps_part[...] = jnp.zeros_like(taps_part)

    conv_bias, scale, shift = vec_ref[0:1, :], vec_ref[1:2, :], vec_ref[2:3, :]
    in_bias = ib_ref[...].reshape(1, hidden)
    for n in (10, 13, 11, 15, 14):
        loads[n].wait()
    real = lax.broadcasted_iota(jnp.int32, (1, LANES), 1) < channels

    inner = GELU_C
    outer = GELU_C * 0.044715

    def normalise(crop, d):
        conv = conv_s[d] + conv_bias
        mean = jnp.sum(conv, axis=1, keepdims=True) * (1.0 / channels)
        centred = jnp.where(real, conv - mean, 0.0)
        variance = jnp.sum(centred * centred, axis=1, keepdims=True) * (1.0 / channels)
        inverse = lax.rsqrt(variance + EPSILON)
        normed = centred * inverse
        first = d * voxels
        norm_s[first : first + voxels] = normed
        inv_s[first : first + voxels] = jnp.broadcast_to(inverse, (voxels, LANES))
        hid_s[crop, first : first + voxels] = (normed * scale + shift).astype(bf)

    def activate(crop, d):
        rows = slice(d * voxels, (d + 1) * voxels)
        pre_s[...] = jnp.dot(hid_s[crop, rows], inw_ref[...], preferred_element_type=f32)
        act_s[...] = jnp.dot(gs[crop, d], outw_ref[...], preferred_element_type=f32)
        sums = jnp.zeros((2 * SUB, hidden), f32)
        for n in range(voxels // (2 * SUB)):
            part_rows = slice(n * 2 * SUB, (n + 1) * 2 * SUB)
            out_rows = slice(d * voxels + n * 2 * SUB, d * voxels + (n + 1) * 2 * SUB)
            pre = pre_s[part_rows] + in_bias
            square = pre * pre
            half = 0.5 * jnp.tanh(pre * (inner + outer * square)) + 0.5
            act = pre * half
            act_low[crop, out_rows] = act.astype(bf)
            slope_act = half + act * (1.0 - half) * (2.0 * inner + (6.0 * outer) * square)
            grad_pre = act_s[part_rows] * slope_act
            gpre_low[crop, out_rows] = grad_pre.astype(bf)
            sums = sums + grad_pre
        accb[...] += sums[:SUB] + sums[SUB:]

    def settle_slope(crop, d):
        rows = slice(d * voxels, (d + 1) * voxels)
        grad_hidden = lax.dot_general(
            gpre_low[crop, rows], inw_ref[...], (((1,), (1,)), ((), ())),
            preferred_element_type=f32,
        )
        normed = norm_s[rows]
        product = grad_hidden * normed
        accf[1] += jnp.sum(product.reshape(voxels // SUB, SUB, LANES), axis=0)
        accf[2] += jnp.sum(grad_hidden.reshape(voxels // SUB, SUB, LANES), axis=0)
        mean_g = jnp.sum(grad_hidden * scale, axis=1, keepdims=True) * (1.0 / channels)
        mean_gn = jnp.sum(product * scale, axis=1, keepdims=True) * (1.0 / channels)
        slope = (grad_hidden * scale - mean_g - normed * mean_gn) * inv_s[rows]
        slope = slope.astype(bf)
        accf[0] += jnp.sum(slope.astype(f32).reshape(voxels // SUB, SUB, LANES), axis=0)
        own_rhs[crop, d] = slope
        s_own[crop, d] = to_native(
            [slope[n * 2 * SUB : (n + 1) * 2 * SUB] for n in range(voxels // (2 * SUB))], channels
        )

    def mlp(crop):
        for stage in (normalise, activate, settle_slope):
            for d in range(depth):
                stage(crop, d)

    def forward(crop, _):
        halo_x.arrive(crop, True)

        @pl.when(crop + 1 < crops)
        def _():
            halo_x.start(crop + 1, True)
            halo_x.start(crop + 1, False)

        spectra(halo_x, crop, xs, f_plane, xhat, channels, arrived=True)
        conv_products(xhat, khat, crop, depth, yhat, False)
        conv = jnp.dot(s_fwd[...], yhat[...], preferred_element_type=f32)
        for d in range(depth):
            conv_s[d] = conv[:, d * LANES : (d + 1) * LANES]

        mlp(crop)
        halo_s.cut_edges(crop)
        halo_s.start(crop, True)
        halo_s.start(crop, False)
        halo_s.centre(crop)
        return 0

    lax.fori_loop(0, crops, forward, 0)

    def own_spectra(step, _):
        crop, pair = step // (depth // 2), step % (depth // 2)
        rhs = jnp.concatenate([own_rhs[crop, 2 * pair], own_rhs[crop, 2 * pair + 1]], axis=1)
        res = jnp.dot(f_own[...], rhs, preferred_element_type=f32)
        res = res[: res.shape[0] // 2] + res[res.shape[0] // 2 :]
        for q in range(2):
            ohat[crop, 2 * pair + q] = res[:, q * LANES : (q + 1) * LANES]
        return 0

    bufs = (part_low, band_low, inbox_c, inbox, mine)
    first_sems = ((hv_send, hv_recv), (rs_send, rs_recv), (ag_send, ag_recv), (sh_send, sh_recv))
    dense = Reduction(
        part, bufs, first_sems, full, full_hbm, out_sems.at[crops], where, counts
    )
    def slope_spectra(crop, then=None):
        spectra(halo_s, crop, xs, f_plane, shat, channels, then)

    def backward(crop):
        conv_products(shat, khat, crop, depth, yhat, True)
        conv = jnp.dot(s_bwd[...], yhat[...], preferred_element_type=f32)
        for d in range(depth):
            total_in = gs[crop, d].astype(f32) + conv[:, d * LANES : (d + 1) * LANES]
            low = total_in.astype(bf)
            gi_ref[crop, d] = to_native(
                [low[n * 2 * SUB : (n + 1) * 2 * SUB] for n in range(voxels // (2 * SUB))],
                channels,
            )

    def gi_out(crop):
        return pltpu.make_async_copy(gi_ref.at[crop], gi_hbm.at[crop], out_sems.at[crop])

    over_voxels = (((0,), (0,)), ((), ()))
    everything = crops * depth * voxels
    for name, left, right in (
        ("in", hid_s[...].reshape(everything, LANES), gpre_low[...].reshape(everything, hidden)),
        ("out", gs[...].reshape(everything, LANES), act_low[...].reshape(everything, hidden)),
    ):
        grads = lax.dot_general(left, right, over_voxels, preferred_element_type=f32)
        for block in range(hidden // LANES):
            first = row_of[name] + block * channels
            piece = grads[0:channels, block * LANES : (block + 1) * LANES]
            part[first // SUB : (first + channels) // SUB] = piece.reshape(
                channels // SUB, SUB, LANES
            )
    for n in range(3):
        row = row_of["small"] + n
        part[row // SUB, row % SUB : row % SUB + 1, :] = jnp.sum(accf[n], axis=0, keepdims=True)
    for block in range(hidden // LANES):
        row = row_of["in_bias"] + block
        part[row // SUB, row % SUB : row % SUB + 1, :] = jnp.sum(
            accb[:, block * LANES : (block + 1) * LANES], axis=0, keepdims=True
        )
    lax.fori_loop(0, crops * depth // 2, own_spectra, 0)
    lag_products(xhat, ohat, crops, depth, ghat)
    lags = jnp.dot(s_lags[...], ghat[...], preferred_element_type=f32)
    for i in range(K):
        rows_i = lags[0 : K * K, i * LANES : (i + 1) * LANES]
        taps_part[i * K * K : (i + 1) * K * K, :] = rows_i
    first_tap = row_of["kernel"] // SUB
    part[first_tap : first_tap + taps_part.shape[0] // SUB] = taps_part[...].reshape(
        taps_part.shape[0] // SUB, SUB, LANES
    )
    dense.start_halves()
    slope_spectra(0, dense.start_scatter)
    backward(0)
    gi_out(0).start()
    dense.start_spread()
    for crop in range(1, crops):
        slope_spectra(crop)
        backward(crop)
        gi_out(crop).start()
    dense.start_share()
    dense.settle()
    for crop in range(crops):
        halo_x.finish(crop)
        halo_s.finish(crop)
        gi_out(crop).wait()


def finish_kernel(
    channels, row_of, factor,
    gi_in, dense_in,
    gi_ref, gk_ref, gb_ref, gf_ref, ginw_ref, gib_ref, goutw_ref,
    gi_buf, dense, red, sems,
):
    load = pltpu.make_async_copy(gi_in, gi_buf, sems.at[0])
    fetch = pltpu.make_async_copy(dense_in, dense, sems.at[1])
    for copy in (load, fetch):
        copy.start()
    load.wait()
    pass_through = pltpu.make_async_copy(gi_buf, gi_ref, sems.at[2])
    pass_through.start()
    fetch.wait()
    hidden = ginw_ref.shape[1]
    for name, out_ref in (("in", ginw_ref), ("out", goutw_ref)):
        for block in range(hidden // LANES):
            first = (row_of[name] + block * channels) // SUB
            piece = dense[first : first + channels // SUB].astype(jnp.float32) * factor
            out_ref[:, block * LANES : (block + 1) * LANES] = piece.reshape(channels, LANES)
    small = row_of["small"] // SUB
    rows = dense[small].astype(jnp.float32) * factor
    gb_ref[...] = rows[0:1, 0:channels].reshape(channels)
    film = [rows[n : n + 1, 0:channels] for n in (1, 2)]
    gf_ref[...] = jnp.concatenate(film, axis=1).reshape(2 * channels)
    lines = [rows[3 + n : 4 + n, :] for n in range(hidden // LANES)]
    gib_ref[...] = jnp.concatenate(lines, axis=1).reshape(hidden)
    first_tap = row_of["kernel"] // SUB
    taps = dense[first_tap : first_tap + red.shape[0] // SUB].astype(jnp.float32)
    red[...] = taps.reshape(red.shape) * factor
    for i in range(K):
        for j in range(K):
            first = (i * K + j) * K
            gk_ref[i, j] = red[first : first + K, 0:channels].reshape(K, 1, channels)
    pass_through.wait()


def local(
    counts, volume, grad_out, report, conv_kernel, conv_bias,
    film_weight, film_bias, in_weight, in_bias, out_weight,
):
    crops, slices, lines, merged = volume.shape
    channels = conv_kernel.shape[0]
    hidden = in_weight.shape[1]
    width = merged // channels
    raw_kernel = jnp.transpose(conv_kernel[:, 0], (1, 2, 3, 0))
    total = counts[0] * counts[1] * counts[2]
    blocks = hidden // LANES
    row_of = {"in": 0, "out": blocks * channels, "small": 2 * blocks * channels}
    row_of["in_bias"] = row_of["small"] + 3
    cores, squad = counts[2], counts[0] * counts[1]
    row_of["kernel"] = -(-(row_of["in_bias"] + blocks) // SUB) * SUB
    taps_rows = -(-K * K * K // SUB) * SUB
    dense_tiles = -(-(row_of["kernel"] + taps_rows) // (SUB * total)) * total
    bf, f32 = jnp.bfloat16, jnp.float32
    dma = pltpu.SemaphoreType.DMA
    tables = fourier_tables(lines, width)
    names = ("plane", "own", "taps", "forward", "backward", "lags")
    spec = tables["plane"].shape[0] // 2
    planes = slices + 2 * HALF
    voxels = lines * width
    edge_lanes = EDGE * channels
    halves = merged // 2 + 2 * edge_lanes
    main = (crops, planes, lines, merged + 2 * edge_lanes)
    side = (crops, 2, planes, 2 * EDGE, halves)
    edges = (2, crops, slices, 2 * EDGE, merged // 2)
    factor = 1.0 / math.sqrt(crops * slices * voxels * total)
    def reduce_buffers(tiles):
        band, chunk = tiles // cores, tiles // total
        return [
            pltpu.VMEM((tiles, SUB, LANES), f32),
            pltpu.VMEM((tiles, SUB, LANES), bf),
            pltpu.VMEM((band, SUB, LANES), bf),
            pltpu.VMEM((cores, band, SUB, LANES), bf),
            pltpu.VMEM((squad, chunk, SUB, LANES), bf),
            pltpu.VMEM((chunk, SUB, LANES), bf),
        ]

    operands = (
        volume,
        grad_out,
        raw_kernel,
        conv_bias,
        report,
        film_weight.T,
        film_bias,
        in_bias,
        in_weight,
        out_weight.T,
        *(tables[name] for name in names),
    )
    gathered = pl.pallas_call(
        functools.partial(kernel, counts, channels, row_of),
        out_shape=(
            jax.ShapeDtypeStruct(volume.shape, bf),
            jax.ShapeDtypeStruct((dense_tiles, SUB, LANES), bf),
        ),
        in_specs=[pl.BlockSpec(memory_space=pltpu.HBM)] * len(operands),
        out_specs=(pl.BlockSpec(memory_space=pltpu.HBM),) * 2,
        scratch_shapes=[pltpu.VMEM(a.shape, a.dtype) for a in operands]
        + [
            pltpu.VMEM(volume.shape, bf),
            pltpu.VMEM((dense_tiles, SUB, LANES), bf),
            dma((len(operands),)),
            dma((crops + 1,)),
            pltpu.VMEM((LANES, hidden), bf),
            pltpu.VMEM((LANES, hidden), bf),
            pltpu.VMEM(main, bf),
            pltpu.VMEM(side, bf),
            pltpu.VMEM(edges, bf),
            pltpu.VMEM(volume.shape, bf),
            pltpu.VMEM(main, bf),
            pltpu.VMEM(side, bf),
            pltpu.VMEM(edges, bf),
            pltpu.VMEM((crops, slices, voxels, LANES), bf),
            pltpu.VMEM((planes // 2, tables["plane"].shape[1], 2 * LANES), bf),
            pltpu.VMEM((crops, slices, voxels, LANES), bf),
            pltpu.VMEM((K * SUB, K * LANES), f32),
            pltpu.VMEM((K, spec, LANES), f32),
            pltpu.VMEM((crops, planes, spec, LANES), f32),
            pltpu.VMEM((crops, planes, spec, LANES), f32),
            pltpu.VMEM((crops, slices, spec, LANES), f32),
            pltpu.VMEM((3 * spec, slices * LANES), bf),
            pltpu.VMEM((3 * spec, K * LANES), bf),
            pltpu.VMEM((slices, voxels, LANES), f32),
            pltpu.VMEM((SUB, LANES), f32),
            pltpu.VMEM((slices * voxels, LANES), f32),
            pltpu.VMEM((slices * voxels, LANES), f32),
            pltpu.VMEM((crops, slices * voxels, LANES), bf),
            pltpu.VMEM((voxels, hidden), f32),
            pltpu.VMEM((voxels, hidden), f32),
            pltpu.VMEM((crops, slices * voxels, hidden), bf),
            pltpu.VMEM((crops, slices * voxels, hidden), bf),
            pltpu.VMEM((SUB, hidden), f32),
            pltpu.VMEM((3, SUB, LANES), f32),
            *reduce_buffers(dense_tiles),
            pltpu.VMEM((taps_rows, LANES), f32),
        ]
        + [dma((crops, len(DIRS)))] * 4
        + [dma((cores,))] * 2 + [dma((squad,))] * 4 + [dma((cores, squad))] * 2,
        compiler_params=pltpu.CompilerParams(
            collective_id=0, has_side_effects=True, vmem_limit_bytes=60 * 1024 * 1024
        ),
        name="block",
    )(*operands)
    grad_input, grad_kernel, grad_bias, grad_film, grad_in_w, grad_in_b, grad_out_w = pl.pallas_call(
        functools.partial(finish_kernel, channels, row_of, factor),
        out_shape=(
            jax.ShapeDtypeStruct(volume.shape, bf),
            jax.ShapeDtypeStruct((K, K, K, 1, channels), f32),
            jax.ShapeDtypeStruct((channels,), f32),
            jax.ShapeDtypeStruct((2 * channels,), f32),
            jax.ShapeDtypeStruct((channels, hidden), f32),
            jax.ShapeDtypeStruct((hidden,), f32),
            jax.ShapeDtypeStruct((channels, hidden), f32),
        ),
        in_specs=[pl.BlockSpec(memory_space=pltpu.HBM)] * 2,
        out_specs=(pl.BlockSpec(memory_space=pltpu.HBM),) + (pl.BlockSpec(memory_space=pltpu.VMEM),) * 6,
        scratch_shapes=[
            pltpu.VMEM(volume.shape, bf),
            pltpu.VMEM((dense_tiles, SUB, LANES), bf),
            pltpu.VMEM((taps_rows, LANES), f32),
            dma((3,)),
        ],
        compiler_params=pltpu.CompilerParams(vmem_limit_bytes=60 * 1024 * 1024),
        name="finish",
    )(*gathered)
    grad_kernel = jnp.transpose(grad_kernel, (4, 3, 0, 1, 2))
    return (
        grad_input, grad_kernel, grad_bias, grad_film, grad_in_w, grad_in_b, grad_out_w.T
    )


def solution(mesh):
    split = P("groups", "depth", "rows", "cols")
    in_specs = (split, split, P("groups")) + (P(),) * 7
    out_specs = (
        split,
        P("groups", None, None, None, None),
        P("groups"),
        P("groups"),
        P("groups", None),
        P("groups"),
        P("groups", None),
    )
    counts = tuple(mesh.shape[name] for name in ("depth", "rows", "cols"))
    return jax.shard_map(
        functools.partial(local, counts),
        mesh=mesh,
        in_specs=in_specs,
        out_specs=out_specs,
        check_vma=False,
    )
```

```python
import functools
import math

import jax
import jax.numpy as jnp
import numpy as np
from jax import lax
from jax.experimental import pallas as pl
from jax.experimental.pallas import tpu as pltpu
from jax.sharding import PartitionSpec as P

K = 7
HALF = K // 2
LANES = 128
SUB = 8
EDGE = 4
EPSILON = 1e-06
MESH = pl.DeviceIdType.MESH
GELU_C = math.sqrt(2.0 / math.pi)
DIRS = tuple(
    (dz, dx, dc)
    for dz in (-1, 0, 1)
    for dx in (-1, 0, 1)
    for dc in (-1, 0, 1)
    if (dz, dx, dc) != (0, 0, 0)
)


def both(*conds):
    out = conds[0]
    for cond in conds[1:]:
        out = jnp.logical_and(out, cond)
    return out


def split_bf16(array):
    high = array.astype(jnp.bfloat16)
    low = (array - high.astype(np.float64)).astype(jnp.bfloat16)
    return high, low


def fourier_tables(rows, width):
    points_h, points_w = rows + 2 * HALF, width + 2 * HALF
    half_w = points_w // 2 + 1
    ends = (0, points_w // 2)
    freqs = [
        (a, b)
        for b in range(half_w)
        for a in range(points_h // 2 + 1 if b in ends else points_h)
    ]
    freqs += [None] * (-len(freqs) % SUB)

    def phases(cells):
        table = np.zeros((len(freqs), len(cells)))
        live = np.zeros((len(freqs), len(cells)))
        for f, freq in enumerate(freqs):
            for n, cell in enumerate(cells):
                if freq is not None and cell is not None:
                    turns = (freq[0] * cell[0] % points_h) / points_h
                    turns += (freq[1] * cell[1] % points_w) / points_w
                    table[f, n] = 2.0 * np.pi * turns
                    live[f, n] = 1.0
        return table, live

    def interleave(real, imag):
        tiles = len(freqs) // SUB
        both_parts = np.stack(
            [real.reshape(tiles, SUB, -1), imag.reshape(tiles, SUB, -1)], axis=1
        )
        return both_parts.reshape(2 * len(freqs), -1)

    def analysis(cells, sign):
        angle, live = phases(cells)
        high, low = split_bf16(interleave(np.cos(angle) * live, sign * np.sin(angle) * live))
        return np.concatenate([high, low], axis=0)

    def synthesis(cells):
        angle, live = phases(cells)
        lone = [f is not None and f[1] in ends and f[0] in (0, points_h // 2) for f in freqs]
        weight = np.where(np.array(lone), 1.0, 2.0)[:, None] / (points_h * points_w)
        table = interleave(np.cos(angle) * weight * live, -np.sin(angle) * weight * live).T
        high, low = split_bf16(table)
        return np.concatenate([high, high, low], axis=1)

    def padded(h, w):
        inside = -HALF <= h < rows + HALF and -HALF <= w < width + HALF
        return (h + HALF, w + HALF) if inside else None

    columns = width + 2 * EDGE
    plane = []
    for s in range(columns // 2):
        for r in range(2 * SUB):
            plane.append(padded(r % SUB, s + columns // 2 * (r // SUB) - EDGE))
    slots = width // 2 + 2 * EDGE
    for s in range(slots):
        for r in range(2 * SUB):
            h = r % EDGE + (-EDGE if r < SUB else rows)
            top = r % SUB < EDGE
            if top:
                col = None if s < EDGE else (s if s < slots - EDGE else s + width // 2)
            else:
                col = None if s >= slots - EDGE else (s if s < EDGE else s + width // 2)
            plane.append(None if col is None else padded(h, col - EDGE))
    own = [
        (r % SUB, s + width // 2 * (r // SUB)) for s in range(width // 2) for r in range(2 * SUB)
    ]
    taps = [(j, k) if k < K else None for j in range(K) for k in range(SUB)]
    lags = [(n // K, n % K) if n < K * K else None for n in range(K * SUB)]
    return {
        "plane": analysis(plane, -1.0),
        "own": analysis(own, -1.0),
        "taps": analysis(taps, 1.0),
        "forward": synthesis(own),
        "backward": synthesis([(h + K - 1, w + K - 1) for h, w in own]),
        "lags": synthesis(lags),
    }


class Halo:
    def __init__(self, own, edges, main, side, sems, where, counts):
        self.own, self.edges, self.main, self.side = own, edges, main, side
        self.send, self.recv = sems
        self.grp, self.z, self.x, self.c = where
        self.nz, self.nx, self.nc = counts
        self.depth, self.lanes = own.shape[1], own.shape[3]
        self.edge_lanes = (self.main.shape[3] - self.lanes) // 2

    def inside(self, dz, dx, dc):
        z, x, c = self.z + dz, self.x + dx, self.c + dc
        return both(z >= 0, z < self.nz, x >= 0, x < self.nx, c >= 0, c < self.nc)

    def copy(self, crop, idx):
        dz, dx, dc = DIRS[idx]
        depth, lanes, edge = self.depth, self.lanes, self.edge_lanes
        src_d = {-1: slice(0, HALF), 0: slice(0, depth), 1: slice(depth - HALF, depth)}[dz]
        dst_d = {
            -1: slice(HALF + depth, 2 * HALF + depth),
            0: slice(HALF, HALF + depth),
            1: slice(0, HALF),
        }[dz]
        every = slice(None)
        full = lanes if dx == 0 else lanes // 2
        src_l = {-1: slice(0, edge), 0: slice(0, full), 1: slice(full - edge, full)}[dc]
        dst_l = {
            -1: slice(edge + full, 2 * edge + full),
            0: slice(edge, edge + full),
            1: slice(0, edge),
        }[dc]
        if dx == 0:
            src = self.own.at[crop, src_d, every, src_l]
            dst = self.main.at[crop, dst_d, every, dst_l]
        else:
            src = self.edges.at[0 if dx < 0 else 1, crop, src_d, every, src_l]
            dst = self.side.at[crop, 1 if dx < 0 else 0, dst_d, every, dst_l]
        return pltpu.make_async_remote_copy(
            src_ref=src,
            dst_ref=dst,
            send_sem=self.send.at[crop, idx],
            recv_sem=self.recv.at[crop, idx],
            device_id=(self.grp, self.z + dz, self.x + dx, self.c + dc),
            device_id_type=MESH,
        )

    def fill_edges(self):
        depth, edge = self.depth, self.edge_lanes

        def clear(cond, *areas):
            @pl.when(cond)
            def _():
                for ref, area in areas:
                    view = ref.at[area]
                    view[...] = jnp.zeros(view.shape, view.dtype)

        every = slice(None)
        low, high = slice(0, HALF), slice(HALF + depth, 2 * HALF + depth)
        main, side = self.main, self.side
        clear(self.z == 0, (main, (every, low)), (side, (every, every, low)))
        clear(self.z == self.nz - 1, (main, (every, high)), (side, (every, every, high)))
        clear(self.x == 0, (side, (every, 0)))
        clear(self.x == self.nx - 1, (side, (every, 1)))
        rest = (every, every, every)
        clear(self.c == 0, (main, rest + (slice(0, edge),)), (side, (every,) + rest + (slice(0, edge),)))
        clear(
            self.c == self.nc - 1,
            (main, rest + (slice(main.shape[3] - edge, main.shape[3]),)),
            (side, (every,) + rest + (slice(side.shape[4] - edge, side.shape[4]),)),
        )

    def cut_edges(self, crop):
        half = self.lanes // 2
        for d in range(self.depth):
            for which, first in enumerate((0, EDGE)):
                for part in range(2):
                    self.edges[which, crop, d, part * EDGE : (part + 1) * EDGE, :] = self.own[
                        crop, d, first : first + EDGE, part * half : (part + 1) * half
                    ]

    def start(self, crop, inner):
        for idx, step in enumerate(DIRS):
            if inner != (step[0] == 0):
                continue

            @pl.when(self.inside(*step))
            def _():
                self.copy(crop, idx).start()

    def centre(self, crop):
        depth, lanes, edge = self.depth, self.lanes, self.edge_lanes
        self.main[crop, HALF : HALF + depth, :, edge : edge + lanes] = self.own[crop]

    def arrive(self, crop, inner):
        for idx, (dz, dx, dc) in enumerate(DIRS):
            if inner != (dz == 0):
                continue

            @pl.when(self.inside(-dz, -dx, -dc))
            def _():
                self.copy(crop, idx).wait_recv()

    def finish(self, crop):
        for idx, step in enumerate(DIRS):
            @pl.when(self.inside(*step))
            def _():
                self.copy(crop, idx).wait_send()


def wrap(index, extent):
    return jnp.where(index >= extent, index - extent, index)


def digits(offset, extent):
    if isinstance(offset, int):
        return divmod(offset, extent)
    return offset // extent, lax.rem(offset, extent)


def each(first, last, fn):
    if last - first <= 2 * SUB:
        for offset in range(first, last):
            fn(offset)
        return

    def step(offset, _):
        fn(offset)
        return 0

    lax.fori_loop(first, last, step, 0)


class Reduction:
    def __init__(self, part, bufs, sems, full, out, out_sem, where, counts):
        self.part, self.full, self.out, self.out_sem = part, full, out, out_sem
        self.low, self.band_low, self.inbox_c, self.inbox, self.mine = bufs
        self.hv, self.rs, self.ag, self.sh = sems
        self.grp, self.z, self.x, self.c = where
        self.nz, self.nx, self.nc = counts
        self.squad = self.nz * self.nx
        self.seat = self.z * self.nx + self.x
        self.band = part.shape[0] // self.nc
        self.chunk = self.band // self.squad

    def mate(self, offset):
        other = wrap(self.c + offset, self.nc)
        return other, (self.grp, self.z, self.x, other)

    def fellow(self, offset):
        dz, dx = digits(offset, self.nx)
        other_z, other_x = wrap(self.z + dz, self.nz), wrap(self.x + dx, self.nx)
        return other_z * self.nx + other_x, (self.grp, other_z, other_x, self.c)

    def remote(self, src, dst, sems, idx, device):
        return pltpu.make_async_remote_copy(
            src_ref=src, dst_ref=dst, send_sem=sems[0].at[idx], recv_sem=sems[1].at[idx],
            device_id=device, device_id_type=MESH,
        )

    def rows(self, seat, core):
        return pl.ds(core * self.band + seat * self.chunk, self.chunk)

    def origin(self, offset):
        dz, dx = digits(offset, self.nx)
        from_z = wrap(self.z + self.nz - dz, self.nz)
        return from_z * self.nx + wrap(self.x + self.nx - dx, self.nx)

    def halve(self, offset):
        other, device = self.mate(offset)
        src = self.low.at[pl.ds(other * self.band, self.band)]
        return self.remote(src, self.inbox_c.at[offset], self.hv, offset, device)

    def scatter(self, offset):
        other, device = self.fellow(offset)
        src = self.band_low.at[pl.ds(other * self.chunk, self.chunk)]
        return self.remote(src, self.inbox.at[offset], self.rs, offset, device)

    def spread(self, offset, seat):
        dst = self.full.at[self.rows(seat, self.c)]
        return self.remote(self.mine, dst, self.ag, offset, self.fellow(offset)[1])

    def share(self, offset, step, core):
        rows = self.rows(self.origin(offset), core)
        sems = [sem.at[step] for sem in self.sh]
        return self.remote(
            self.full.at[rows], self.out.at[rows], sems, offset, self.mate(step)[1]
        )

    def write_band(self):
        band = pl.ds(self.c * self.band, self.band)
        return pltpu.make_async_copy(self.full.at[band], self.out.at[band], self.out_sem)

    def start_halves(self):
        self.low[...] = self.part[...].astype(jnp.bfloat16)
        each(1, self.nc, lambda offset: self.halve(offset).start())

    def start_scatter(self):
        each(1, self.nc, lambda offset: self.halve(offset).wait())
        band = pl.ds(self.c * self.band, self.band)
        acc = self.part[band]
        for offset in range(1, self.nc):
            acc = acc + self.inbox_c[offset].astype(jnp.float32)
        self.part[band] = acc
        self.band_low[...] = acc.astype(jnp.bfloat16)
        each(1, self.squad, lambda offset: self.scatter(offset).start())

    def start_spread(self):
        each(1, self.squad, lambda offset: self.scatter(offset).wait())

        def add(offset, acc):
            return acc + self.inbox[offset].astype(jnp.float32)

        acc = self.part[self.rows(self.seat, self.c)]
        if self.squad <= 2 * SUB:
            for offset in range(1, self.squad):
                acc = add(offset, acc)
        else:
            acc = lax.fori_loop(1, self.squad, add, acc)
        self.mine[...] = acc.astype(jnp.bfloat16)
        self.full[self.rows(self.seat, self.c)] = self.mine[...]
        each(1, self.squad, lambda offset: self.spread(offset, self.seat).start())
        each(1, self.nc, lambda step: self.share(0, step, self.c).start())

    def start_share(self):
        def pass_on(offset):
            self.spread(offset, self.origin(offset)).wait_recv()
            each(1, self.nc, lambda step: self.share(offset, step, self.c).start())

        each(1, self.squad, pass_on)
        self.write_band().start()

    def settle(self):
        each(1, self.squad, lambda offset: self.spread(offset, self.seat).wait_send())

        def close(offset):
            def one(step):
                self.share(offset, step, self.c).wait_send()
                core = wrap(self.c + self.nc - step, self.nc)
                self.share(offset, step, core).wait_recv()

            each(1, self.nc, one)

        each(0, self.squad, close)
        self.write_band().wait()


def slot_slices(array, channels):
    return [array[:, s * channels : (s + 1) * channels] for s in range(array.shape[1] // channels)]


def gather_plane(main, side, crop, plane, xs, lane, channels):
    wide = main[crop, plane]
    half = wide.shape[1] // 2
    wide = jnp.concatenate([wide[:, :half], wide[:, half:]], axis=0)
    rim = jnp.concatenate([side[crop, 0, plane], side[crop, 1, plane]], axis=0)
    for n, cell in enumerate(slot_slices(wide, channels) + slot_slices(rim, channels)):
        xs[n * 2 * SUB : (n + 1) * 2 * SUB, lane : lane + channels] = cell


def spectra(halo, crop, xs, table, out, channels, then=None, arrived=False):
    depth, rows = halo.depth, out.shape[2]
    own = list(range(HALF, HALF + depth))
    order = own + [p for p in range(depth + 2 * HALF) if p not in own]
    if not arrived:
        halo.arrive(crop, True)
    for pair in range(len(order) // 2):
        planes = order[2 * pair : 2 * pair + 2]
        if pair == depth // 2:
            if then is not None:
                then()
            halo.arrive(crop, False)
        for q, plane in enumerate(planes):
            gather_plane(halo.main, halo.side, crop, plane, xs.at[pair], q * LANES, channels)
        res = jnp.dot(table[...], xs[pair], preferred_element_type=jnp.float32)
        res = res[:rows] + res[rows:]
        for q, plane in enumerate(planes):
            out[crop, plane] = res[:, q * LANES : (q + 1) * LANES]


def store_split(ref, tile, lane, re, im):
    value = jnp.concatenate([re, im], axis=0)
    high = value.astype(jnp.bfloat16)
    low = (value - high.astype(jnp.float32)).astype(jnp.bfloat16)
    rows = ref.shape[0] // 3
    for n, part in enumerate((high, low, high)):
        first = pl.multiple_of(tile * 2 * SUB, 2 * SUB) + n * rows
        ref[pl.ds(first, 2 * SUB), lane : lane + LANES] = part


def tile_of(ref, lead, tile):
    first = pl.multiple_of(tile * 2 * SUB, 2 * SUB)
    return ref[lead + (pl.ds(first, SUB),)], ref[lead + (pl.ds(first + SUB, SUB),)]


def conv_products(xhat, khat, crop, depth, yhat, flip):
    tiles = yhat.shape[0] // (3 * 2 * SUB)

    def step(tile, _):
        taps = [tile_of(khat, (i,), tile) for i in range(K)]
        data = [tile_of(xhat, (crop, p), tile) for p in range(depth + K - 1)]
        for d in range(depth):
            re = im = None
            for i in range(K):
                kr, ki = taps[i]
                xr, xi = data[d + K - 1 - i if flip else d + i]
                if flip:
                    a, b = xr * kr + xi * ki, xi * kr - xr * ki
                else:
                    a, b = xr * kr - xi * ki, xr * ki + xi * kr
                re, im = (a, b) if re is None else (re + a, im + b)
            store_split(yhat, tile, d * LANES, re, im)
        return 0

    lax.fori_loop(0, tiles, step, 0, unroll=4)


def lag_products(xhat, ohat, crops, depth, ghat):
    tiles = ghat.shape[0] // (3 * 2 * SUB)

    def step(tile, _):
        accs = [[None, None] for _ in range(K)]
        for crop in range(crops):
            data = [tile_of(xhat, (crop, p), tile) for p in range(depth + K - 1)]
            slope = [tile_of(ohat, (crop, d), tile) for d in range(depth)]
            for i in range(K):
                for d in range(depth):
                    xr, xi = data[d + i]
                    sr, si = slope[d]
                    a, b = xr * sr + xi * si, xi * sr - xr * si
                    acc = accs[i]
                    accs[i] = [a, b] if acc[0] is None else [acc[0] + a, acc[1] + b]
        for i in range(K):
            store_split(ghat, tile, i * LANES, accs[i][0], accs[i][1])
        return 0

    lax.fori_loop(0, tiles, step, 0, unroll=4)


def to_native(slots, channels):
    line = jnp.concatenate([slot[:, :channels] for slot in slots], axis=1)
    return jnp.concatenate([line[:SUB], line[SUB:]], axis=1)


def kernel(
    counts, channels, row_of,
    *refs,
):
    count = 16
    operands, (gi_hbm, full_hbm), staged, refs = (
        refs[:count], refs[count : count + 2], refs[count + 2 : 2 * count + 2], refs[2 * count + 2 :]
    )
    (
        x_raw, g_raw, kernel_ref, bias_ref, report_ref, fw_ref, fb_ref, ib_ref, inw_raw, outw_raw,
        f_plane, f_own, f_taps, s_fwd, s_bwd, s_lags,
    ) = staged
    (
    gi_ref, full, load_sems, out_sems,
    inw_ref, outw_ref, x_main, x_side, x_edges, s_own, s_main, s_side, s_edges,
    gs, xs, own_rhs, taps_s, khat, xhat, shat, ohat, yhat, ghat, conv_s,
    vec_ref, norm_s, inv_s, hid_s, pre_s, act_s, act_low, gpre_low, accb, accf, part, part_low, band_low, inbox_c, inbox, mine, taps_part,
    x_send, x_recv, sl_send, sl_recv,
    hv_send, hv_recv, rs_send, rs_recv, ag_send, ag_recv, sh_send, sh_recv,
    ) = refs
    nz, nx, nc = counts
    total = nz * nx * nc
    grp, z, x, c = (lax.axis_index(name) for name in ("groups", "depth", "rows", "cols"))
    crops, depth = x_raw.shape[:2]
    hidden = inw_raw.shape[1]
    voxels = s_fwd.shape[0]
    bf, f32 = jnp.bfloat16, jnp.float32

    def peer(offset):
        rest, dc = digits(offset, nc)
        dz, dx = digits(rest, nx)
        return grp, wrap(z + dz, nz), wrap(x + dx, nx), wrap(c + dc, nc)

    loads = [
        pltpu.make_async_copy(src, dst, load_sems.at[n])
        for n, (src, dst) in enumerate(zip(operands, staged))
    ]
    for n in (0, 12, 2, 10, 1, 3, 4, 5, 6, 7, 8, 9, 13, 11, 15, 14):
        loads[n].start()
    barrier = pltpu.get_barrier_semaphore()

    each(
        1, total,
        lambda offset: pl.semaphore_signal(
            barrier, inc=1, device_id=peer(offset), device_id_type=MESH
        ),
    )
    where = (grp, z, x, c)
    halo_x = Halo(x_raw, x_edges, x_main, x_side, (x_send, x_recv), where, counts)
    halo_s = Halo(s_own, s_edges, s_main, s_side, (sl_send, sl_recv), where, counts)
    loads[0].wait()
    for crop in range(crops):
        halo_x.cut_edges(crop)
    pl.semaphore_wait(barrier, total - 1)
    halo_x.start(0, True)
    halo_x.start(0, False)
    halo_x.fill_edges()
    halo_s.fill_edges()
    for crop in range(crops):
        halo_x.centre(crop)
    for n in (2, 12):
        loads[n].wait()
    spare = LANES - channels
    xs[...] = jnp.zeros_like(xs)
    gs[...] = jnp.zeros_like(gs)
    taps_s[...] = jnp.zeros_like(taps_s)
    for i in range(K):
        for j in range(K):
            taps_s[j * SUB : j * SUB + K, i * LANES : i * LANES + channels] = kernel_ref[
                i, j
            ].astype(f32)
    res = jnp.dot(f_taps[...], taps_s[...].astype(bf), preferred_element_type=f32)
    half = res.shape[0] // 2
    res = res[:half] + res[half:]
    for i in range(K):
        khat[i] = res[:, i * LANES : (i + 1) * LANES]
    for n in (1, 3, 4, 5, 6, 7, 8, 9):
        loads[n].wait()
    for raw, ready in ((inw_raw, inw_ref), (outw_raw, outw_ref)):
        ready[0:channels, :] = raw[...]
        ready[channels:, :] = jnp.zeros((spare, hidden), bf)
    for crop in range(crops):
        for d in range(depth):
            wide = g_raw[crop, d]
            middle = wide.shape[1] // 2
            wide = jnp.concatenate([wide[:, :middle], wide[:, middle:]], axis=0)
            for n, cell in enumerate(slot_slices(wide, channels)):
                first = n * 2 * SUB
                gs[crop, d, first : first + 2 * SUB, 0:channels] = cell
    for crop in range(crops):
        for d in range(depth):
            act_s[crop, d] = jnp.dot(
                gs[crop, d], outw_ref[...], preferred_element_type=f32
            )
    vec_ref[...] = jnp.zeros_like(vec_ref)
    vec_ref[0:1, 0:channels] = bias_ref[...].reshape(1, channels)
    film = lax.dot_general(
        report_ref[...].astype(f32).reshape(1, report_ref.shape[0]).astype(bf), fw_ref[...],
        (((1,), (1,)), ((), ())), preferred_element_type=f32,
    )
    film = film + fb_ref[...].reshape(1, 2 * channels)
    vec_ref[1:2, 0:channels] = film[:, :channels] + 1.0
    vec_ref[2:3, 0:channels] = film[:, channels:]
    accb[...] = jnp.zeros_like(accb)
    accf[...] = jnp.zeros_like(accf)
    tail = row_of["small"] // SUB
    part[tail:] = jnp.zeros((part.shape[0] - tail, SUB, LANES), f32)
    taps_part[...] = jnp.zeros_like(taps_part)

    conv_bias, scale, shift = vec_ref[0:1, :], vec_ref[1:2, :], vec_ref[2:3, :]
    in_bias = ib_ref[...].reshape(1, hidden)
    for n in (10, 13, 11, 15, 14):
        loads[n].wait()
    real = lax.broadcasted_iota(jnp.int32, (1, LANES), 1) < channels

    inner = GELU_C
    outer = GELU_C * 0.044715

    def normalise(crop, d):
        conv = conv_s[d] + conv_bias
        mean = jnp.sum(conv, axis=1, keepdims=True) * (1.0 / channels)
        centred = jnp.where(real, conv - mean, 0.0)
        variance = jnp.sum(centred * centred, axis=1, keepdims=True) * (1.0 / channels)
        inverse = lax.rsqrt(variance + EPSILON)
        normed = centred * inverse
        first = d * voxels
        norm_s[first : first + voxels] = normed
        inv_s[first : first + voxels] = jnp.broadcast_to(inverse, (voxels, LANES))
        hid_s[crop, first : first + voxels] = (normed * scale + shift).astype(bf)

    def activate(crop, d):
        rows = slice(d * voxels, (d + 1) * voxels)
        pre_s[...] = jnp.dot(hid_s[crop, rows], inw_ref[...], preferred_element_type=f32)
        sums = jnp.zeros((2 * SUB, hidden), f32)
        for n in range(voxels // (2 * SUB)):
            part_rows = slice(n * 2 * SUB, (n + 1) * 2 * SUB)
            out_rows = slice(d * voxels + n * 2 * SUB, d * voxels + (n + 1) * 2 * SUB)
            pre = pre_s[part_rows] + in_bias
            square = pre * pre
            half = 0.5 * jnp.tanh(pre * (inner + outer * square)) + 0.5
            act = pre * half
            act_low[crop, out_rows] = act.astype(bf)
            slope_act = half + act * (1.0 - half) * (2.0 * inner + (6.0 * outer) * square)
            grad_pre = act_s[crop, d, part_rows] * slope_act
            gpre_low[crop, out_rows] = grad_pre.astype(bf)
            sums = sums + grad_pre
        accb[...] += sums[:SUB] + sums[SUB:]

    def settle_slope(crop, d):
        rows = slice(d * voxels, (d + 1) * voxels)
        grad_hidden = lax.dot_general(
            gpre_low[crop, rows], inw_ref[...], (((1,), (1,)), ((), ())),
            preferred_element_type=f32,
        )
        normed = norm_s[rows]
        product = grad_hidden * normed
        accf[1] += jnp.sum(product.reshape(voxels // SUB, SUB, LANES), axis=0)
        accf[2] += jnp.sum(grad_hidden.reshape(voxels // SUB, SUB, LANES), axis=0)
        mean_g = jnp.sum(grad_hidden * scale, axis=1, keepdims=True) * (1.0 / channels)
        mean_gn = jnp.sum(product * scale, axis=1, keepdims=True) * (1.0 / channels)
        slope = (grad_hidden * scale - mean_g - normed * mean_gn) * inv_s[rows]
        slope = slope.astype(bf)
        accf[0] += jnp.sum(slope.astype(f32).reshape(voxels // SUB, SUB, LANES), axis=0)
        own_rhs[crop, d] = slope
        s_own[crop, d] = to_native(
            [slope[n * 2 * SUB : (n + 1) * 2 * SUB] for n in range(voxels // (2 * SUB))], channels
        )

    def mlp(crop):
        for stage in (normalise, activate, settle_slope):
            for d in range(depth):
                stage(crop, d)

    def forward(crop, _):
        halo_x.arrive(crop, True)

        @pl.when(crop + 1 < crops)
        def _():
            halo_x.start(crop + 1, True)
            halo_x.start(crop + 1, False)

        spectra(halo_x, crop, xs, f_plane, xhat, channels, arrived=True)
        conv_products(xhat, khat, crop, depth, yhat, False)
        conv = jnp.dot(s_fwd[...], yhat[...], preferred_element_type=f32)
        for d in range(depth):
            conv_s[d] = conv[:, d * LANES : (d + 1) * LANES]

        mlp(crop)
        halo_s.cut_edges(crop)
        halo_s.start(crop, True)
        halo_s.start(crop, False)
        halo_s.centre(crop)
        return 0

    lax.fori_loop(0, crops, forward, 0)

    def own_spectra(step, _):
        crop, pair = step // (depth // 2), step % (depth // 2)
        rhs = jnp.concatenate([own_rhs[crop, 2 * pair], own_rhs[crop, 2 * pair + 1]], axis=1)
        res = jnp.dot(f_own[...], rhs, preferred_element_type=f32)
        res = res[: res.shape[0] // 2] + res[res.shape[0] // 2 :]
        for q in range(2):
            ohat[crop, 2 * pair + q] = res[:, q * LANES : (q + 1) * LANES]
        return 0

    bufs = (part_low, band_low, inbox_c, inbox, mine)
    first_sems = ((hv_send, hv_recv), (rs_send, rs_recv), (ag_send, ag_recv), (sh_send, sh_recv))
    dense = Reduction(
        part, bufs, first_sems, full, full_hbm, out_sems.at[crops], where, counts
    )
    def slope_spectra(crop, then=None):
        spectra(halo_s, crop, xs, f_plane, shat, channels, then)

    def backward(crop):
        conv_products(shat, khat, crop, depth, yhat, True)
        conv = jnp.dot(s_bwd[...], yhat[...], preferred_element_type=f32)
        for d in range(depth):
            total_in = gs[crop, d].astype(f32) + conv[:, d * LANES : (d + 1) * LANES]
            low = total_in.astype(bf)
            gi_ref[crop, d] = to_native(
                [low[n * 2 * SUB : (n + 1) * 2 * SUB] for n in range(voxels // (2 * SUB))],
                channels,
            )

    def gi_out(crop):
        return pltpu.make_async_copy(gi_ref.at[crop], gi_hbm.at[crop], out_sems.at[crop])

    over_voxels = (((0,), (0,)), ((), ()))
    everything = crops * depth * voxels
    for name, left, right in (
        ("in", hid_s[...].reshape(everything, LANES), gpre_low[...].reshape(everything, hidden)),
        ("out", gs[...].reshape(everything, LANES), act_low[...].reshape(everything, hidden)),
    ):
        grads = lax.dot_general(left, right, over_voxels, preferred_element_type=f32)
        for block in range(hidden // LANES):
            first = row_of[name] + block * channels
            piece = grads[0:channels, block * LANES : (block + 1) * LANES]
            part[first // SUB : (first + channels) // SUB] = piece.reshape(
                channels // SUB, SUB, LANES
            )
    for n in range(3):
        row = row_of["small"] + n
        part[row // SUB, row % SUB : row % SUB + 1, :] = jnp.sum(accf[n], axis=0, keepdims=True)
    for block in range(hidden // LANES):
        row = row_of["in_bias"] + block
        part[row // SUB, row % SUB : row % SUB + 1, :] = jnp.sum(
            accb[:, block * LANES : (block + 1) * LANES], axis=0, keepdims=True
        )
    for pair in range(crops * depth // 2):
        own_spectra(pair, 0)
    lag_products(xhat, ohat, crops, depth, ghat)
    lags = jnp.dot(s_lags[...], ghat[...], preferred_element_type=f32)
    for i in range(K):
        rows_i = lags[0 : K * K, i * LANES : (i + 1) * LANES]
        taps_part[i * K * K : (i + 1) * K * K, :] = rows_i
    first_tap = row_of["kernel"] // SUB
    part[first_tap : first_tap + taps_part.shape[0] // SUB] = taps_part[...].reshape(
        taps_part.shape[0] // SUB, SUB, LANES
    )
    dense.start_halves()
    slope_spectra(0, dense.start_scatter)
    backward(0)
    gi_out(0).start()
    dense.start_spread()
    for crop in range(1, crops):
        slope_spectra(crop)
        backward(crop)
        gi_out(crop).start()
    dense.start_share()
    dense.settle()
    for crop in range(crops):
        halo_x.finish(crop)
        halo_s.finish(crop)
        gi_out(crop).wait()


def finish_kernel(
    channels, row_of, factor,
    gi_in, dense_in,
    gi_ref, gk_ref, gb_ref, gf_ref, ginw_ref, gib_ref, goutw_ref,
    dense, red, sems,
):
    load = pltpu.make_async_copy(gi_in, gi_ref, sems.at[0])
    fetch = pltpu.make_async_copy(dense_in, dense, sems.at[1])
    for copy in (load, fetch):
        copy.start()
    fetch.wait()
    hidden = ginw_ref.shape[1]
    for name, out_ref in (("in", ginw_ref), ("out", goutw_ref)):
        for block in range(hidden // LANES):
            first = (row_of[name] + block * channels) // SUB
            piece = dense[first : first + channels // SUB].astype(jnp.float32) * factor
            out_ref[:, block * LANES : (block + 1) * LANES] = piece.reshape(channels, LANES)
    small = row_of["small"] // SUB
    rows = dense[small].astype(jnp.float32) * factor
    gb_ref[...] = rows[0:1, 0:channels].reshape(channels)
    film = [rows[n : n + 1, 0:channels] for n in (1, 2)]
    gf_ref[...] = jnp.concatenate(film, axis=1).reshape(2 * channels)
    lines = [rows[3 + n : 4 + n, :] for n in range(hidden // LANES)]
    gib_ref[...] = jnp.concatenate(lines, axis=1).reshape(hidden)
    first_tap = row_of["kernel"] // SUB
    taps = dense[first_tap : first_tap + red.shape[0] // SUB].astype(jnp.float32)
    red[...] = taps.reshape(red.shape) * factor
    for i in range(K):
        for j in range(K):
            first = (i * K + j) * K
            gk_ref[i, j] = red[first : first + K, 0:channels].reshape(K, 1, channels)
    load.wait()


def local(
    counts, volume, grad_out, report, conv_kernel, conv_bias,
    film_weight, film_bias, in_weight, in_bias, out_weight,
):
    crops, slices, lines, merged = volume.shape
    channels = conv_kernel.shape[0]
    hidden = in_weight.shape[1]
    width = merged // channels
    raw_kernel = jnp.transpose(conv_kernel[:, 0], (1, 2, 3, 0))
    total = counts[0] * counts[1] * counts[2]
    blocks = hidden // LANES
    row_of = {"in": 0, "out": blocks * channels, "small": 2 * blocks * channels}
    row_of["in_bias"] = row_of["small"] + 3
    cores, squad = counts[2], counts[0] * counts[1]
    row_of["kernel"] = -(-(row_of["in_bias"] + blocks) // SUB) * SUB
    taps_rows = -(-K * K * K // SUB) * SUB
    dense_tiles = -(-(row_of["kernel"] + taps_rows) // (SUB * total)) * total
    bf, f32 = jnp.bfloat16, jnp.float32
    dma = pltpu.SemaphoreType.DMA
    tables = fourier_tables(lines, width)
    names = ("plane", "own", "taps", "forward", "backward", "lags")
    spec = tables["plane"].shape[0] // 2
    planes = slices + 2 * HALF
    voxels = lines * width
    edge_lanes = EDGE * channels
    halves = merged // 2 + 2 * edge_lanes
    main = (crops, planes, lines, merged + 2 * edge_lanes)
    side = (crops, 2, planes, 2 * EDGE, halves)
    edges = (2, crops, slices, 2 * EDGE, merged // 2)
    factor = 1.0 / math.sqrt(crops * slices * voxels * total)
    def reduce_buffers(tiles):
        band, chunk = tiles // cores, tiles // total
        return [
            pltpu.VMEM((tiles, SUB, LANES), f32),
            pltpu.VMEM((tiles, SUB, LANES), bf),
            pltpu.VMEM((band, SUB, LANES), bf),
            pltpu.VMEM((cores, band, SUB, LANES), bf),
            pltpu.VMEM((squad, chunk, SUB, LANES), bf),
            pltpu.VMEM((chunk, SUB, LANES), bf),
        ]

    operands = (
        volume,
        grad_out,
        raw_kernel,
        conv_bias,
        report,
        film_weight.T,
        film_bias,
        in_bias,
        in_weight,
        out_weight.T,
        *(tables[name] for name in names),
    )
    gathered = pl.pallas_call(
        functools.partial(kernel, counts, channels, row_of),
        out_shape=(
            jax.ShapeDtypeStruct(volume.shape, bf),
            jax.ShapeDtypeStruct((dense_tiles, SUB, LANES), bf),
        ),
        in_specs=[pl.BlockSpec(memory_space=pltpu.HBM)] * len(operands),
        out_specs=(pl.BlockSpec(memory_space=pltpu.HBM),) * 2,
        scratch_shapes=[pltpu.VMEM(a.shape, a.dtype) for a in operands]
        + [
            pltpu.VMEM(volume.shape, bf),
            pltpu.VMEM((dense_tiles, SUB, LANES), bf),
            dma((len(operands),)),
            dma((crops + 1,)),
            pltpu.VMEM((LANES, hidden), bf),
            pltpu.VMEM((LANES, hidden), bf),
            pltpu.VMEM(main, bf),
            pltpu.VMEM(side, bf),
            pltpu.VMEM(edges, bf),
            pltpu.VMEM(volume.shape, bf),
            pltpu.VMEM(main, bf),
            pltpu.VMEM(side, bf),
            pltpu.VMEM(edges, bf),
            pltpu.VMEM((crops, slices, voxels, LANES), bf),
            pltpu.VMEM((planes // 2, tables["plane"].shape[1], 2 * LANES), bf),
            pltpu.VMEM((crops, slices, voxels, LANES), bf),
            pltpu.VMEM((K * SUB, K * LANES), f32),
            pltpu.VMEM((K, spec, LANES), f32),
            pltpu.VMEM((crops, planes, spec, LANES), f32),
            pltpu.VMEM((crops, planes, spec, LANES), f32),
            pltpu.VMEM((crops, slices, spec, LANES), f32),
            pltpu.VMEM((3 * spec, slices * LANES), bf),
            pltpu.VMEM((3 * spec, K * LANES), bf),
            pltpu.VMEM((slices, voxels, LANES), f32),
            pltpu.VMEM((SUB, LANES), f32),
            pltpu.VMEM((slices * voxels, LANES), f32),
            pltpu.VMEM((slices * voxels, LANES), f32),
            pltpu.VMEM((crops, slices * voxels, LANES), bf),
            pltpu.VMEM((voxels, hidden), f32),
            pltpu.VMEM((crops, slices, voxels, hidden), f32),
            pltpu.VMEM((crops, slices * voxels, hidden), bf),
            pltpu.VMEM((crops, slices * voxels, hidden), bf),
            pltpu.VMEM((SUB, hidden), f32),
            pltpu.VMEM((3, SUB, LANES), f32),
            *reduce_buffers(dense_tiles),
            pltpu.VMEM((taps_rows, LANES), f32),
        ]
        + [dma((crops, len(DIRS)))] * 4
        + [dma((cores,))] * 2 + [dma((squad,))] * 4 + [dma((cores, squad))] * 2,
        compiler_params=pltpu.CompilerParams(
            collective_id=0, has_side_effects=True, vmem_limit_bytes=60 * 1024 * 1024
        ),
        name="block",
    )(*operands)
    grad_input, grad_kernel, grad_bias, grad_film, grad_in_w, grad_in_b, grad_out_w = pl.pallas_call(
        functools.partial(finish_kernel, channels, row_of, factor),
        out_shape=(
            jax.ShapeDtypeStruct(volume.shape, bf),
            jax.ShapeDtypeStruct((K, K, K, 1, channels), f32),
            jax.ShapeDtypeStruct((channels,), f32),
            jax.ShapeDtypeStruct((2 * channels,), f32),
            jax.ShapeDtypeStruct((channels, hidden), f32),
            jax.ShapeDtypeStruct((hidden,), f32),
            jax.ShapeDtypeStruct((channels, hidden), f32),
        ),
        in_specs=[pl.BlockSpec(memory_space=pltpu.HBM)] * 2,
        out_specs=(pl.BlockSpec(memory_space=pltpu.VMEM),) * 7,
        scratch_shapes=[
            pltpu.VMEM((dense_tiles, SUB, LANES), bf),
            pltpu.VMEM((taps_rows, LANES), f32),
            dma((2,)),
        ],
        compiler_params=pltpu.CompilerParams(vmem_limit_bytes=60 * 1024 * 1024),
        name="finish",
    )(*gathered)
    grad_kernel = jnp.transpose(grad_kernel, (4, 3, 0, 1, 2))
    return (
        grad_input, grad_kernel, grad_bias, grad_film, grad_in_w, grad_in_b, grad_out_w.T
    )


def solution(mesh):
    split = P("groups", "depth", "rows", "cols")
    in_specs = (split, split, P("groups")) + (P(),) * 7
    out_specs = (
        split,
        P("groups", None, None, None, None),
        P("groups"),
        P("groups"),
        P("groups", None),
        P("groups"),
        P("groups", None),
    )
    counts = tuple(mesh.shape[name] for name in ("depth", "rows", "cols"))
    return jax.shard_map(
        functools.partial(local, counts),
        mesh=mesh,
        in_specs=in_specs,
        out_specs=out_specs,
        check_vma=False,
    )
```

```python
import functools
import math

import jax
import jax.numpy as jnp
import numpy as np
from jax import lax
from jax.experimental import pallas as pl
from jax.experimental.pallas import tpu as pltpu
from jax.sharding import PartitionSpec as P

K = 7
HALF = K // 2
LANES = 128
SUB = 8
EDGE = 4
EPSILON = 1e-06
MESH = pl.DeviceIdType.MESH
GELU_C = math.sqrt(2.0 / math.pi)
DIRS = tuple(
    (dz, dx, dc)
    for dz in (-1, 0, 1)
    for dx in (-1, 0, 1)
    for dc in (-1, 0, 1)
    if (dz, dx, dc) != (0, 0, 0)
)


def both(*conds):
    out = conds[0]
    for cond in conds[1:]:
        out = jnp.logical_and(out, cond)
    return out


def split_bf16(array):
    high = array.astype(jnp.bfloat16)
    low = (array - high.astype(np.float64)).astype(jnp.bfloat16)
    return high, low


def fourier_tables(rows, width):
    points_h, points_w = rows + 2 * HALF, width + 2 * HALF
    half_w = points_w // 2 + 1
    ends = (0, points_w // 2)
    freqs = [
        (a, b)
        for b in range(half_w)
        for a in range(points_h // 2 + 1 if b in ends else points_h)
    ]
    freqs += [None] * (-len(freqs) % SUB)

    def phases(cells):
        table = np.zeros((len(freqs), len(cells)))
        live = np.zeros((len(freqs), len(cells)))
        for f, freq in enumerate(freqs):
            for n, cell in enumerate(cells):
                if freq is not None and cell is not None:
                    turns = (freq[0] * cell[0] % points_h) / points_h
                    turns += (freq[1] * cell[1] % points_w) / points_w
                    table[f, n] = 2.0 * np.pi * turns
                    live[f, n] = 1.0
        return table, live

    def interleave(real, imag):
        tiles = len(freqs) // SUB
        both_parts = np.stack(
            [real.reshape(tiles, SUB, -1), imag.reshape(tiles, SUB, -1)], axis=1
        )
        return both_parts.reshape(2 * len(freqs), -1)

    def combinations(cells):
        angle, live = phases(cells)
        real, imag = np.cos(angle) * live, np.sin(angle) * live
        stacked = np.stack(
            [p.reshape(len(freqs) // SUB, SUB, -1) for p in (real, imag - real, imag + real)], axis=1
        )
        high, low = split_bf16(stacked.reshape(3 * len(freqs), -1))
        return np.concatenate([high, low], axis=0)

    def analysis(cells, sign):
        angle, live = phases(cells)
        high, low = split_bf16(interleave(np.cos(angle) * live, sign * np.sin(angle) * live))
        return np.concatenate([high, low], axis=0)

    def synthesis(cells):
        angle, live = phases(cells)
        lone = [f is not None and f[1] in ends and f[0] in (0, points_h // 2) for f in freqs]
        weight = np.where(np.array(lone), 1.0, 2.0)[:, None] / (points_h * points_w)
        table = interleave(np.cos(angle) * weight * live, -np.sin(angle) * weight * live).T
        high, low = split_bf16(table)
        return np.concatenate([high, high, low], axis=1)

    def padded(h, w):
        inside = -HALF <= h < rows + HALF and -HALF <= w < width + HALF
        return (h + HALF, w + HALF) if inside else None

    columns = width + 2 * EDGE
    plane = []
    for s in range(columns // 2):
        for r in range(2 * SUB):
            plane.append(padded(r % SUB, s + columns // 2 * (r // SUB) - EDGE))
    slots = width // 2 + 2 * EDGE
    for s in range(slots):
        for r in range(2 * SUB):
            h = r % EDGE + (-EDGE if r < SUB else rows)
            top = r % SUB < EDGE
            if top:
                col = None if s < EDGE else (s if s < slots - EDGE else s + width // 2)
            else:
                col = None if s >= slots - EDGE else (s if s < EDGE else s + width // 2)
            plane.append(None if col is None else padded(h, col - EDGE))
    own = [
        (r % SUB, s + width // 2 * (r // SUB)) for s in range(width // 2) for r in range(2 * SUB)
    ]
    taps = [(j, k) if k < K else None for j in range(K) for k in range(SUB)]
    lags = [(n // K, n % K) if n < K * K else None for n in range(K * SUB)]
    return {
        "plane": analysis(plane, -1.0),
        "own": analysis(own, -1.0),
        "taps": combinations(taps),
        "forward": synthesis(own),
        "backward": synthesis([(h + K - 1, w + K - 1) for h, w in own]),
        "lags": synthesis(lags),
    }


class Halo:
    def __init__(self, own, edges, main, side, sems, where, counts):
        self.own, self.edges, self.main, self.side = own, edges, main, side
        self.send, self.recv = sems
        self.grp, self.z, self.x, self.c = where
        self.nz, self.nx, self.nc = counts
        self.depth, self.lanes = own.shape[1], own.shape[3]
        self.edge_lanes = (self.main.shape[3] - self.lanes) // 2

    def inside(self, dz, dx, dc):
        z, x, c = self.z + dz, self.x + dx, self.c + dc
        return both(z >= 0, z < self.nz, x >= 0, x < self.nx, c >= 0, c < self.nc)

    def copy(self, crop, idx):
        dz, dx, dc = DIRS[idx]
        depth, lanes, edge = self.depth, self.lanes, self.edge_lanes
        src_d = {-1: slice(0, HALF), 0: slice(0, depth), 1: slice(depth - HALF, depth)}[dz]
        dst_d = {
            -1: slice(HALF + depth, 2 * HALF + depth),
            0: slice(HALF, HALF + depth),
            1: slice(0, HALF),
        }[dz]
        every = slice(None)
        full = lanes if dx == 0 else lanes // 2
        src_l = {-1: slice(0, edge), 0: slice(0, full), 1: slice(full - edge, full)}[dc]
        dst_l = {
            -1: slice(edge + full, 2 * edge + full),
            0: slice(edge, edge + full),
            1: slice(0, edge),
        }[dc]
        if dx == 0:
            src = self.own.at[crop, src_d, every, src_l]
            dst = self.main.at[crop, dst_d, every, dst_l]
        else:
            src = self.edges.at[0 if dx < 0 else 1, crop, src_d, every, src_l]
            dst = self.side.at[crop, 1 if dx < 0 else 0, dst_d, every, dst_l]
        return pltpu.make_async_remote_copy(
            src_ref=src,
            dst_ref=dst,
            send_sem=self.send.at[crop, idx],
            recv_sem=self.recv.at[crop, idx],
            device_id=(self.grp, self.z + dz, self.x + dx, self.c + dc),
            device_id_type=MESH,
        )

    def fill_edges(self):
        depth, edge = self.depth, self.edge_lanes

        def clear(cond, *areas):
            @pl.when(cond)
            def _():
                for ref, area in areas:
                    view = ref.at[area]
                    view[...] = jnp.zeros(view.shape, view.dtype)

        every = slice(None)
        low, high = slice(0, HALF), slice(HALF + depth, 2 * HALF + depth)
        main, side = self.main, self.side
        clear(self.z == 0, (main, (every, low)), (side, (every, every, low)))
        clear(self.z == self.nz - 1, (main, (every, high)), (side, (every, every, high)))
        clear(self.x == 0, (side, (every, 0)))
        clear(self.x == self.nx - 1, (side, (every, 1)))
        rest = (every, every, every)
        clear(self.c == 0, (main, rest + (slice(0, edge),)), (side, (every,) + rest + (slice(0, edge),)))
        clear(
            self.c == self.nc - 1,
            (main, rest + (slice(main.shape[3] - edge, main.shape[3]),)),
            (side, (every,) + rest + (slice(side.shape[4] - edge, side.shape[4]),)),
        )

    def cut_edges(self, crop):
        half = self.lanes // 2
        for d in range(self.depth):
            for which, first in enumerate((0, EDGE)):
                for part in range(2):
                    self.edges[which, crop, d, part * EDGE : (part + 1) * EDGE, :] = self.own[
                        crop, d, first : first + EDGE, part * half : (part + 1) * half
                    ]

    def start(self, crop, inner):
        for idx, step in enumerate(DIRS):
            if inner != (step[0] == 0):
                continue

            @pl.when(self.inside(*step))
            def _():
                self.copy(crop, idx).start()

    def centre(self, crop):
        depth, lanes, edge = self.depth, self.lanes, self.edge_lanes
        self.main[crop, HALF : HALF + depth, :, edge : edge + lanes] = self.own[crop]

    def arrive(self, crop, inner):
        for idx, (dz, dx, dc) in enumerate(DIRS):
            if inner != (dz == 0):
                continue

            @pl.when(self.inside(-dz, -dx, -dc))
            def _():
                self.copy(crop, idx).wait_recv()

    def finish(self, crop):
        for idx, step in enumerate(DIRS):
            @pl.when(self.inside(*step))
            def _():
                self.copy(crop, idx).wait_send()


def wrap(index, extent):
    return jnp.where(index >= extent, index - extent, index)


def digits(offset, extent):
    if isinstance(offset, int):
        return divmod(offset, extent)
    return offset // extent, lax.rem(offset, extent)


def each(first, last, fn):
    if last - first <= 2 * SUB:
        for offset in range(first, last):
            fn(offset)
        return

    def step(offset, _):
        fn(offset)
        return 0

    lax.fori_loop(first, last, step, 0)


class Reduction:
    def __init__(self, part, bufs, sems, full, out, out_sem, where, counts):
        self.part, self.full, self.out, self.out_sem = part, full, out, out_sem
        self.low, self.band_low, self.inbox_c, self.inbox, self.mine = bufs
        self.hv, self.rs, self.ag, self.sh = sems
        self.grp, self.z, self.x, self.c = where
        self.nz, self.nx, self.nc = counts
        self.squad = self.nz * self.nx
        self.seat = self.z * self.nx + self.x
        self.band = part.shape[0] // self.nc
        self.chunk = self.band // self.squad

    def mate(self, offset):
        other = wrap(self.c + offset, self.nc)
        return other, (self.grp, self.z, self.x, other)

    def fellow(self, offset):
        dz, dx = digits(offset, self.nx)
        other_z, other_x = wrap(self.z + dz, self.nz), wrap(self.x + dx, self.nx)
        return other_z * self.nx + other_x, (self.grp, other_z, other_x, self.c)

    def remote(self, src, dst, sems, idx, device):
        return pltpu.make_async_remote_copy(
            src_ref=src, dst_ref=dst, send_sem=sems[0].at[idx], recv_sem=sems[1].at[idx],
            device_id=device, device_id_type=MESH,
        )

    def rows(self, seat, core):
        return pl.ds(core * self.band + seat * self.chunk, self.chunk)

    def origin(self, offset):
        dz, dx = digits(offset, self.nx)
        from_z = wrap(self.z + self.nz - dz, self.nz)
        return from_z * self.nx + wrap(self.x + self.nx - dx, self.nx)

    def halve(self, offset):
        other, device = self.mate(offset)
        src = self.low.at[pl.ds(other * self.band, self.band)]
        return self.remote(src, self.inbox_c.at[offset], self.hv, offset, device)

    def scatter(self, offset):
        other, device = self.fellow(offset)
        src = self.band_low.at[pl.ds(other * self.chunk, self.chunk)]
        return self.remote(src, self.inbox.at[offset], self.rs, offset, device)

    def spread(self, offset, seat):
        dst = self.full.at[self.rows(seat, self.c)]
        return self.remote(self.mine, dst, self.ag, offset, self.fellow(offset)[1])

    def share(self, offset, step, core):
        rows = self.rows(self.origin(offset), core)
        sems = [sem.at[step] for sem in self.sh]
        return self.remote(
            self.full.at[rows], self.out.at[rows], sems, offset, self.mate(step)[1]
        )

    def write_band(self):
        band = pl.ds(self.c * self.band, self.band)
        return pltpu.make_async_copy(self.full.at[band], self.out.at[band], self.out_sem)

    def start_halves(self):
        self.low[...] = self.part[...].astype(jnp.bfloat16)
        each(1, self.nc, lambda offset: self.halve(offset).start())

    def start_scatter(self):
        each(1, self.nc, lambda offset: self.halve(offset).wait())
        band = pl.ds(self.c * self.band, self.band)
        acc = self.part[band]
        for offset in range(1, self.nc):
            acc = acc + self.inbox_c[offset].astype(jnp.float32)
        self.part[band] = acc
        self.band_low[...] = acc.astype(jnp.bfloat16)
        each(1, self.squad, lambda offset: self.scatter(offset).start())

    def start_spread(self):
        each(1, self.squad, lambda offset: self.scatter(offset).wait())

        def add(offset, acc):
            return acc + self.inbox[offset].astype(jnp.float32)

        acc = self.part[self.rows(self.seat, self.c)]
        if self.squad <= 2 * SUB:
            for offset in range(1, self.squad):
                acc = add(offset, acc)
        else:
            acc = lax.fori_loop(1, self.squad, add, acc)
        self.mine[...] = acc.astype(jnp.bfloat16)
        self.full[self.rows(self.seat, self.c)] = self.mine[...]
        each(1, self.squad, lambda offset: self.spread(offset, self.seat).start())
        each(1, self.nc, lambda step: self.share(0, step, self.c).start())

    def start_share(self):
        def pass_on(offset):
            self.spread(offset, self.origin(offset)).wait_recv()
            each(1, self.nc, lambda step: self.share(offset, step, self.c).start())

        each(1, self.squad, pass_on)
        self.write_band().start()

    def settle(self):
        each(1, self.squad, lambda offset: self.spread(offset, self.seat).wait_send())

        def close(offset):
            def one(step):
                self.share(offset, step, self.c).wait_send()
                core = wrap(self.c + self.nc - step, self.nc)
                self.share(offset, step, core).wait_recv()

            each(1, self.nc, one)

        each(0, self.squad, close)
        self.write_band().wait()


def slot_slices(array, channels):
    return [array[:, s * channels : (s + 1) * channels] for s in range(array.shape[1] // channels)]


def gather_plane(main, side, crop, plane, xs, lane, channels):
    wide = main[crop, plane]
    half = wide.shape[1] // 2
    wide = jnp.concatenate([wide[:, :half], wide[:, half:]], axis=0)
    rim = jnp.concatenate([side[crop, 0, plane], side[crop, 1, plane]], axis=0)
    for n, cell in enumerate(slot_slices(wide, channels) + slot_slices(rim, channels)):
        xs[n * 2 * SUB : (n + 1) * 2 * SUB, lane : lane + channels] = cell


def spectra(halo, crop, xs, table, out, channels, then=None, arrived=False):
    depth, rows = halo.depth, out.shape[2]
    own = list(range(HALF, HALF + depth))
    order = own + [p for p in range(depth + 2 * HALF) if p not in own]
    if not arrived:
        halo.arrive(crop, True)
    for pair in range(len(order) // 2):
        planes = order[2 * pair : 2 * pair + 2]
        if pair == depth // 2:
            if then is not None:
                then()
            halo.arrive(crop, False)
        for q, plane in enumerate(planes):
            gather_plane(halo.main, halo.side, crop, plane, xs.at[pair], q * LANES, channels)
        res = jnp.dot(table[...], xs[pair], preferred_element_type=jnp.float32)
        res = res[:rows] + res[rows:]
        for q, plane in enumerate(planes):
            out[crop, plane] = res[:, q * LANES : (q + 1) * LANES]


def store_split(ref, tile, lane, re, im):
    value = jnp.concatenate([re, im], axis=0)
    high = value.astype(jnp.bfloat16)
    low = (value - high.astype(jnp.float32)).astype(jnp.bfloat16)
    rows = ref.shape[0] // 3
    for n, part in enumerate((high, low, high)):
        first = pl.multiple_of(tile * 2 * SUB, 2 * SUB) + n * rows
        ref[pl.ds(first, 2 * SUB), lane : lane + LANES] = part


def tile_of(ref, lead, tile):
    first = pl.multiple_of(tile * 2 * SUB, 2 * SUB)
    return ref[lead + (pl.ds(first, SUB),)], ref[lead + (pl.ds(first + SUB, SUB),)]


def conv_products(xhat, khat, crop, depth, yhat, flip):
    tiles = yhat.shape[0] // (3 * 2 * SUB)

    def step(tile, _):
        first = pl.multiple_of(tile * 3 * SUB, SUB)
        taps = [
            [khat[i, pl.ds(first + n * SUB, SUB)] for n in range(3)] for i in range(K)
        ]
        data = [tile_of(xhat, (crop, p), tile) for p in range(depth + K - 1)]
        data = [(xr, xi, xr + xi) for xr, xi in data]
        for d in range(depth):
            common = from_real = from_imag = None
            for i in range(K):
                real, less, more = taps[i]
                xr, xi, both_parts = data[d + K - 1 - i if flip else d + i]
                a = both_parts * real
                b, c = (xr * more, xi * less) if flip else (xr * less, xi * more)
                if common is None:
                    common, from_real, from_imag = a, b, c
                else:
                    common, from_real, from_imag = common + a, from_real + b, from_imag + c
            if flip:
                re, im = common + from_imag, common - from_real
            else:
                re, im = common - from_imag, common + from_real
            store_split(yhat, tile, d * LANES, re, im)
        return 0

    lax.fori_loop(0, tiles, step, 0, unroll=4)


def lag_products(xhat, ohat, crops, depth, ghat):
    tiles = ghat.shape[0] // (3 * 2 * SUB)

    def step(tile, _):
        accs = [[None, None] for _ in range(K)]
        for crop in range(crops):
            data = [tile_of(xhat, (crop, p), tile) for p in range(depth + K - 1)]
            slope = [tile_of(ohat, (crop, d), tile) for d in range(depth)]
            for i in range(K):
                for d in range(depth):
                    xr, xi = data[d + i]
                    sr, si = slope[d]
                    a, b = xr * sr + xi * si, xi * sr - xr * si
                    acc = accs[i]
                    accs[i] = [a, b] if acc[0] is None else [acc[0] + a, acc[1] + b]
        for i in range(K):
            store_split(ghat, tile, i * LANES, accs[i][0], accs[i][1])
        return 0

    lax.fori_loop(0, tiles, step, 0, unroll=4)


def to_native(slots, channels):
    line = jnp.concatenate([slot[:, :channels] for slot in slots], axis=1)
    return jnp.concatenate([line[:SUB], line[SUB:]], axis=1)


def kernel(
    counts, channels, row_of,
    *refs,
):
    count = 16
    operands, (gi_hbm, full_hbm), staged, refs = (
        refs[:count], refs[count : count + 2], refs[count + 2 : 2 * count + 2], refs[2 * count + 2 :]
    )
    (
        x_raw, g_raw, kernel_ref, bias_ref, report_ref, fw_ref, fb_ref, ib_ref, inw_raw, outw_raw,
        f_plane, f_own, f_taps, s_fwd, s_bwd, s_lags,
    ) = staged
    (
    gi_ref, full, load_sems, out_sems,
    inw_ref, outw_ref, x_main, x_side, x_edges, s_own, s_main, s_side, s_edges,
    gs, xs, own_rhs, taps_s, khat, xhat, shat, ohat, yhat, ghat, conv_s,
    vec_ref, norm_s, inv_s, hid_s, pre_s, act_s, act_low, gpre_low, accb, accf, part, part_low, band_low, inbox_c, inbox, mine, taps_part,
    x_send, x_recv, sl_send, sl_recv,
    hv_send, hv_recv, rs_send, rs_recv, ag_send, ag_recv, sh_send, sh_recv,
    ) = refs
    nz, nx, nc = counts
    total = nz * nx * nc
    grp, z, x, c = (lax.axis_index(name) for name in ("groups", "depth", "rows", "cols"))
    crops, depth = x_raw.shape[:2]
    hidden = inw_raw.shape[1]
    voxels = s_fwd.shape[0]
    bf, f32 = jnp.bfloat16, jnp.float32

    def peer(offset):
        rest, dc = digits(offset, nc)
        dz, dx = digits(rest, nx)
        return grp, wrap(z + dz, nz), wrap(x + dx, nx), wrap(c + dc, nc)

    loads = [
        pltpu.make_async_copy(src, dst, load_sems.at[n])
        for n, (src, dst) in enumerate(zip(operands, staged))
    ]
    for n in (0, 12, 2, 10, 1, 3, 4, 5, 6, 7, 8, 9, 13, 11, 15, 14):
        loads[n].start()
    barrier = pltpu.get_barrier_semaphore()

    each(
        1, total,
        lambda offset: pl.semaphore_signal(
            barrier, inc=1, device_id=peer(offset), device_id_type=MESH
        ),
    )
    where = (grp, z, x, c)
    halo_x = Halo(x_raw, x_edges, x_main, x_side, (x_send, x_recv), where, counts)
    halo_s = Halo(s_own, s_edges, s_main, s_side, (sl_send, sl_recv), where, counts)
    loads[0].wait()
    for crop in range(crops):
        halo_x.cut_edges(crop)
    pl.semaphore_wait(barrier, total - 1)
    halo_x.start(0, True)
    halo_x.start(0, False)
    halo_x.fill_edges()
    halo_s.fill_edges()
    for crop in range(crops):
        halo_x.centre(crop)
    for n in (2, 12):
        loads[n].wait()
    spare = LANES - channels
    xs[...] = jnp.zeros_like(xs)
    gs[...] = jnp.zeros_like(gs)
    taps_s[...] = jnp.zeros_like(taps_s)
    for i in range(K):
        for j in range(K):
            taps_s[j * SUB : j * SUB + K, i * LANES : i * LANES + channels] = kernel_ref[
                i, j
            ].astype(f32)
    res = jnp.dot(f_taps[...], taps_s[...].astype(bf), preferred_element_type=f32)
    half = res.shape[0] // 2
    res = res[:half] + res[half:]
    for i in range(K):
        khat[i] = res[:, i * LANES : (i + 1) * LANES]
    for n in (1, 3, 4, 5, 6, 7, 8, 9):
        loads[n].wait()
    for raw, ready in ((inw_raw, inw_ref), (outw_raw, outw_ref)):
        ready[0:channels, :] = raw[...]
        ready[channels:, :] = jnp.zeros((spare, hidden), bf)
    for crop in range(crops):
        for d in range(depth):
            wide = g_raw[crop, d]
            middle = wide.shape[1] // 2
            wide = jnp.concatenate([wide[:, :middle], wide[:, middle:]], axis=0)
            for n, cell in enumerate(slot_slices(wide, channels)):
                first = n * 2 * SUB
                gs[crop, d, first : first + 2 * SUB, 0:channels] = cell
    for crop in range(crops):
        for d in range(depth):
            act_s[crop, d] = jnp.dot(
                gs[crop, d], outw_ref[...], preferred_element_type=f32
            )
    vec_ref[...] = jnp.zeros_like(vec_ref)
    vec_ref[0:1, 0:channels] = bias_ref[...].reshape(1, channels)
    film = lax.dot_general(
        report_ref[...].astype(f32).reshape(1, report_ref.shape[0]).astype(bf), fw_ref[...],
        (((1,), (1,)), ((), ())), preferred_element_type=f32,
    )
    film = film + fb_ref[...].reshape(1, 2 * channels)
    vec_ref[1:2, 0:channels] = film[:, :channels] + 1.0
    vec_ref[2:3, 0:channels] = film[:, channels:]
    accb[...] = jnp.zeros_like(accb)
    accf[...] = jnp.zeros_like(accf)
    tail = row_of["small"] // SUB
    part[tail:] = jnp.zeros((part.shape[0] - tail, SUB, LANES), f32)
    taps_part[...] = jnp.zeros_like(taps_part)

    conv_bias, scale, shift = vec_ref[0:1, :], vec_ref[1:2, :], vec_ref[2:3, :]
    in_bias = ib_ref[...].reshape(1, hidden)
    for n in (10, 13, 11, 15, 14):
        loads[n].wait()
    real = lax.broadcasted_iota(jnp.int32, (1, LANES), 1) < channels

    inner = GELU_C
    outer = GELU_C * 0.044715

    def normalise(crop, d):
        conv = conv_s[d] + conv_bias
        mean = jnp.sum(conv, axis=1, keepdims=True) * (1.0 / channels)
        centred = jnp.where(real, conv - mean, 0.0)
        variance = jnp.sum(centred * centred, axis=1, keepdims=True) * (1.0 / channels)
        inverse = lax.rsqrt(variance + EPSILON)
        normed = centred * inverse
        first = d * voxels
        norm_s[first : first + voxels] = normed
        inv_s[first : first + voxels] = jnp.broadcast_to(inverse, (voxels, LANES))
        hid_s[crop, first : first + voxels] = (normed * scale + shift).astype(bf)

    def activate(crop, d):
        rows = slice(d * voxels, (d + 1) * voxels)
        pre_s[...] = jnp.dot(hid_s[crop, rows], inw_ref[...], preferred_element_type=f32)
        sums = jnp.zeros((2 * SUB, hidden), f32)
        for n in range(voxels // (2 * SUB)):
            part_rows = slice(n * 2 * SUB, (n + 1) * 2 * SUB)
            out_rows = slice(d * voxels + n * 2 * SUB, d * voxels + (n + 1) * 2 * SUB)
            pre = pre_s[part_rows] + in_bias
            square = pre * pre
            half = 0.5 * jnp.tanh(pre * (inner + outer * square)) + 0.5
            act = pre * half
            act_low[crop, out_rows] = act.astype(bf)
            slope_act = half + act * (1.0 - half) * (2.0 * inner + (6.0 * outer) * square)
            grad_pre = act_s[crop, d, part_rows] * slope_act
            gpre_low[crop, out_rows] = grad_pre.astype(bf)
            sums = sums + grad_pre
        accb[...] += sums[:SUB] + sums[SUB:]

    def settle_slope(crop, d):
        rows = slice(d * voxels, (d + 1) * voxels)
        grad_hidden = lax.dot_general(
            gpre_low[crop, rows], inw_ref[...], (((1,), (1,)), ((), ())),
            preferred_element_type=f32,
        )
        normed = norm_s[rows]
        product = grad_hidden * normed
        accf[1] += jnp.sum(product.reshape(voxels // SUB, SUB, LANES), axis=0)
        accf[2] += jnp.sum(grad_hidden.reshape(voxels // SUB, SUB, LANES), axis=0)
        mean_g = jnp.sum(grad_hidden * scale, axis=1, keepdims=True) * (1.0 / channels)
        mean_gn = jnp.sum(product * scale, axis=1, keepdims=True) * (1.0 / channels)
        slope = (grad_hidden * scale - mean_g - normed * mean_gn) * inv_s[rows]
        slope = slope.astype(bf)
        accf[0] += jnp.sum(slope.astype(f32).reshape(voxels // SUB, SUB, LANES), axis=0)
        own_rhs[crop, d] = slope
        s_own[crop, d] = to_native(
            [slope[n * 2 * SUB : (n + 1) * 2 * SUB] for n in range(voxels // (2 * SUB))], channels
        )

    def mlp(crop):
        for stage in (normalise, activate, settle_slope):
            for d in range(depth):
                stage(crop, d)

    def forward(crop, _):
        halo_x.arrive(crop, True)

        @pl.when(crop + 1 < crops)
        def _():
            halo_x.start(crop + 1, True)
            halo_x.start(crop + 1, False)

        spectra(halo_x, crop, xs, f_plane, xhat, channels, arrived=True)
        conv_products(xhat, khat, crop, depth, yhat, False)
        conv = jnp.dot(s_fwd[...], yhat[...], preferred_element_type=f32)
        for d in range(depth):
            conv_s[d] = conv[:, d * LANES : (d + 1) * LANES]

        mlp(crop)
        halo_s.cut_edges(crop)
        halo_s.start(crop, True)
        halo_s.start(crop, False)
        halo_s.centre(crop)
        return 0

    lax.fori_loop(0, crops, forward, 0)

    def own_spectra(step, _):
        crop, pair = step // (depth // 2), step % (depth // 2)
        rhs = jnp.concatenate([own_rhs[crop, 2 * pair], own_rhs[crop, 2 * pair + 1]], axis=1)
        res = jnp.dot(f_own[...], rhs, preferred_element_type=f32)
        res = res[: res.shape[0] // 2] + res[res.shape[0] // 2 :]
        for q in range(2):
            ohat[crop, 2 * pair + q] = res[:, q * LANES : (q + 1) * LANES]
        return 0

    bufs = (part_low, band_low, inbox_c, inbox, mine)
    first_sems = ((hv_send, hv_recv), (rs_send, rs_recv), (ag_send, ag_recv), (sh_send, sh_recv))
    dense = Reduction(
        part, bufs, first_sems, full, full_hbm, out_sems.at[crops], where, counts
    )
    def slope_spectra(crop, then=None):
        spectra(halo_s, crop, xs, f_plane, shat, channels, then)

    def backward(crop):
        conv_products(shat, khat, crop, depth, yhat, True)
        conv = jnp.dot(s_bwd[...], yhat[...], preferred_element_type=f32)
        for d in range(depth):
            total_in = gs[crop, d].astype(f32) + conv[:, d * LANES : (d + 1) * LANES]
            low = total_in.astype(bf)
            gi_ref[crop, d] = to_native(
                [low[n * 2 * SUB : (n + 1) * 2 * SUB] for n in range(voxels // (2 * SUB))],
                channels,
            )

    def gi_out(crop):
        return pltpu.make_async_copy(gi_ref.at[crop], gi_hbm.at[crop], out_sems.at[crop])

    over_voxels = (((0,), (0,)), ((), ()))
    everything = crops * depth * voxels
    for name, left, right in (
        ("in", hid_s[...].reshape(everything, LANES), gpre_low[...].reshape(everything, hidden)),
        ("out", gs[...].reshape(everything, LANES), act_low[...].reshape(everything, hidden)),
    ):
        grads = lax.dot_general(left, right, over_voxels, preferred_element_type=f32)
        for block in range(hidden // LANES):
            first = row_of[name] + block * channels
            piece = grads[0:channels, block * LANES : (block + 1) * LANES]
            part[first // SUB : (first + channels) // SUB] = piece.reshape(
                channels // SUB, SUB, LANES
            )
    for n in range(3):
        row = row_of["small"] + n
        part[row // SUB, row % SUB : row % SUB + 1, :] = jnp.sum(accf[n], axis=0, keepdims=True)
    for block in range(hidden // LANES):
        row = row_of["in_bias"] + block
        part[row // SUB, row % SUB : row % SUB + 1, :] = jnp.sum(
            accb[:, block * LANES : (block + 1) * LANES], axis=0, keepdims=True
        )
    for pair in range(crops * depth // 2):
        own_spectra(pair, 0)
    lag_products(xhat, ohat, crops, depth, ghat)
    lags = jnp.dot(s_lags[...], ghat[...], preferred_element_type=f32)
    for i in range(K):
        rows_i = lags[0 : K * K, i * LANES : (i + 1) * LANES]
        taps_part[i * K * K : (i + 1) * K * K, :] = rows_i
    spare = LANES - channels
    folds = channels // spare
    packed = row_of["packed"]
    extra = packed // folds
    for n in range(folds):
        piece = taps_part[packed : packed + extra, n * spare : (n + 1) * spare]
        taps_part[n * extra : (n + 1) * extra, channels:] = piece
    first_tap = row_of["kernel"] // SUB
    tap_tiles = -(-packed // SUB)
    part[first_tap : first_tap + tap_tiles] = taps_part[0 : tap_tiles * SUB].reshape(
        tap_tiles, SUB, LANES
    )
    dense.start_halves()
    slope_spectra(0, dense.start_scatter)
    backward(0)
    gi_out(0).start()
    dense.start_spread()
    for crop in range(1, crops):
        slope_spectra(crop)
        backward(crop)
        gi_out(crop).start()
    dense.start_share()
    dense.settle()
    for crop in range(crops):
        halo_x.finish(crop)
        halo_s.finish(crop)
        gi_out(crop).wait()


def finish_kernel(
    channels, row_of, factor,
    gi_in, dense_in,
    gi_ref, gk_ref, gb_ref, gf_ref, ginw_ref, gib_ref, goutw_ref,
    dense, red, sems,
):
    load = pltpu.make_async_copy(gi_in, gi_ref, sems.at[0])
    fetch = pltpu.make_async_copy(dense_in, dense, sems.at[1])
    for copy in (load, fetch):
        copy.start()
    fetch.wait()
    hidden = ginw_ref.shape[1]
    for name, out_ref in (("in", ginw_ref), ("out", goutw_ref)):
        for block in range(hidden // LANES):
            first = (row_of[name] + block * channels) // SUB
            piece = dense[first : first + channels // SUB].astype(jnp.float32) * factor
            out_ref[:, block * LANES : (block + 1) * LANES] = piece.reshape(channels, LANES)
    small = row_of["small"] // SUB
    rows = dense[small].astype(jnp.float32) * factor
    gb_ref[...] = rows[0:1, 0:channels].reshape(channels)
    film = [rows[n : n + 1, 0:channels] for n in (1, 2)]
    gf_ref[...] = jnp.concatenate(film, axis=1).reshape(2 * channels)
    lines = [rows[3 + n : 4 + n, :] for n in range(hidden // LANES)]
    gib_ref[...] = jnp.concatenate(lines, axis=1).reshape(hidden)
    first_tap = row_of["kernel"] // SUB
    packed = row_of["packed"]
    tap_tiles = -(-packed // SUB)
    taps = dense[first_tap : first_tap + tap_tiles].astype(jnp.float32)
    red[0 : tap_tiles * SUB] = taps.reshape(tap_tiles * SUB, LANES) * factor
    spare = LANES - channels
    folds = channels // spare
    extra = packed // folds
    for n in range(folds):
        piece = red[n * extra : (n + 1) * extra, channels:]
        red[packed : packed + extra, n * spare : (n + 1) * spare] = piece
    for i in range(K):
        for j in range(K):
            first = (i * K + j) * K
            gk_ref[i, j] = red[first : first + K, 0:channels].reshape(K, 1, channels)
    load.wait()


def local(
    counts, volume, grad_out, report, conv_kernel, conv_bias,
    film_weight, film_bias, in_weight, in_bias, out_weight,
):
    crops, slices, lines, merged = volume.shape
    channels = conv_kernel.shape[0]
    hidden = in_weight.shape[1]
    width = merged // channels
    raw_kernel = jnp.transpose(conv_kernel[:, 0], (1, 2, 3, 0))
    total = counts[0] * counts[1] * counts[2]
    blocks = hidden // LANES
    row_of = {"in": 0, "out": blocks * channels, "small": 2 * blocks * channels}
    row_of["in_bias"] = row_of["small"] + 3
    cores, squad = counts[2], counts[0] * counts[1]
    row_of["kernel"] = -(-(row_of["in_bias"] + blocks) // SUB) * SUB
    folds = channels // (LANES - channels)
    row_of["packed"] = -(-K * K * K // (folds + 1)) * folds
    taps_rows = (-(-K * K * K // SUB) + 1) * SUB
    tap_tiles = -(-row_of["packed"] // SUB)
    dense_tiles = -(-(row_of["kernel"] // SUB + tap_tiles) // total) * total
    bf, f32 = jnp.bfloat16, jnp.float32
    dma = pltpu.SemaphoreType.DMA
    tables = fourier_tables(lines, width)
    names = ("plane", "own", "taps", "forward", "backward", "lags")
    spec = tables["plane"].shape[0] // 2
    planes = slices + 2 * HALF
    voxels = lines * width
    edge_lanes = EDGE * channels
    halves = merged // 2 + 2 * edge_lanes
    main = (crops, planes, lines, merged + 2 * edge_lanes)
    side = (crops, 2, planes, 2 * EDGE, halves)
    edges = (2, crops, slices, 2 * EDGE, merged // 2)
    factor = 1.0 / math.sqrt(crops * slices * voxels * total)
    def reduce_buffers(tiles):
        band, chunk = tiles // cores, tiles // total
        return [
            pltpu.VMEM((tiles, SUB, LANES), f32),
            pltpu.VMEM((tiles, SUB, LANES), bf),
            pltpu.VMEM((band, SUB, LANES), bf),
            pltpu.VMEM((cores, band, SUB, LANES), bf),
            pltpu.VMEM((squad, chunk, SUB, LANES), bf),
            pltpu.VMEM((chunk, SUB, LANES), bf),
        ]

    operands = (
        volume,
        grad_out,
        raw_kernel,
        conv_bias,
        report,
        film_weight.T,
        film_bias,
        in_bias,
        in_weight,
        out_weight.T,
        *(tables[name] for name in names),
    )
    gathered = pl.pallas_call(
        functools.partial(kernel, counts, channels, row_of),
        out_shape=(
            jax.ShapeDtypeStruct(volume.shape, bf),
            jax.ShapeDtypeStruct((dense_tiles, SUB, LANES), bf),
        ),
        in_specs=[pl.BlockSpec(memory_space=pltpu.HBM)] * len(operands),
        out_specs=(pl.BlockSpec(memory_space=pltpu.HBM),) * 2,
        scratch_shapes=[pltpu.VMEM(a.shape, a.dtype) for a in operands]
        + [
            pltpu.VMEM(volume.shape, bf),
            pltpu.VMEM((dense_tiles, SUB, LANES), bf),
            dma((len(operands),)),
            dma((crops + 1,)),
            pltpu.VMEM((LANES, hidden), bf),
            pltpu.VMEM((LANES, hidden), bf),
            pltpu.VMEM(main, bf),
            pltpu.VMEM(side, bf),
            pltpu.VMEM(edges, bf),
            pltpu.VMEM(volume.shape, bf),
            pltpu.VMEM(main, bf),
            pltpu.VMEM(side, bf),
            pltpu.VMEM(edges, bf),
            pltpu.VMEM((crops, slices, voxels, LANES), bf),
            pltpu.VMEM((planes // 2, tables["plane"].shape[1], 2 * LANES), bf),
            pltpu.VMEM((crops, slices, voxels, LANES), bf),
            pltpu.VMEM((K * SUB, K * LANES), f32),
            pltpu.VMEM((K, spec // 2 * 3, LANES), f32),
            pltpu.VMEM((crops, planes, spec, LANES), f32),
            pltpu.VMEM((crops, planes, spec, LANES), f32),
            pltpu.VMEM((crops, slices, spec, LANES), f32),
            pltpu.VMEM((3 * spec, slices * LANES), bf),
            pltpu.VMEM((3 * spec, K * LANES), bf),
            pltpu.VMEM((slices, voxels, LANES), f32),
            pltpu.VMEM((SUB, LANES), f32),
            pltpu.VMEM((slices * voxels, LANES), f32),
            pltpu.VMEM((slices * voxels, LANES), f32),
            pltpu.VMEM((crops, slices * voxels, LANES), bf),
            pltpu.VMEM((voxels, hidden), f32),
            pltpu.VMEM((crops, slices, voxels, hidden), f32),
            pltpu.VMEM((crops, slices * voxels, hidden), bf),
            pltpu.VMEM((crops, slices * voxels, hidden), bf),
            pltpu.VMEM((SUB, hidden), f32),
            pltpu.VMEM((3, SUB, LANES), f32),
            *reduce_buffers(dense_tiles),
            pltpu.VMEM((taps_rows, LANES), f32),
        ]
        + [dma((crops, len(DIRS)))] * 4
        + [dma((cores,))] * 2 + [dma((squad,))] * 4 + [dma((cores, squad))] * 2,
        compiler_params=pltpu.CompilerParams(
            collective_id=0, has_side_effects=True, vmem_limit_bytes=60 * 1024 * 1024
        ),
        name="block",
    )(*operands)
    grad_input, grad_kernel, grad_bias, grad_film, grad_in_w, grad_in_b, grad_out_w = pl.pallas_call(
        functools.partial(finish_kernel, channels, row_of, factor),
        out_shape=(
            jax.ShapeDtypeStruct(volume.shape, bf),
            jax.ShapeDtypeStruct((K, K, K, 1, channels), f32),
            jax.ShapeDtypeStruct((channels,), f32),
            jax.ShapeDtypeStruct((2 * channels,), f32),
            jax.ShapeDtypeStruct((channels, hidden), f32),
            jax.ShapeDtypeStruct((hidden,), f32),
            jax.ShapeDtypeStruct((channels, hidden), f32),
        ),
        in_specs=[pl.BlockSpec(memory_space=pltpu.HBM)] * 2,
        out_specs=(pl.BlockSpec(memory_space=pltpu.VMEM),) * 7,
        scratch_shapes=[
            pltpu.VMEM((dense_tiles, SUB, LANES), bf),
            pltpu.VMEM((taps_rows, LANES), f32),
            dma((2,)),
        ],
        compiler_params=pltpu.CompilerParams(vmem_limit_bytes=60 * 1024 * 1024),
        name="finish",
    )(*gathered)
    grad_kernel = jnp.transpose(grad_kernel, (4, 3, 0, 1, 2))
    return (
        grad_input, grad_kernel, grad_bias, grad_film, grad_in_w, grad_in_b, grad_out_w.T
    )


def solution(mesh):
    split = P("groups", "depth", "rows", "cols")
    in_specs = (split, split, P("groups")) + (P(),) * 7
    out_specs = (
        split,
        P("groups", None, None, None, None),
        P("groups"),
        P("groups"),
        P("groups", None),
        P("groups"),
        P("groups", None),
    )
    counts = tuple(mesh.shape[name] for name in ("depth", "rows", "cols"))
    return jax.shard_map(
        functools.partial(local, counts),
        mesh=mesh,
        in_specs=in_specs,
        out_specs=out_specs,
        check_vma=False,
    )
```

```python
import functools
import math

import jax
import jax.numpy as jnp
import numpy as np
from jax import lax
from jax.experimental import pallas as pl
from jax.experimental.pallas import tpu as pltpu
from jax.sharding import PartitionSpec as P

K = 7
HALF = K // 2
LANES = 128
SUB = 8
EDGE = 4
EPSILON = 1e-06
MESH = pl.DeviceIdType.MESH
GELU_C = math.sqrt(2.0 / math.pi)
DIRS = sorted(
    (
        (dz, dx, dc)
        for dz in (-1, 0, 1)
        for dx in (-1, 0, 1)
        for dc in (-1, 0, 1)
        if (dz, dx, dc) != (0, 0, 0)
    ),
    key=lambda step: (abs(step[0]) + abs(step[1]) + abs(step[2])),
)


def both(*conds):
    out = conds[0]
    for cond in conds[1:]:
        out = jnp.logical_and(out, cond)
    return out


def split_bf16(array):
    high = array.astype(jnp.bfloat16)
    low = (array - high.astype(np.float64)).astype(jnp.bfloat16)
    return high, low


def fourier_tables(rows, width):
    points_h, points_w = rows + 2 * HALF, width + 2 * HALF
    half_w = points_w // 2 + 1
    ends = (0, points_w // 2)
    freqs = [
        (a, b)
        for b in range(half_w)
        for a in range(points_h // 2 + 1 if b in ends else points_h)
    ]
    freqs += [None] * (-len(freqs) % SUB)

    def phases(cells):
        table = np.zeros((len(freqs), len(cells)))
        live = np.zeros((len(freqs), len(cells)))
        for f, freq in enumerate(freqs):
            for n, cell in enumerate(cells):
                if freq is not None and cell is not None:
                    turns = (freq[0] * cell[0] % points_h) / points_h
                    turns += (freq[1] * cell[1] % points_w) / points_w
                    table[f, n] = 2.0 * np.pi * turns
                    live[f, n] = 1.0
        return table, live

    def interleave(real, imag):
        tiles = len(freqs) // SUB
        both_parts = np.stack(
            [real.reshape(tiles, SUB, -1), imag.reshape(tiles, SUB, -1)], axis=1
        )
        return both_parts.reshape(2 * len(freqs), -1)

    def combinations(cells):
        angle, live = phases(cells)
        real, imag = np.cos(angle) * live, np.sin(angle) * live
        stacked = np.stack(
            [p.reshape(len(freqs) // SUB, SUB, -1) for p in (real, imag - real, imag + real)], axis=1
        )
        high, low = split_bf16(stacked.reshape(3 * len(freqs), -1))
        return np.concatenate([high, low], axis=0)

    def analysis(cells, sign):
        angle, live = phases(cells)
        high, low = split_bf16(interleave(np.cos(angle) * live, sign * np.sin(angle) * live))
        return np.concatenate([high, low], axis=0)

    def synthesis(cells):
        angle, live = phases(cells)
        lone = [f is not None and f[1] in ends and f[0] in (0, points_h // 2) for f in freqs]
        weight = np.where(np.array(lone), 1.0, 2.0)[:, None] / (points_h * points_w)
        table = interleave(np.cos(angle) * weight * live, -np.sin(angle) * weight * live).T
        high, low = split_bf16(table)
        return np.concatenate([high, high, low], axis=1)

    def padded(h, w):
        inside = -HALF <= h < rows + HALF and -HALF <= w < width + HALF
        return (h + HALF, w + HALF) if inside else None

    columns = width + 2 * EDGE
    plane = []
    for s in range(columns // 2):
        for r in range(2 * SUB):
            plane.append(padded(r % SUB, s + columns // 2 * (r // SUB) - EDGE))
    slots = width // 2 + 2 * EDGE
    for s in range(slots):
        for r in range(2 * SUB):
            h = r % EDGE + (-EDGE if r < SUB else rows)
            top = r % SUB < EDGE
            if top:
                col = None if s < EDGE else (s if s < slots - EDGE else s + width // 2)
            else:
                col = None if s >= slots - EDGE else (s if s < EDGE else s + width // 2)
            plane.append(None if col is None else padded(h, col - EDGE))
    own = [
        (r % SUB, s + width // 2 * (r // SUB)) for s in range(width // 2) for r in range(2 * SUB)
    ]
    taps = [(j, k) if k < K else None for j in range(K) for k in range(SUB)]
    lags = [(n // K, n % K) if n < K * K else None for n in range(K * SUB)]
    return {
        "plane": analysis(plane, -1.0),
        "own": analysis(own, -1.0),
        "taps": combinations(taps),
        "forward": synthesis(own),
        "backward": synthesis([(h + K - 1, w + K - 1) for h, w in own]),
        "lags": synthesis(lags),
    }


class Halo:
    def __init__(self, own, edges, main, side, sems, where, counts):
        self.own, self.edges, self.main, self.side = own, edges, main, side
        self.send, self.recv = sems
        self.grp, self.z, self.x, self.c = where
        self.nz, self.nx, self.nc = counts
        self.depth, self.lanes = own.shape[1], own.shape[3]
        self.edge_lanes = (self.main.shape[3] - self.lanes) // 2

    def inside(self, dz, dx, dc):
        z, x, c = self.z + dz, self.x + dx, self.c + dc
        return both(z >= 0, z < self.nz, x >= 0, x < self.nx, c >= 0, c < self.nc)

    def copy(self, crop, idx):
        dz, dx, dc = DIRS[idx]
        depth, lanes, edge = self.depth, self.lanes, self.edge_lanes
        src_d = {-1: slice(0, HALF), 0: slice(0, depth), 1: slice(depth - HALF, depth)}[dz]
        dst_d = {
            -1: slice(HALF + depth, 2 * HALF + depth),
            0: slice(HALF, HALF + depth),
            1: slice(0, HALF),
        }[dz]
        every = slice(None)
        full = lanes if dx == 0 else lanes // 2
        src_l = {-1: slice(0, edge), 0: slice(0, full), 1: slice(full - edge, full)}[dc]
        dst_l = {
            -1: slice(edge + full, 2 * edge + full),
            0: slice(edge, edge + full),
            1: slice(0, edge),
        }[dc]
        if dx == 0:
            src = self.own.at[crop, src_d, every, src_l]
            dst = self.main.at[crop, dst_d, every, dst_l]
        else:
            src = self.edges.at[0 if dx < 0 else 1, crop, src_d, every, src_l]
            dst = self.side.at[crop, 1 if dx < 0 else 0, dst_d, every, dst_l]
        return pltpu.make_async_remote_copy(
            src_ref=src,
            dst_ref=dst,
            send_sem=self.send.at[crop, idx],
            recv_sem=self.recv.at[crop, idx],
            device_id=(self.grp, self.z + dz, self.x + dx, self.c + dc),
            device_id_type=MESH,
        )

    def fill_edges(self):
        depth, edge = self.depth, self.edge_lanes

        def clear(cond, *areas):
            @pl.when(cond)
            def _():
                for ref, area in areas:
                    view = ref.at[area]
                    view[...] = jnp.zeros(view.shape, view.dtype)

        every = slice(None)
        low, high = slice(0, HALF), slice(HALF + depth, 2 * HALF + depth)
        main, side = self.main, self.side
        clear(self.z == 0, (main, (every, low)), (side, (every, every, low)))
        clear(self.z == self.nz - 1, (main, (every, high)), (side, (every, every, high)))
        clear(self.x == 0, (side, (every, 0)))
        clear(self.x == self.nx - 1, (side, (every, 1)))
        rest = (every, every, every)
        clear(self.c == 0, (main, rest + (slice(0, edge),)), (side, (every,) + rest + (slice(0, edge),)))
        clear(
            self.c == self.nc - 1,
            (main, rest + (slice(main.shape[3] - edge, main.shape[3]),)),
            (side, (every,) + rest + (slice(side.shape[4] - edge, side.shape[4]),)),
        )

    def cut_edges(self, crop):
        half = self.lanes // 2
        for d in range(self.depth):
            for which, first in enumerate((0, EDGE)):
                for part in range(2):
                    self.edges[which, crop, d, part * EDGE : (part + 1) * EDGE, :] = self.own[
                        crop, d, first : first + EDGE, part * half : (part + 1) * half
                    ]

    def start(self, crop, inner):
        for idx, step in enumerate(DIRS):
            if inner is not None and inner != (step[0] == 0):
                continue

            @pl.when(self.inside(*step))
            def _():
                self.copy(crop, idx).start()

    def centre(self, crop):
        depth, lanes, edge = self.depth, self.lanes, self.edge_lanes
        self.main[crop, HALF : HALF + depth, :, edge : edge + lanes] = self.own[crop]

    def arrive(self, crop, inner):
        for idx, (dz, dx, dc) in enumerate(DIRS):
            if inner != (dz == 0):
                continue

            @pl.when(self.inside(-dz, -dx, -dc))
            def _():
                self.copy(crop, idx).wait_recv()

    def finish(self, crop):
        for idx, step in enumerate(DIRS):
            @pl.when(self.inside(*step))
            def _():
                self.copy(crop, idx).wait_send()


def wrap(index, extent):
    return jnp.where(index >= extent, index - extent, index)


def digits(offset, extent):
    if isinstance(offset, int):
        return divmod(offset, extent)
    return offset // extent, lax.rem(offset, extent)


def each(first, last, fn):
    if last - first <= 2 * SUB:
        for offset in range(first, last):
            fn(offset)
        return

    def step(offset, _):
        fn(offset)
        return 0

    lax.fori_loop(first, last, step, 0)


class Reduction:
    def __init__(self, part, bufs, sems, full, out, out_sem, where, counts):
        self.part, self.full, self.out, self.out_sem = part, full, out, out_sem
        self.low, self.band_low, self.inbox_c, self.inbox, self.mine = bufs
        self.hv, self.rs, self.ag, self.sh = sems
        self.grp, self.z, self.x, self.c = where
        self.nz, self.nx, self.nc = counts
        self.squad = self.nz * self.nx
        self.seat = self.z * self.nx + self.x
        self.band = part.shape[0] // self.nc
        self.chunk = self.band // self.squad

    def mate(self, offset):
        other = wrap(self.c + offset, self.nc)
        return other, (self.grp, self.z, self.x, other)

    def fellow(self, offset):
        dz, dx = digits(offset, self.nx)
        other_z, other_x = wrap(self.z + dz, self.nz), wrap(self.x + dx, self.nx)
        return other_z * self.nx + other_x, (self.grp, other_z, other_x, self.c)

    def remote(self, src, dst, sems, idx, device):
        return pltpu.make_async_remote_copy(
            src_ref=src, dst_ref=dst, send_sem=sems[0].at[idx], recv_sem=sems[1].at[idx],
            device_id=device, device_id_type=MESH,
        )

    def rows(self, seat, core):
        return pl.ds(core * self.band + seat * self.chunk, self.chunk)

    def origin(self, offset):
        dz, dx = digits(offset, self.nx)
        from_z = wrap(self.z + self.nz - dz, self.nz)
        return from_z * self.nx + wrap(self.x + self.nx - dx, self.nx)

    def halve(self, offset):
        other, device = self.mate(offset)
        src = self.low.at[pl.ds(other * self.band, self.band)]
        return self.remote(src, self.inbox_c.at[offset], self.hv, offset, device)

    def scatter(self, offset):
        other, device = self.fellow(offset)
        src = self.band_low.at[pl.ds(other * self.chunk, self.chunk)]
        return self.remote(src, self.inbox.at[offset], self.rs, offset, device)

    def spread(self, offset, seat):
        dst = self.full.at[self.rows(seat, self.c)]
        return self.remote(self.mine, dst, self.ag, offset, self.fellow(offset)[1])

    def share(self, offset, step, core):
        rows = self.rows(self.origin(offset), core)
        sems = [sem.at[step] for sem in self.sh]
        return self.remote(
            self.full.at[rows], self.out.at[rows], sems, offset, self.mate(step)[1]
        )

    def write_band(self):
        band = pl.ds(self.c * self.band, self.band)
        return pltpu.make_async_copy(self.full.at[band], self.out.at[band], self.out_sem)

    def start_halves(self):
        self.low[...] = self.part[...].astype(jnp.bfloat16)
        each(1, self.nc, lambda offset: self.halve(offset).start())

    def start_scatter(self):
        each(1, self.nc, lambda offset: self.halve(offset).wait())
        band = pl.ds(self.c * self.band, self.band)
        acc = self.part[band]
        for offset in range(1, self.nc):
            acc = acc + self.inbox_c[offset].astype(jnp.float32)
        self.part[band] = acc
        self.band_low[...] = acc.astype(jnp.bfloat16)
        each(1, self.squad, lambda offset: self.scatter(offset).start())

    def start_spread(self):
        each(1, self.squad, lambda offset: self.scatter(offset).wait())

        def add(offset, acc):
            return acc + self.inbox[offset].astype(jnp.float32)

        acc = self.part[self.rows(self.seat, self.c)]
        if self.squad <= 2 * SUB:
            for offset in range(1, self.squad):
                acc = add(offset, acc)
        else:
            acc = lax.fori_loop(1, self.squad, add, acc)
        self.mine[...] = acc.astype(jnp.bfloat16)
        self.full[self.rows(self.seat, self.c)] = self.mine[...]
        each(1, self.squad, lambda offset: self.spread(offset, self.seat).start())
        each(1, self.nc, lambda step: self.share(0, step, self.c).start())

    def start_share(self):
        def pass_on(offset):
            self.spread(offset, self.origin(offset)).wait_recv()
            each(1, self.nc, lambda step: self.share(offset, step, self.c).start())

        each(1, self.squad, pass_on)
        self.write_band().start()

    def settle(self):
        each(1, self.squad, lambda offset: self.spread(offset, self.seat).wait_send())

        def close(offset):
            def one(step):
                self.share(offset, step, self.c).wait_send()
                core = wrap(self.c + self.nc - step, self.nc)
                self.share(offset, step, core).wait_recv()

            each(1, self.nc, one)

        each(0, self.squad, close)
        self.write_band().wait()


def slot_slices(array, channels):
    return [array[:, s * channels : (s + 1) * channels] for s in range(array.shape[1] // channels)]


def gather_plane(main, side, crop, plane, xs, lane, channels):
    wide = main[crop, plane]
    half = wide.shape[1] // 2
    wide = jnp.concatenate([wide[:, :half], wide[:, half:]], axis=0)
    rim = jnp.concatenate([side[crop, 0, plane], side[crop, 1, plane]], axis=0)
    for n, cell in enumerate(slot_slices(wide, channels) + slot_slices(rim, channels)):
        xs[n * 2 * SUB : (n + 1) * 2 * SUB, lane : lane + channels] = cell


def spectra(halo, crop, xs, table, out, channels, then=None, arrived=False):
    depth, rows = halo.depth, out.shape[2]
    own = list(range(HALF, HALF + depth))
    order = own + [p for p in range(depth + 2 * HALF) if p not in own]
    if not arrived:
        halo.arrive(crop, True)
    for pair in range(len(order) // 2):
        planes = order[2 * pair : 2 * pair + 2]
        if pair == depth // 2:
            if then is not None:
                then()
            halo.arrive(crop, False)
        for q, plane in enumerate(planes):
            gather_plane(halo.main, halo.side, crop, plane, xs.at[pair], q * LANES, channels)
        res = jnp.dot(table[...], xs[pair], preferred_element_type=jnp.float32)
        res = res[:rows] + res[rows:]
        for q, plane in enumerate(planes):
            out[crop, plane] = res[:, q * LANES : (q + 1) * LANES]


def store_split(ref, tile, lane, re, im):
    value = jnp.concatenate([re, im], axis=0)
    high = value.astype(jnp.bfloat16)
    low = (value - high.astype(jnp.float32)).astype(jnp.bfloat16)
    rows = ref.shape[0] // 3
    for n, part in enumerate((high, low, high)):
        first = pl.multiple_of(tile * 2 * SUB, 2 * SUB) + n * rows
        ref[pl.ds(first, 2 * SUB), lane : lane + LANES] = part


def tile_of(ref, lead, tile):
    first = pl.multiple_of(tile * 2 * SUB, 2 * SUB)
    return ref[lead + (pl.ds(first, SUB),)], ref[lead + (pl.ds(first + SUB, SUB),)]


def conv_products(xhat, khat, crop, depth, yhat, flip):
    tiles = yhat.shape[0] // (3 * 2 * SUB)

    def step(tile, _):
        first = pl.multiple_of(tile * 3 * SUB, SUB)
        taps = [
            [khat[i, pl.ds(first + n * SUB, SUB)] for n in range(3)] for i in range(K)
        ]
        data = [tile_of(xhat, (crop, p), tile) for p in range(depth + K - 1)]
        data = [(xr, xi, xr + xi) for xr, xi in data]
        for d in range(depth):
            common = from_real = from_imag = None
            for i in range(K):
                real, less, more = taps[i]
                xr, xi, both_parts = data[d + K - 1 - i if flip else d + i]
                a = both_parts * real
                b, c = (xr * more, xi * less) if flip else (xr * less, xi * more)
                if common is None:
                    common, from_real, from_imag = a, b, c
                else:
                    common, from_real, from_imag = common + a, from_real + b, from_imag + c
            if flip:
                re, im = common + from_imag, common - from_real
            else:
                re, im = common - from_imag, common + from_real
            store_split(yhat, tile, d * LANES, re, im)
        return 0

    lax.fori_loop(0, tiles, step, 0, unroll=4)


def lag_products(xhat, ohat, crops, depth, ghat):
    tiles = ghat.shape[0] // (3 * 2 * SUB)

    def step(tile, _):
        accs = [[None, None] for _ in range(K)]
        for crop in range(crops):
            data = [tile_of(xhat, (crop, p), tile) for p in range(depth + K - 1)]
            slope = [tile_of(ohat, (crop, d), tile) for d in range(depth)]
            for i in range(K):
                for d in range(depth):
                    xr, xi = data[d + i]
                    sr, si = slope[d]
                    a, b = xr * sr + xi * si, xi * sr - xr * si
                    acc = accs[i]
                    accs[i] = [a, b] if acc[0] is None else [acc[0] + a, acc[1] + b]
        for i in range(K):
            store_split(ghat, tile, i * LANES, accs[i][0], accs[i][1])
        return 0

    lax.fori_loop(0, tiles, step, 0, unroll=4)


def to_native(slots, channels):
    line = jnp.concatenate([slot[:, :channels] for slot in slots], axis=1)
    return jnp.concatenate([line[:SUB], line[SUB:]], axis=1)


def kernel(
    counts, channels, row_of,
    *refs,
):
    count = 16
    operands, (gi_hbm, full_hbm), staged, refs = (
        refs[:count], refs[count : count + 2], refs[count + 2 : 2 * count + 2], refs[2 * count + 2 :]
    )
    (
        x_raw, g_raw, kernel_ref, bias_ref, report_ref, fw_ref, fb_ref, ib_ref, inw_raw, outw_raw,
        f_plane, f_own, f_taps, s_fwd, s_bwd, s_lags,
    ) = staged
    (
    gi_ref, full, load_sems, out_sems,
    inw_ref, outw_ref, x_main, x_side, x_edges, s_own, s_main, s_side, s_edges,
    gs, xs, own_rhs, taps_s, khat, xhat, shat, ohat, yhat, ghat, conv_s,
    vec_ref, norm_s, inv_s, hid_s, pre_s, act_s, act_low, gpre_low, accb, accf, part, part_low, band_low, inbox_c, inbox, mine, taps_part,
    x_send, x_recv, sl_send, sl_recv,
    hv_send, hv_recv, rs_send, rs_recv, ag_send, ag_recv, sh_send, sh_recv,
    ) = refs
    nz, nx, nc = counts
    total = nz * nx * nc
    grp, z, x, c = (lax.axis_index(name) for name in ("groups", "depth", "rows", "cols"))
    crops, depth = x_raw.shape[:2]
    hidden = inw_raw.shape[1]
    voxels = s_fwd.shape[0]
    bf, f32 = jnp.bfloat16, jnp.float32

    def peer(offset):
        rest, dc = digits(offset, nc)
        dz, dx = digits(rest, nx)
        return grp, wrap(z + dz, nz), wrap(x + dx, nx), wrap(c + dc, nc)

    loads = [
        pltpu.make_async_copy(src, dst, load_sems.at[n])
        for n, (src, dst) in enumerate(zip(operands, staged))
    ]
    for n in (0, 12, 2, 10, 1, 3, 4, 5, 6, 7, 8, 9, 13, 11, 15, 14):
        loads[n].start()
    barrier = pltpu.get_barrier_semaphore()

    each(
        1, total,
        lambda offset: pl.semaphore_signal(
            barrier, inc=1, device_id=peer(offset), device_id_type=MESH
        ),
    )
    where = (grp, z, x, c)
    halo_x = Halo(x_raw, x_edges, x_main, x_side, (x_send, x_recv), where, counts)
    halo_s = Halo(s_own, s_edges, s_main, s_side, (sl_send, sl_recv), where, counts)
    loads[0].wait()
    for crop in range(crops):
        halo_x.cut_edges(crop)
    pl.semaphore_wait(barrier, total - 1)
    halo_x.start(0, None)
    halo_x.fill_edges()
    halo_s.fill_edges()
    for crop in range(crops):
        halo_x.centre(crop)
    for n in (2, 12):
        loads[n].wait()
    spare = LANES - channels
    xs[...] = jnp.zeros_like(xs)
    gs[...] = jnp.zeros_like(gs)
    taps_s[...] = jnp.zeros_like(taps_s)
    for i in range(K):
        for j in range(K):
            taps_s[j * SUB : j * SUB + K, i * LANES : i * LANES + channels] = kernel_ref[
                i, j
            ].astype(f32)
    res = jnp.dot(f_taps[...], taps_s[...].astype(bf), preferred_element_type=f32)
    half = res.shape[0] // 2
    res = res[:half] + res[half:]
    for i in range(K):
        khat[i] = res[:, i * LANES : (i + 1) * LANES]
    for n in (1, 3, 4, 5, 6, 7, 8, 9):
        loads[n].wait()
    for raw, ready in ((inw_raw, inw_ref), (outw_raw, outw_ref)):
        ready[0:channels, :] = raw[...]
        ready[channels:, :] = jnp.zeros((spare, hidden), bf)
    for crop in range(crops):
        for d in range(depth):
            wide = g_raw[crop, d]
            middle = wide.shape[1] // 2
            wide = jnp.concatenate([wide[:, :middle], wide[:, middle:]], axis=0)
            for n, cell in enumerate(slot_slices(wide, channels)):
                first = n * 2 * SUB
                gs[crop, d, first : first + 2 * SUB, 0:channels] = cell
    for crop in range(crops):
        for d in range(depth):
            act_s[crop, d] = jnp.dot(
                gs[crop, d], outw_ref[...], preferred_element_type=f32
            )
    vec_ref[...] = jnp.zeros_like(vec_ref)
    vec_ref[0:1, 0:channels] = bias_ref[...].reshape(1, channels)
    film = lax.dot_general(
        report_ref[...].astype(f32).reshape(1, report_ref.shape[0]).astype(bf), fw_ref[...],
        (((1,), (1,)), ((), ())), preferred_element_type=f32,
    )
    film = film + fb_ref[...].reshape(1, 2 * channels)
    vec_ref[1:2, 0:channels] = film[:, :channels] + 1.0
    vec_ref[2:3, 0:channels] = film[:, channels:]
    accb[...] = jnp.zeros_like(accb)
    accf[...] = jnp.zeros_like(accf)
    tail = row_of["small"] // SUB
    part[tail:] = jnp.zeros((part.shape[0] - tail, SUB, LANES), f32)
    taps_part[...] = jnp.zeros_like(taps_part)

    conv_bias, scale, shift = vec_ref[0:1, :], vec_ref[1:2, :], vec_ref[2:3, :]
    in_bias = ib_ref[...].reshape(1, hidden)
    for n in (10, 13, 11, 15, 14):
        loads[n].wait()
    real = lax.broadcasted_iota(jnp.int32, (1, LANES), 1) < channels

    inner = GELU_C
    outer = GELU_C * 0.044715

    def normalise(crop, d):
        conv = conv_s[d] + conv_bias
        mean = jnp.sum(conv, axis=1, keepdims=True) * (1.0 / channels)
        centred = jnp.where(real, conv - mean, 0.0)
        variance = jnp.sum(centred * centred, axis=1, keepdims=True) * (1.0 / channels)
        inverse = lax.rsqrt(variance + EPSILON)
        normed = centred * inverse
        first = d * voxels
        norm_s[first : first + voxels] = normed
        inv_s[first : first + voxels] = jnp.broadcast_to(inverse, (voxels, LANES))
        hid_s[crop, first : first + voxels] = (normed * scale + shift).astype(bf)

    def activate(crop, d):
        rows = slice(d * voxels, (d + 1) * voxels)
        pre_s[...] = jnp.dot(hid_s[crop, rows], inw_ref[...], preferred_element_type=f32)
        sums = jnp.zeros((2 * SUB, hidden), f32)
        for n in range(voxels // (2 * SUB)):
            part_rows = slice(n * 2 * SUB, (n + 1) * 2 * SUB)
            out_rows = slice(d * voxels + n * 2 * SUB, d * voxels + (n + 1) * 2 * SUB)
            pre = pre_s[part_rows] + in_bias
            square = pre * pre
            half = 0.5 * jnp.tanh(pre * (inner + outer * square)) + 0.5
            act = pre * half
            act_low[crop, out_rows] = act.astype(bf)
            slope_act = half + act * (1.0 - half) * (2.0 * inner + (6.0 * outer) * square)
            grad_pre = act_s[crop, d, part_rows] * slope_act
            gpre_low[crop, out_rows] = grad_pre.astype(bf)
            sums = sums + grad_pre
        accb[...] += sums[:SUB] + sums[SUB:]

    def settle_slope(crop, d):
        rows = slice(d * voxels, (d + 1) * voxels)
        grad_hidden = lax.dot_general(
            gpre_low[crop, rows], inw_ref[...], (((1,), (1,)), ((), ())),
            preferred_element_type=f32,
        )
        normed = norm_s[rows]
        product = grad_hidden * normed
        accf[1] += jnp.sum(product.reshape(voxels // SUB, SUB, LANES), axis=0)
        accf[2] += jnp.sum(grad_hidden.reshape(voxels // SUB, SUB, LANES), axis=0)
        mean_g = jnp.sum(grad_hidden * scale, axis=1, keepdims=True) * (1.0 / channels)
        mean_gn = jnp.sum(product * scale, axis=1, keepdims=True) * (1.0 / channels)
        slope = (grad_hidden * scale - mean_g - normed * mean_gn) * inv_s[rows]
        slope = slope.astype(bf)
        accf[0] += jnp.sum(slope.astype(f32).reshape(voxels // SUB, SUB, LANES), axis=0)
        own_rhs[crop, d] = slope
        s_own[crop, d] = to_native(
            [slope[n * 2 * SUB : (n + 1) * 2 * SUB] for n in range(voxels // (2 * SUB))], channels
        )

    def mlp(crop):
        for stage in (normalise, activate, settle_slope):
            for d in range(depth):
                stage(crop, d)

    def forward(crop, _):
        halo_x.arrive(crop, True)

        @pl.when(crop + 1 < crops)
        def _():
            halo_x.start(crop + 1, None)

        spectra(halo_x, crop, xs, f_plane, xhat, channels, arrived=True)
        conv_products(xhat, khat, crop, depth, yhat, False)
        conv = jnp.dot(s_fwd[...], yhat[...], preferred_element_type=f32)
        for d in range(depth):
            conv_s[d] = conv[:, d * LANES : (d + 1) * LANES]

        mlp(crop)
        halo_s.cut_edges(crop)
        halo_s.start(crop, None)
        halo_s.centre(crop)
        return 0

    lax.fori_loop(0, crops, forward, 0)

    def own_spectra(step, _):
        crop, pair = step // (depth // 2), step % (depth // 2)
        rhs = jnp.concatenate([own_rhs[crop, 2 * pair], own_rhs[crop, 2 * pair + 1]], axis=1)
        res = jnp.dot(f_own[...], rhs, preferred_element_type=f32)
        res = res[: res.shape[0] // 2] + res[res.shape[0] // 2 :]
        for q in range(2):
            ohat[crop, 2 * pair + q] = res[:, q * LANES : (q + 1) * LANES]
        return 0

    bufs = (part_low, band_low, inbox_c, inbox, mine)
    first_sems = ((hv_send, hv_recv), (rs_send, rs_recv), (ag_send, ag_recv), (sh_send, sh_recv))
    dense = Reduction(
        part, bufs, first_sems, full, full_hbm, out_sems.at[crops], where, counts
    )
    def slope_spectra(crop, then=None):
        spectra(halo_s, crop, xs, f_plane, shat, channels, then)

    def backward(crop):
        conv_products(shat, khat, crop, depth, yhat, True)
        conv = jnp.dot(s_bwd[...], yhat[...], preferred_element_type=f32)
        for d in range(depth):
            total_in = gs[crop, d].astype(f32) + conv[:, d * LANES : (d + 1) * LANES]
            low = total_in.astype(bf)
            gi_ref[crop, d] = to_native(
                [low[n * 2 * SUB : (n + 1) * 2 * SUB] for n in range(voxels // (2 * SUB))],
                channels,
            )

    def gi_out(crop):
        return pltpu.make_async_copy(gi_ref.at[crop], gi_hbm.at[crop], out_sems.at[crop])

    over_voxels = (((0,), (0,)), ((), ()))
    everything = crops * depth * voxels
    for name, left, right in (
        ("in", hid_s[...].reshape(everything, LANES), gpre_low[...].reshape(everything, hidden)),
        ("out", gs[...].reshape(everything, LANES), act_low[...].reshape(everything, hidden)),
    ):
        grads = lax.dot_general(left, right, over_voxels, preferred_element_type=f32)
        for block in range(hidden // LANES):
            first = row_of[name] + block * channels
            piece = grads[0:channels, block * LANES : (block + 1) * LANES]
            part[first // SUB : (first + channels) // SUB] = piece.reshape(
                channels // SUB, SUB, LANES
            )
    for n in range(3):
        row = row_of["small"] + n
        part[row // SUB, row % SUB : row % SUB + 1, :] = jnp.sum(accf[n], axis=0, keepdims=True)
    for block in range(hidden // LANES):
        row = row_of["in_bias"] + block
        part[row // SUB, row % SUB : row % SUB + 1, :] = jnp.sum(
            accb[:, block * LANES : (block + 1) * LANES], axis=0, keepdims=True
        )
    for pair in range(crops * depth // 2):
        own_spectra(pair, 0)
    lag_products(xhat, ohat, crops, depth, ghat)
    lags = jnp.dot(s_lags[...], ghat[...], preferred_element_type=f32)
    for i in range(K):
        rows_i = lags[0 : K * K, i * LANES : (i + 1) * LANES]
        taps_part[i * K * K : (i + 1) * K * K, :] = rows_i
    spare = LANES - channels
    folds = channels // spare
    packed = row_of["packed"]
    extra = packed // folds
    for n in range(folds):
        piece = taps_part[packed : packed + extra, n * spare : (n + 1) * spare]
        taps_part[n * extra : (n + 1) * extra, channels:] = piece
    first_tap = row_of["kernel"] // SUB
    tap_tiles = -(-packed // SUB)
    part[first_tap : first_tap + tap_tiles] = taps_part[0 : tap_tiles * SUB].reshape(
        tap_tiles, SUB, LANES
    )
    dense.start_halves()
    slope_spectra(0, dense.start_scatter)
    backward(0)
    gi_out(0).start()
    dense.start_spread()
    for crop in range(1, crops):
        slope_spectra(crop)
        backward(crop)
        gi_out(crop).start()
    dense.start_share()
    dense.settle()
    for crop in range(crops):
        halo_x.finish(crop)
        halo_s.finish(crop)
        gi_out(crop).wait()


def finish_kernel(
    channels, row_of, factor,
    gi_in, dense_in,
    gi_ref, gk_ref, gb_ref, gf_ref, ginw_ref, gib_ref, goutw_ref,
    dense, red, sems,
):
    load = pltpu.make_async_copy(gi_in, gi_ref, sems.at[0])
    fetch = pltpu.make_async_copy(dense_in, dense, sems.at[1])
    for copy in (load, fetch):
        copy.start()
    fetch.wait()
    hidden = ginw_ref.shape[1]
    for name, out_ref in (("in", ginw_ref), ("out", goutw_ref)):
        for block in range(hidden // LANES):
            first = (row_of[name] + block * channels) // SUB
            piece = dense[first : first + channels // SUB].astype(jnp.float32) * factor
            out_ref[:, block * LANES : (block + 1) * LANES] = piece.reshape(channels, LANES)
    small = row_of["small"] // SUB
    rows = dense[small].astype(jnp.float32) * factor
    gb_ref[...] = rows[0:1, 0:channels].reshape(channels)
    film = [rows[n : n + 1, 0:channels] for n in (1, 2)]
    gf_ref[...] = jnp.concatenate(film, axis=1).reshape(2 * channels)
    lines = [rows[3 + n : 4 + n, :] for n in range(hidden // LANES)]
    gib_ref[...] = jnp.concatenate(lines, axis=1).reshape(hidden)
    first_tap = row_of["kernel"] // SUB
    packed = row_of["packed"]
    tap_tiles = -(-packed // SUB)
    taps = dense[first_tap : first_tap + tap_tiles].astype(jnp.float32)
    red[0 : tap_tiles * SUB] = taps.reshape(tap_tiles * SUB, LANES) * factor
    spare = LANES - channels
    folds = channels // spare
    extra = packed // folds
    for n in range(folds):
        piece = red[n * extra : (n + 1) * extra, channels:]
        red[packed : packed + extra, n * spare : (n + 1) * spare] = piece
    for i in range(K):
        for j in range(K):
            first = (i * K + j) * K
            gk_ref[i, j] = red[first : first + K, 0:channels].reshape(K, 1, channels)
    load.wait()


def local(
    counts, volume, grad_out, report, conv_kernel, conv_bias,
    film_weight, film_bias, in_weight, in_bias, out_weight,
):
    crops, slices, lines, merged = volume.shape
    channels = conv_kernel.shape[0]
    hidden = in_weight.shape[1]
    width = merged // channels
    raw_kernel = jnp.transpose(conv_kernel[:, 0], (1, 2, 3, 0))
    total = counts[0] * counts[1] * counts[2]
    blocks = hidden // LANES
    row_of = {"in": 0, "out": blocks * channels, "small": 2 * blocks * channels}
    row_of["in_bias"] = row_of["small"] + 3
    cores, squad = counts[2], counts[0] * counts[1]
    row_of["kernel"] = -(-(row_of["in_bias"] + blocks) // SUB) * SUB
    folds = channels // (LANES - channels)
    row_of["packed"] = -(-K * K * K // (folds + 1)) * folds
    taps_rows = (-(-K * K * K // SUB) + 1) * SUB
    tap_tiles = -(-row_of["packed"] // SUB)
    dense_tiles = -(-(row_of["kernel"] // SUB + tap_tiles) // total) * total
    bf, f32 = jnp.bfloat16, jnp.float32
    dma = pltpu.SemaphoreType.DMA
    tables = fourier_tables(lines, width)
    names = ("plane", "own", "taps", "forward", "backward", "lags")
    spec = tables["plane"].shape[0] // 2
    planes = slices + 2 * HALF
    voxels = lines * width
    edge_lanes = EDGE * channels
    halves = merged // 2 + 2 * edge_lanes
    main = (crops, planes, lines, merged + 2 * edge_lanes)
    side = (crops, 2, planes, 2 * EDGE, halves)
    edges = (2, crops, slices, 2 * EDGE, merged // 2)
    factor = 1.0 / math.sqrt(crops * slices * voxels * total)
    def reduce_buffers(tiles):
        band, chunk = tiles // cores, tiles // total
        return [
            pltpu.VMEM((tiles, SUB, LANES), f32),
            pltpu.VMEM((tiles, SUB, LANES), bf),
            pltpu.VMEM((band, SUB, LANES), bf),
            pltpu.VMEM((cores, band, SUB, LANES), bf),
            pltpu.VMEM((squad, chunk, SUB, LANES), bf),
            pltpu.VMEM((chunk, SUB, LANES), bf),
        ]

    operands = (
        volume,
        grad_out,
        raw_kernel,
        conv_bias,
        report,
        film_weight.T,
        film_bias,
        in_bias,
        in_weight,
        out_weight.T,
        *(tables[name] for name in names),
    )
    gathered = pl.pallas_call(
        functools.partial(kernel, counts, channels, row_of),
        out_shape=(
            jax.ShapeDtypeStruct(volume.shape, bf),
            jax.ShapeDtypeStruct((dense_tiles, SUB, LANES), bf),
        ),
        in_specs=[pl.BlockSpec(memory_space=pltpu.HBM)] * len(operands),
        out_specs=(pl.BlockSpec(memory_space=pltpu.HBM),) * 2,
        scratch_shapes=[pltpu.VMEM(a.shape, a.dtype) for a in operands]
        + [
            pltpu.VMEM(volume.shape, bf),
            pltpu.VMEM((dense_tiles, SUB, LANES), bf),
            dma((len(operands),)),
            dma((crops + 1,)),
            pltpu.VMEM((LANES, hidden), bf),
            pltpu.VMEM((LANES, hidden), bf),
            pltpu.VMEM(main, bf),
            pltpu.VMEM(side, bf),
            pltpu.VMEM(edges, bf),
            pltpu.VMEM(volume.shape, bf),
            pltpu.VMEM(main, bf),
            pltpu.VMEM(side, bf),
            pltpu.VMEM(edges, bf),
            pltpu.VMEM((crops, slices, voxels, LANES), bf),
            pltpu.VMEM((planes // 2, tables["plane"].shape[1], 2 * LANES), bf),
            pltpu.VMEM((crops, slices, voxels, LANES), bf),
            pltpu.VMEM((K * SUB, K * LANES), f32),
            pltpu.VMEM((K, spec // 2 * 3, LANES), f32),
            pltpu.VMEM((crops, planes, spec, LANES), f32),
            pltpu.VMEM((crops, planes, spec, LANES), f32),
            pltpu.VMEM((crops, slices, spec, LANES), f32),
            pltpu.VMEM((3 * spec, slices * LANES), bf),
            pltpu.VMEM((3 * spec, K * LANES), bf),
            pltpu.VMEM((slices, voxels, LANES), f32),
            pltpu.VMEM((SUB, LANES), f32),
            pltpu.VMEM((slices * voxels, LANES), f32),
            pltpu.VMEM((slices * voxels, LANES), f32),
            pltpu.VMEM((crops, slices * voxels, LANES), bf),
            pltpu.VMEM((voxels, hidden), f32),
            pltpu.VMEM((crops, slices, voxels, hidden), f32),
            pltpu.VMEM((crops, slices * voxels, hidden), bf),
            pltpu.VMEM((crops, slices * voxels, hidden), bf),
            pltpu.VMEM((SUB, hidden), f32),
            pltpu.VMEM((3, SUB, LANES), f32),
            *reduce_buffers(dense_tiles),
            pltpu.VMEM((taps_rows, LANES), f32),
        ]
        + [dma((crops, len(DIRS)))] * 4
        + [dma((cores,))] * 2 + [dma((squad,))] * 4 + [dma((cores, squad))] * 2,
        compiler_params=pltpu.CompilerParams(
            collective_id=0, has_side_effects=True, vmem_limit_bytes=60 * 1024 * 1024
        ),
        name="block",
    )(*operands)
    grad_input, grad_kernel, grad_bias, grad_film, grad_in_w, grad_in_b, grad_out_w = pl.pallas_call(
        functools.partial(finish_kernel, channels, row_of, factor),
        out_shape=(
            jax.ShapeDtypeStruct(volume.shape, bf),
            jax.ShapeDtypeStruct((K, K, K, 1, channels), f32),
            jax.ShapeDtypeStruct((channels,), f32),
            jax.ShapeDtypeStruct((2 * channels,), f32),
            jax.ShapeDtypeStruct((channels, hidden), f32),
            jax.ShapeDtypeStruct((hidden,), f32),
            jax.ShapeDtypeStruct((channels, hidden), f32),
        ),
        in_specs=[pl.BlockSpec(memory_space=pltpu.HBM)] * 2,
        out_specs=(pl.BlockSpec(memory_space=pltpu.VMEM),) * 7,
        scratch_shapes=[
            pltpu.VMEM((dense_tiles, SUB, LANES), bf),
            pltpu.VMEM((taps_rows, LANES), f32),
            dma((2,)),
        ],
        compiler_params=pltpu.CompilerParams(vmem_limit_bytes=60 * 1024 * 1024),
        name="finish",
    )(*gathered)
    grad_kernel = jnp.transpose(grad_kernel, (4, 3, 0, 1, 2))
    return (
        grad_input, grad_kernel, grad_bias, grad_film, grad_in_w, grad_in_b, grad_out_w.T
    )


def solution(mesh):
    split = P("groups", "depth", "rows", "cols")
    in_specs = (split, split, P("groups")) + (P(),) * 7
    out_specs = (
        split,
        P("groups", None, None, None, None),
        P("groups"),
        P("groups"),
        P("groups", None),
        P("groups"),
        P("groups", None),
    )
    counts = tuple(mesh.shape[name] for name in ("depth", "rows", "cols"))
    return jax.shard_map(
        functools.partial(local, counts),
        mesh=mesh,
        in_specs=in_specs,
        out_specs=out_specs,
        check_vma=False,
    )
```

```python
import functools
import math

import jax
import jax.numpy as jnp
import numpy as np
from jax import lax
from jax.experimental import pallas as pl
from jax.experimental.pallas import tpu as pltpu
from jax.sharding import PartitionSpec as P

K = 7
HALF = K // 2
LANES = 128
SUB = 8
EDGE = 4
EPSILON = 1e-06
MESH = pl.DeviceIdType.MESH
GELU_C = math.sqrt(2.0 / math.pi)
DIRS = sorted(
    (
        (dz, dx, dc)
        for dz in (-1, 0, 1)
        for dx in (-1, 0, 1)
        for dc in (-1, 0, 1)
        if (dz, dx, dc) != (0, 0, 0)
    ),
    key=lambda step: (abs(step[0]) + abs(step[1]) + abs(step[2])),
)


def both(*conds):
    out = conds[0]
    for cond in conds[1:]:
        out = jnp.logical_and(out, cond)
    return out


def split_bf16(array):
    high = array.astype(jnp.bfloat16)
    low = (array - high.astype(np.float64)).astype(jnp.bfloat16)
    return high, low


def fourier_tables(rows, width):
    points_h, points_w = rows + 2 * HALF, width + 2 * HALF
    half_w = points_w // 2 + 1
    ends = (0, points_w // 2)
    freqs = [
        (a, b)
        for b in range(half_w)
        for a in range(points_h // 2 + 1 if b in ends else points_h)
    ]
    freqs += [None] * (-len(freqs) % SUB)

    def phases(cells):
        table = np.zeros((len(freqs), len(cells)))
        live = np.zeros((len(freqs), len(cells)))
        for f, freq in enumerate(freqs):
            for n, cell in enumerate(cells):
                if freq is not None and cell is not None:
                    turns = (freq[0] * cell[0] % points_h) / points_h
                    turns += (freq[1] * cell[1] % points_w) / points_w
                    table[f, n] = 2.0 * np.pi * turns
                    live[f, n] = 1.0
        return table, live

    def interleave(real, imag):
        tiles = len(freqs) // SUB
        both_parts = np.stack(
            [real.reshape(tiles, SUB, -1), imag.reshape(tiles, SUB, -1)], axis=1
        )
        return both_parts.reshape(2 * len(freqs), -1)

    def combinations(cells):
        angle, live = phases(cells)
        real, imag = np.cos(angle) * live, np.sin(angle) * live
        stacked = np.stack(
            [p.reshape(len(freqs) // SUB, SUB, -1) for p in (real, imag - real, imag + real)], axis=1
        )
        high, low = split_bf16(stacked.reshape(3 * len(freqs), -1))
        return np.concatenate([high, low], axis=0)

    def analysis(cells, sign):
        angle, live = phases(cells)
        high, low = split_bf16(interleave(np.cos(angle) * live, sign * np.sin(angle) * live))
        return np.concatenate([high, low], axis=0)

    def synthesis(cells):
        angle, live = phases(cells)
        lone = [f is not None and f[1] in ends and f[0] in (0, points_h // 2) for f in freqs]
        weight = np.where(np.array(lone), 1.0, 2.0)[:, None] / (points_h * points_w)
        table = interleave(np.cos(angle) * weight * live, -np.sin(angle) * weight * live).T
        high, low = split_bf16(table)
        return np.concatenate([high, high, low], axis=1)

    def padded(h, w):
        inside = -HALF <= h < rows + HALF and -HALF <= w < width + HALF
        return (h + HALF, w + HALF) if inside else None

    columns = width + 2 * EDGE
    plane = []
    for s in range(columns // 2):
        for r in range(2 * SUB):
            plane.append(padded(r % SUB, s + columns // 2 * (r // SUB) - EDGE))
    slots = width // 2 + 2 * EDGE
    for s in range(slots):
        for r in range(2 * SUB):
            h = r % EDGE + (-EDGE if r < SUB else rows)
            top = r % SUB < EDGE
            if top:
                col = None if s < EDGE else (s if s < slots - EDGE else s + width // 2)
            else:
                col = None if s >= slots - EDGE else (s if s < EDGE else s + width // 2)
            plane.append(None if col is None else padded(h, col - EDGE))
    own = [
        (r % SUB, s + width // 2 * (r // SUB)) for s in range(width // 2) for r in range(2 * SUB)
    ]
    taps = [(j, k) if k < K else None for j in range(K) for k in range(SUB)]
    lags = [(n // K, n % K) if n < K * K else None for n in range(K * SUB)]
    return {
        "plane": analysis(plane, -1.0),
        "own": analysis(own, -1.0),
        "taps": combinations(taps),
        "forward": synthesis(own),
        "backward": synthesis([(h + K - 1, w + K - 1) for h, w in own]),
        "lags": synthesis(lags),
    }


class Halo:
    def __init__(self, own, edges, main, side, sems, where, counts):
        self.own, self.edges, self.main, self.side = own, edges, main, side
        self.send, self.recv = sems
        self.grp, self.z, self.x, self.c = where
        self.nz, self.nx, self.nc = counts
        self.depth, self.lanes = own.shape[1], own.shape[3]
        self.edge_lanes = (self.main.shape[3] - self.lanes) // 2

    def inside(self, dz, dx, dc):
        z, x, c = self.z + dz, self.x + dx, self.c + dc
        return both(z >= 0, z < self.nz, x >= 0, x < self.nx, c >= 0, c < self.nc)

    def copy(self, crop, idx):
        dz, dx, dc = DIRS[idx]
        depth, lanes, edge = self.depth, self.lanes, self.edge_lanes
        src_d = {-1: slice(0, HALF), 0: slice(0, depth), 1: slice(depth - HALF, depth)}[dz]
        dst_d = {
            -1: slice(HALF + depth, 2 * HALF + depth),
            0: slice(HALF, HALF + depth),
            1: slice(0, HALF),
        }[dz]
        every = slice(None)
        full = lanes if dx == 0 else lanes // 2
        src_l = {-1: slice(0, edge), 0: slice(0, full), 1: slice(full - edge, full)}[dc]
        dst_l = {
            -1: slice(edge + full, 2 * edge + full),
            0: slice(edge, edge + full),
            1: slice(0, edge),
        }[dc]
        if dx == 0:
            src = self.own.at[crop, src_d, every, src_l]
            dst = self.main.at[crop, dst_d, every, dst_l]
        else:
            src = self.edges.at[0 if dx < 0 else 1, crop, src_d, every, src_l]
            dst = self.side.at[crop, 1 if dx < 0 else 0, dst_d, every, dst_l]
        return pltpu.make_async_remote_copy(
            src_ref=src,
            dst_ref=dst,
            send_sem=self.send.at[crop, idx],
            recv_sem=self.recv.at[crop, idx],
            device_id=(self.grp, self.z + dz, self.x + dx, self.c + dc),
            device_id_type=MESH,
        )

    def fill_edges(self):
        depth, edge = self.depth, self.edge_lanes

        def clear(cond, *areas):
            @pl.when(cond)
            def _():
                for ref, area in areas:
                    view = ref.at[area]
                    view[...] = jnp.zeros(view.shape, view.dtype)

        every = slice(None)
        low, high = slice(0, HALF), slice(HALF + depth, 2 * HALF + depth)
        main, side = self.main, self.side
        clear(self.z == 0, (main, (every, low)), (side, (every, every, low)))
        clear(self.z == self.nz - 1, (main, (every, high)), (side, (every, every, high)))
        clear(self.x == 0, (side, (every, 0)))
        clear(self.x == self.nx - 1, (side, (every, 1)))
        rest = (every, every, every)
        clear(self.c == 0, (main, rest + (slice(0, edge),)), (side, (every,) + rest + (slice(0, edge),)))
        clear(
            self.c == self.nc - 1,
            (main, rest + (slice(main.shape[3] - edge, main.shape[3]),)),
            (side, (every,) + rest + (slice(side.shape[4] - edge, side.shape[4]),)),
        )

    def cut_edges(self, crop):
        half = self.lanes // 2
        for d in range(self.depth):
            for which, first in enumerate((0, EDGE)):
                for part in range(2):
                    self.edges[which, crop, d, part * EDGE : (part + 1) * EDGE, :] = self.own[
                        crop, d, first : first + EDGE, part * half : (part + 1) * half
                    ]

    def start(self, crop, inner):
        for idx, step in enumerate(DIRS):
            if inner is not None and inner != (step[0] == 0):
                continue

            @pl.when(self.inside(*step))
            def _():
                self.copy(crop, idx).start()

    def centre(self, crop):
        depth, lanes, edge = self.depth, self.lanes, self.edge_lanes
        self.main[crop, HALF : HALF + depth, :, edge : edge + lanes] = self.own[crop]

    def arrive(self, crop, inner):
        for idx, (dz, dx, dc) in enumerate(DIRS):
            if inner != (dz == 0):
                continue

            @pl.when(self.inside(-dz, -dx, -dc))
            def _():
                self.copy(crop, idx).wait_recv()

    def finish(self, crop):
        for idx, step in enumerate(DIRS):
            @pl.when(self.inside(*step))
            def _():
                self.copy(crop, idx).wait_send()


def wrap(index, extent):
    return jnp.where(index >= extent, index - extent, index)


def digits(offset, extent):
    if isinstance(offset, int):
        return divmod(offset, extent)
    return offset // extent, lax.rem(offset, extent)


def each(first, last, fn):
    if last - first <= 2 * SUB:
        for offset in range(first, last):
            fn(offset)
        return

    def step(offset, _):
        fn(offset)
        return 0

    lax.fori_loop(first, last, step, 0)


class Reduction:
    def __init__(self, part, bufs, sems, full, out, out_sem, where, counts):
        self.part, self.full, self.out, self.out_sem = part, full, out, out_sem
        self.low, self.band_low, self.inbox_c, self.inbox, self.mine = bufs
        self.hv, self.rs, self.ag, self.sh = sems
        self.grp, self.z, self.x, self.c = where
        self.nz, self.nx, self.nc = counts
        self.squad = self.nz * self.nx
        self.seat = self.z * self.nx + self.x
        self.band = part.shape[0] // self.nc
        self.chunk = self.band // self.squad

    def mate(self, offset):
        other = wrap(self.c + offset, self.nc)
        return other, (self.grp, self.z, self.x, other)

    def fellow(self, offset):
        dz, dx = digits(offset, self.nx)
        other_z, other_x = wrap(self.z + dz, self.nz), wrap(self.x + dx, self.nx)
        return other_z * self.nx + other_x, (self.grp, other_z, other_x, self.c)

    def remote(self, src, dst, sems, idx, device):
        return pltpu.make_async_remote_copy(
            src_ref=src, dst_ref=dst, send_sem=sems[0].at[idx], recv_sem=sems[1].at[idx],
            device_id=device, device_id_type=MESH,
        )

    def rows(self, seat, core):
        return pl.ds(core * self.band + seat * self.chunk, self.chunk)

    def origin(self, offset):
        dz, dx = digits(offset, self.nx)
        from_z = wrap(self.z + self.nz - dz, self.nz)
        return from_z * self.nx + wrap(self.x + self.nx - dx, self.nx)

    def halve(self, offset):
        other, device = self.mate(offset)
        src = self.low.at[pl.ds(other * self.band, self.band)]
        return self.remote(src, self.inbox_c.at[offset], self.hv, offset, device)

    def scatter(self, offset):
        other, device = self.fellow(offset)
        src = self.band_low.at[pl.ds(other * self.chunk, self.chunk)]
        return self.remote(src, self.inbox.at[offset], self.rs, offset, device)

    def spread(self, offset, seat):
        dst = self.full.at[self.rows(seat, self.c)]
        return self.remote(self.mine, dst, self.ag, offset, self.fellow(offset)[1])

    def share(self, offset, step, core):
        rows = self.rows(self.origin(offset), core)
        sems = [sem.at[step] for sem in self.sh]
        return self.remote(
            self.full.at[rows], self.out.at[rows], sems, offset, self.mate(step)[1]
        )

    def write_band(self):
        band = pl.ds(self.c * self.band, self.band)
        return pltpu.make_async_copy(self.full.at[band], self.out.at[band], self.out_sem)

    def start_halves(self):
        self.low[...] = self.part[...].astype(jnp.bfloat16)
        each(1, self.nc, lambda offset: self.halve(offset).start())

    def start_scatter(self):
        each(1, self.nc, lambda offset: self.halve(offset).wait())
        band = pl.ds(self.c * self.band, self.band)
        acc = self.part[band]
        for offset in range(1, self.nc):
            acc = acc + self.inbox_c[offset].astype(jnp.float32)
        self.part[band] = acc
        self.band_low[...] = acc.astype(jnp.bfloat16)
        each(1, self.squad, lambda offset: self.scatter(offset).start())

    def start_spread(self):
        each(1, self.squad, lambda offset: self.scatter(offset).wait())

        def add(offset, acc):
            return acc + self.inbox[offset].astype(jnp.float32)

        acc = self.part[self.rows(self.seat, self.c)]
        if self.squad <= 2 * SUB:
            for offset in range(1, self.squad):
                acc = add(offset, acc)
        else:
            acc = lax.fori_loop(1, self.squad, add, acc)
        self.mine[...] = acc.astype(jnp.bfloat16)
        self.full[self.rows(self.seat, self.c)] = self.mine[...]
        each(1, self.squad, lambda offset: self.spread(offset, self.seat).start())
        each(1, self.nc, lambda step: self.share(0, step, self.c).start())

    def start_share(self):
        def pass_on(offset):
            self.spread(offset, self.origin(offset)).wait_recv()
            each(1, self.nc, lambda step: self.share(offset, step, self.c).start())

        each(1, self.squad, pass_on)
        self.write_band().start()

    def settle(self):
        each(1, self.squad, lambda offset: self.spread(offset, self.seat).wait_send())

        def close(offset):
            def one(step):
                self.share(offset, step, self.c).wait_send()
                core = wrap(self.c + self.nc - step, self.nc)
                self.share(offset, step, core).wait_recv()

            each(1, self.nc, one)

        each(0, self.squad, close)
        self.write_band().wait()


def slot_slices(array, channels):
    return [array[:, s * channels : (s + 1) * channels] for s in range(array.shape[1] // channels)]


def gather_plane(main, side, crop, plane, xs, lane, channels):
    wide = main[crop, plane]
    half = wide.shape[1] // 2
    wide = jnp.concatenate([wide[:, :half], wide[:, half:]], axis=0)
    rim = jnp.concatenate([side[crop, 0, plane], side[crop, 1, plane]], axis=0)
    for n, cell in enumerate(slot_slices(wide, channels) + slot_slices(rim, channels)):
        xs[n * 2 * SUB : (n + 1) * 2 * SUB, lane : lane + channels] = cell


def spectra(halo, crop, xs, table, out, channels, then=None, arrived=False):
    depth, rows = halo.depth, out.shape[2]
    own = list(range(HALF, HALF + depth))
    order = own + [p for p in range(depth + 2 * HALF) if p not in own]
    if not arrived:
        halo.arrive(crop, True)
    for pair in range(len(order) // 2):
        planes = order[2 * pair : 2 * pair + 2]
        if pair == depth // 2:
            if then is not None:
                then()
            halo.arrive(crop, False)
        for q, plane in enumerate(planes):
            gather_plane(halo.main, halo.side, crop, plane, xs.at[pair], q * LANES, channels)
        res = jnp.dot(table[...], xs[pair], preferred_element_type=jnp.float32)
        res = res[:rows] + res[rows:]
        for q, plane in enumerate(planes):
            out[crop, plane] = res[:, q * LANES : (q + 1) * LANES]


def store_split(ref, tile, lane, re, im):
    value = jnp.concatenate([re, im], axis=0)
    high = value.astype(jnp.bfloat16)
    low = (value - high.astype(jnp.float32)).astype(jnp.bfloat16)
    rows = ref.shape[0] // 3
    for n, part in enumerate((high, low, high)):
        first = pl.multiple_of(tile * 2 * SUB, 2 * SUB) + n * rows
        ref[pl.ds(first, 2 * SUB), lane : lane + LANES] = part


def tile_of(ref, lead, tile):
    first = pl.multiple_of(tile * 2 * SUB, 2 * SUB)
    return ref[lead + (pl.ds(first, SUB),)], ref[lead + (pl.ds(first + SUB, SUB),)]


def conv_products(xhat, khat, crop, depth, yhat, flip):
    tiles = yhat.shape[0] // (3 * 2 * SUB)

    def step(tile, _):
        first = pl.multiple_of(tile * 3 * SUB, SUB)
        taps = [
            [khat[i, pl.ds(first + n * SUB, SUB)] for n in range(3)] for i in range(K)
        ]
        data = [tile_of(xhat, (crop, p), tile) for p in range(depth + K - 1)]
        data = [(xr, xi, xr + xi) for xr, xi in data]
        for d in range(depth):
            common = from_real = from_imag = None
            for i in range(K):
                real, less, more = taps[i]
                xr, xi, both_parts = data[d + K - 1 - i if flip else d + i]
                a = both_parts * real
                b, c = (xr * more, xi * less) if flip else (xr * less, xi * more)
                if common is None:
                    common, from_real, from_imag = a, b, c
                else:
                    common, from_real, from_imag = common + a, from_real + b, from_imag + c
            if flip:
                re, im = common + from_imag, common - from_real
            else:
                re, im = common - from_imag, common + from_real
            store_split(yhat, tile, d * LANES, re, im)
        return 0

    lax.fori_loop(0, tiles, step, 0, unroll=4)


def lag_products(xhat, ohat, crops, depth, ghat):
    tiles = ghat.shape[0] // (3 * 2 * SUB)

    def step(tile, _):
        accs = [[None] * 3 for _ in range(K)]
        for crop in range(crops):
            data = [tile_of(xhat, (crop, p), tile) for p in range(depth + K - 1)]
            slope = [tile_of(ohat, (crop, d), tile) for d in range(depth)]
            data = [(xr, xi, xr + xi) for xr, xi in data]
            slope = [(sr, si - sr, si + sr) for sr, si in slope]
            for i in range(K):
                for d in range(depth):
                    xr, xi, both_parts = data[d + i]
                    real, less, more = slope[d]
                    terms = [both_parts * real, xi * less, xr * more]
                    old = accs[i]
                    accs[i] = [t if o is None else o + t for o, t in zip(old, terms)]
        accs = [(common + imag, common - real) for common, imag, real in accs]
        for i in range(K):
            store_split(ghat, tile, i * LANES, accs[i][0], accs[i][1])
        return 0

    lax.fori_loop(0, tiles, step, 0, unroll=4)


def to_native(slots, channels):
    line = jnp.concatenate([slot[:, :channels] for slot in slots], axis=1)
    return jnp.concatenate([line[:SUB], line[SUB:]], axis=1)


def kernel(
    counts, channels, row_of,
    *refs,
):
    count = 16
    operands, (gi_hbm, full_hbm), staged, refs = (
        refs[:count], refs[count : count + 2], refs[count + 2 : 2 * count + 2], refs[2 * count + 2 :]
    )
    (
        x_raw, g_raw, kernel_ref, bias_ref, report_ref, fw_ref, fb_ref, ib_ref, inw_raw, outw_raw,
        f_plane, f_own, f_taps, s_fwd, s_bwd, s_lags,
    ) = staged
    (
    gi_ref, full, load_sems, out_sems,
    inw_ref, outw_ref, x_main, x_side, x_edges, s_own, s_main, s_side, s_edges,
    gs, xs, own_rhs, taps_s, khat, xhat, shat, ohat, yhat, ghat, conv_s,
    vec_ref, norm_s, inv_s, hid_s, pre_s, act_s, act_low, gpre_low, accb, accf, part, part_low, band_low, inbox_c, inbox, mine, taps_part,
    x_send, x_recv, sl_send, sl_recv,
    hv_send, hv_recv, rs_send, rs_recv, ag_send, ag_recv, sh_send, sh_recv,
    ) = refs
    nz, nx, nc = counts
    total = nz * nx * nc
    grp, z, x, c = (lax.axis_index(name) for name in ("groups", "depth", "rows", "cols"))
    crops, depth = x_raw.shape[:2]
    hidden = inw_raw.shape[1]
    voxels = s_fwd.shape[0]
    bf, f32 = jnp.bfloat16, jnp.float32

    def peer(offset):
        rest, dc = digits(offset, nc)
        dz, dx = digits(rest, nx)
        return grp, wrap(z + dz, nz), wrap(x + dx, nx), wrap(c + dc, nc)

    loads = [
        pltpu.make_async_copy(src, dst, load_sems.at[n])
        for n, (src, dst) in enumerate(zip(operands, staged))
    ]
    for n in (0, 12, 2, 10, 1, 3, 4, 5, 6, 7, 8, 9, 13, 11, 15, 14):
        loads[n].start()
    barrier = pltpu.get_barrier_semaphore()

    each(
        1, total,
        lambda offset: pl.semaphore_signal(
            barrier, inc=1, device_id=peer(offset), device_id_type=MESH
        ),
    )
    where = (grp, z, x, c)
    halo_x = Halo(x_raw, x_edges, x_main, x_side, (x_send, x_recv), where, counts)
    halo_s = Halo(s_own, s_edges, s_main, s_side, (sl_send, sl_recv), where, counts)
    loads[0].wait()
    for crop in range(crops):
        halo_x.cut_edges(crop)
    pl.semaphore_wait(barrier, total - 1)
    halo_x.start(0, None)
    halo_x.fill_edges()
    halo_s.fill_edges()
    for crop in range(crops):
        halo_x.centre(crop)
    for n in (2, 12):
        loads[n].wait()
    spare = LANES - channels
    xs[...] = jnp.zeros_like(xs)
    gs[...] = jnp.zeros_like(gs)
    taps_s[...] = jnp.zeros_like(taps_s)
    for i in range(K):
        for j in range(K):
            taps_s[j * SUB : j * SUB + K, i * LANES : i * LANES + channels] = kernel_ref[
                i, j
            ].astype(f32)
    res = jnp.dot(f_taps[...], taps_s[...].astype(bf), preferred_element_type=f32)
    half = res.shape[0] // 2
    res = res[:half] + res[half:]
    for i in range(K):
        khat[i] = res[:, i * LANES : (i + 1) * LANES]
    for n in (1, 3, 4, 5, 6, 7, 8, 9):
        loads[n].wait()
    for raw, ready in ((inw_raw, inw_ref), (outw_raw, outw_ref)):
        ready[0:channels, :] = raw[...]
        ready[channels:, :] = jnp.zeros((spare, hidden), bf)
    for crop in range(crops):
        for d in range(depth):
            wide = g_raw[crop, d]
            middle = wide.shape[1] // 2
            wide = jnp.concatenate([wide[:, :middle], wide[:, middle:]], axis=0)
            for n, cell in enumerate(slot_slices(wide, channels)):
                first = n * 2 * SUB
                gs[crop, d, first : first + 2 * SUB, 0:channels] = cell
    for crop in range(crops):
        for d in range(depth):
            act_s[crop, d] = jnp.dot(
                gs[crop, d], outw_ref[...], preferred_element_type=f32
            )
    vec_ref[...] = jnp.zeros_like(vec_ref)
    vec_ref[0:1, 0:channels] = bias_ref[...].reshape(1, channels)
    film = lax.dot_general(
        report_ref[...].astype(f32).reshape(1, report_ref.shape[0]).astype(bf), fw_ref[...],
        (((1,), (1,)), ((), ())), preferred_element_type=f32,
    )
    film = film + fb_ref[...].reshape(1, 2 * channels)
    vec_ref[1:2, 0:channels] = film[:, :channels] + 1.0
    vec_ref[2:3, 0:channels] = film[:, channels:]
    accb[...] = jnp.zeros_like(accb)
    accf[...] = jnp.zeros_like(accf)
    tail = row_of["small"] // SUB
    part[tail:] = jnp.zeros((part.shape[0] - tail, SUB, LANES), f32)
    taps_part[...] = jnp.zeros_like(taps_part)

    conv_bias, scale, shift = vec_ref[0:1, :], vec_ref[1:2, :], vec_ref[2:3, :]
    in_bias = ib_ref[...].reshape(1, hidden)
    for n in (10, 13, 11, 15, 14):
        loads[n].wait()
    real = lax.broadcasted_iota(jnp.int32, (1, LANES), 1) < channels

    inner = GELU_C
    outer = GELU_C * 0.044715

    def normalise(crop, d):
        conv = conv_s[d] + conv_bias
        mean = jnp.sum(conv, axis=1, keepdims=True) * (1.0 / channels)
        centred = jnp.where(real, conv - mean, 0.0)
        variance = jnp.sum(centred * centred, axis=1, keepdims=True) * (1.0 / channels)
        inverse = lax.rsqrt(variance + EPSILON)
        normed = centred * inverse
        first = d * voxels
        norm_s[first : first + voxels] = normed
        inv_s[first : first + voxels] = jnp.broadcast_to(inverse, (voxels, LANES))
        hid_s[crop, first : first + voxels] = (normed * scale + shift).astype(bf)

    def activate(crop, d):
        rows = slice(d * voxels, (d + 1) * voxels)
        pre_s[...] = jnp.dot(hid_s[crop, rows], inw_ref[...], preferred_element_type=f32)
        sums = jnp.zeros((2 * SUB, hidden), f32)
        for n in range(voxels // (2 * SUB)):
            part_rows = slice(n * 2 * SUB, (n + 1) * 2 * SUB)
            out_rows = slice(d * voxels + n * 2 * SUB, d * voxels + (n + 1) * 2 * SUB)
            pre = pre_s[part_rows] + in_bias
            square = pre * pre
            half = 0.5 * jnp.tanh(pre * (inner + outer * square)) + 0.5
            act = pre * half
            act_low[crop, out_rows] = act.astype(bf)
            slope_act = half + act * (1.0 - half) * (2.0 * inner + (6.0 * outer) * square)
            grad_pre = act_s[crop, d, part_rows] * slope_act
            gpre_low[crop, out_rows] = grad_pre.astype(bf)
            sums = sums + grad_pre
        accb[...] += sums[:SUB] + sums[SUB:]

    def settle_slope(crop, d):
        rows = slice(d * voxels, (d + 1) * voxels)
        grad_hidden = lax.dot_general(
            gpre_low[crop, rows], inw_ref[...], (((1,), (1,)), ((), ())),
            preferred_element_type=f32,
        )
        normed = norm_s[rows]
        product = grad_hidden * normed
        accf[1] += jnp.sum(product.reshape(voxels // SUB, SUB, LANES), axis=0)
        accf[2] += jnp.sum(grad_hidden.reshape(voxels // SUB, SUB, LANES), axis=0)
        mean_g = jnp.sum(grad_hidden * scale, axis=1, keepdims=True) * (1.0 / channels)
        mean_gn = jnp.sum(product * scale, axis=1, keepdims=True) * (1.0 / channels)
        slope = (grad_hidden * scale - mean_g - normed * mean_gn) * inv_s[rows]
        slope = slope.astype(bf)
        accf[0] += jnp.sum(slope.astype(f32).reshape(voxels // SUB, SUB, LANES), axis=0)
        own_rhs[crop, d] = slope
        s_own[crop, d] = to_native(
            [slope[n * 2 * SUB : (n + 1) * 2 * SUB] for n in range(voxels // (2 * SUB))], channels
        )

    def mlp(crop):
        for stage in (normalise, activate, settle_slope):
            for d in range(depth):
                stage(crop, d)

    def forward(crop, _):
        halo_x.arrive(crop, True)

        @pl.when(crop + 1 < crops)
        def _():
            halo_x.start(crop + 1, None)

        spectra(halo_x, crop, xs, f_plane, xhat, channels, arrived=True)
        conv_products(xhat, khat, crop, depth, yhat, False)
        conv = jnp.dot(s_fwd[...], yhat[...], preferred_element_type=f32)
        for d in range(depth):
            conv_s[d] = conv[:, d * LANES : (d + 1) * LANES]

        mlp(crop)
        halo_s.cut_edges(crop)
        halo_s.start(crop, None)
        halo_s.centre(crop)
        return 0

    lax.fori_loop(0, crops, forward, 0)

    def own_spectra(step, _):
        crop, pair = step // (depth // 2), step % (depth // 2)
        rhs = jnp.concatenate([own_rhs[crop, 2 * pair], own_rhs[crop, 2 * pair + 1]], axis=1)
        res = jnp.dot(f_own[...], rhs, preferred_element_type=f32)
        res = res[: res.shape[0] // 2] + res[res.shape[0] // 2 :]
        for q in range(2):
            ohat[crop, 2 * pair + q] = res[:, q * LANES : (q + 1) * LANES]
        return 0

    bufs = (part_low, band_low, inbox_c, inbox, mine)
    first_sems = ((hv_send, hv_recv), (rs_send, rs_recv), (ag_send, ag_recv), (sh_send, sh_recv))
    dense = Reduction(
        part, bufs, first_sems, full, full_hbm, out_sems.at[crops], where, counts
    )
    def slope_spectra(crop, then=None):
        spectra(halo_s, crop, xs, f_plane, shat, channels, then)

    def backward(crop):
        conv_products(shat, khat, crop, depth, yhat, True)
        conv = jnp.dot(s_bwd[...], yhat[...], preferred_element_type=f32)
        for d in range(depth):
            total_in = gs[crop, d].astype(f32) + conv[:, d * LANES : (d + 1) * LANES]
            low = total_in.astype(bf)
            gi_ref[crop, d] = to_native(
                [low[n * 2 * SUB : (n + 1) * 2 * SUB] for n in range(voxels // (2 * SUB))],
                channels,
            )

    def gi_out(crop):
        return pltpu.make_async_copy(gi_ref.at[crop], gi_hbm.at[crop], out_sems.at[crop])

    over_voxels = (((0,), (0,)), ((), ()))
    everything = crops * depth * voxels
    for name, left, right in (
        ("in", hid_s[...].reshape(everything, LANES), gpre_low[...].reshape(everything, hidden)),
        ("out", gs[...].reshape(everything, LANES), act_low[...].reshape(everything, hidden)),
    ):
        grads = lax.dot_general(left, right, over_voxels, preferred_element_type=f32)
        for block in range(hidden // LANES):
            first = row_of[name] + block * channels
            piece = grads[0:channels, block * LANES : (block + 1) * LANES]
            part[first // SUB : (first + channels) // SUB] = piece.reshape(
                channels // SUB, SUB, LANES
            )
    for n in range(3):
        row = row_of["small"] + n
        part[row // SUB, row % SUB : row % SUB + 1, :] = jnp.sum(accf[n], axis=0, keepdims=True)
    for block in range(hidden // LANES):
        row = row_of["in_bias"] + block
        part[row // SUB, row % SUB : row % SUB + 1, :] = jnp.sum(
            accb[:, block * LANES : (block + 1) * LANES], axis=0, keepdims=True
        )
    for pair in range(crops * depth // 2):
        own_spectra(pair, 0)
    lag_products(xhat, ohat, crops, depth, ghat)
    lags = jnp.dot(s_lags[...], ghat[...], preferred_element_type=f32)
    for i in range(K):
        rows_i = lags[0 : K * K, i * LANES : (i + 1) * LANES]
        taps_part[i * K * K : (i + 1) * K * K, :] = rows_i
    spare = LANES - channels
    folds = channels // spare
    packed = row_of["packed"]
    extra = packed // folds
    for n in range(folds):
        piece = taps_part[packed : packed + extra, n * spare : (n + 1) * spare]
        taps_part[n * extra : (n + 1) * extra, channels:] = piece
    first_tap = row_of["kernel"] // SUB
    tap_tiles = -(-packed // SUB)
    part[first_tap : first_tap + tap_tiles] = taps_part[0 : tap_tiles * SUB].reshape(
        tap_tiles, SUB, LANES
    )
    dense.start_halves()
    slope_spectra(0, dense.start_scatter)
    backward(0)
    gi_out(0).start()
    dense.start_spread()
    for crop in range(1, crops):
        slope_spectra(crop)
        backward(crop)
        gi_out(crop).start()
    dense.start_share()
    dense.settle()
    for crop in range(crops):
        halo_x.finish(crop)
        halo_s.finish(crop)
        gi_out(crop).wait()


def finish_kernel(
    channels, row_of, factor,
    gi_in, dense_in,
    gi_ref, gk_ref, gb_ref, gf_ref, ginw_ref, gib_ref, goutw_ref,
    dense, red, sems,
):
    load = pltpu.make_async_copy(gi_in, gi_ref, sems.at[0])
    fetch = pltpu.make_async_copy(dense_in, dense, sems.at[1])
    for copy in (load, fetch):
        copy.start()
    fetch.wait()
    hidden = ginw_ref.shape[1]
    for name, out_ref in (("in", ginw_ref), ("out", goutw_ref)):
        for block in range(hidden // LANES):
            first = (row_of[name] + block * channels) // SUB
            piece = dense[first : first + channels // SUB].astype(jnp.float32) * factor
            out_ref[:, block * LANES : (block + 1) * LANES] = piece.reshape(channels, LANES)
    small = row_of["small"] // SUB
    rows = dense[small].astype(jnp.float32) * factor
    gb_ref[...] = rows[0:1, 0:channels].reshape(channels)
    film = [rows[n : n + 1, 0:channels] for n in (1, 2)]
    gf_ref[...] = jnp.concatenate(film, axis=1).reshape(2 * channels)
    lines = [rows[3 + n : 4 + n, :] for n in range(hidden // LANES)]
    gib_ref[...] = jnp.concatenate(lines, axis=1).reshape(hidden)
    first_tap = row_of["kernel"] // SUB
    packed = row_of["packed"]
    tap_tiles = -(-packed // SUB)
    taps = dense[first_tap : first_tap + tap_tiles].astype(jnp.float32)
    red[0 : tap_tiles * SUB] = taps.reshape(tap_tiles * SUB, LANES) * factor
    spare = LANES - channels
    folds = channels // spare
    extra = packed // folds
    for n in range(folds):
        piece = red[n * extra : (n + 1) * extra, channels:]
        red[packed : packed + extra, n * spare : (n + 1) * spare] = piece
    for i in range(K):
        for j in range(K):
            first = (i * K + j) * K
            gk_ref[i, j] = red[first : first + K, 0:channels].reshape(K, 1, channels)
    load.wait()


def local(
    counts, volume, grad_out, report, conv_kernel, conv_bias,
    film_weight, film_bias, in_weight, in_bias, out_weight,
):
    crops, slices, lines, merged = volume.shape
    channels = conv_kernel.shape[0]
    hidden = in_weight.shape[1]
    width = merged // channels
    raw_kernel = jnp.transpose(conv_kernel[:, 0], (1, 2, 3, 0))
    total = counts[0] * counts[1] * counts[2]
    blocks = hidden // LANES
    row_of = {"in": 0, "out": blocks * channels, "small": 2 * blocks * channels}
    row_of["in_bias"] = row_of["small"] + 3
    cores, squad = counts[2], counts[0] * counts[1]
    row_of["kernel"] = -(-(row_of["in_bias"] + blocks) // SUB) * SUB
    folds = channels // (LANES - channels)
    row_of["packed"] = -(-K * K * K // (folds + 1)) * folds
    taps_rows = (-(-K * K * K // SUB) + 1) * SUB
    tap_tiles = -(-row_of["packed"] // SUB)
    dense_tiles = -(-(row_of["kernel"] // SUB + tap_tiles) // total) * total
    bf, f32 = jnp.bfloat16, jnp.float32
    dma = pltpu.SemaphoreType.DMA
    tables = fourier_tables(lines, width)
    names = ("plane", "own", "taps", "forward", "backward", "lags")
    spec = tables["plane"].shape[0] // 2
    planes = slices + 2 * HALF
    voxels = lines * width
    edge_lanes = EDGE * channels
    halves = merged // 2 + 2 * edge_lanes
    main = (crops, planes, lines, merged + 2 * edge_lanes)
    side = (crops, 2, planes, 2 * EDGE, halves)
    edges = (2, crops, slices, 2 * EDGE, merged // 2)
    factor = 1.0 / math.sqrt(crops * slices * voxels * total)
    def reduce_buffers(tiles):
        band, chunk = tiles // cores, tiles // total
        return [
            pltpu.VMEM((tiles, SUB, LANES), f32),
            pltpu.VMEM((tiles, SUB, LANES), bf),
            pltpu.VMEM((band, SUB, LANES), bf),
            pltpu.VMEM((cores, band, SUB, LANES), bf),
            pltpu.VMEM((squad, chunk, SUB, LANES), bf),
            pltpu.VMEM((chunk, SUB, LANES), bf),
        ]

    operands = (
        volume,
        grad_out,
        raw_kernel,
        conv_bias,
        report,
        film_weight.T,
        film_bias,
        in_bias,
        in_weight,
        out_weight.T,
        *(tables[name] for name in names),
    )
    gathered = pl.pallas_call(
        functools.partial(kernel, counts, channels, row_of),
        out_shape=(
            jax.ShapeDtypeStruct(volume.shape, bf),
            jax.ShapeDtypeStruct((dense_tiles, SUB, LANES), bf),
        ),
        in_specs=[pl.BlockSpec(memory_space=pltpu.HBM)] * len(operands),
        out_specs=(pl.BlockSpec(memory_space=pltpu.HBM),) * 2,
        scratch_shapes=[pltpu.VMEM(a.shape, a.dtype) for a in operands]
        + [
            pltpu.VMEM(volume.shape, bf),
            pltpu.VMEM((dense_tiles, SUB, LANES), bf),
            dma((len(operands),)),
            dma((crops + 1,)),
            pltpu.VMEM((LANES, hidden), bf),
            pltpu.VMEM((LANES, hidden), bf),
            pltpu.VMEM(main, bf),
            pltpu.VMEM(side, bf),
            pltpu.VMEM(edges, bf),
            pltpu.VMEM(volume.shape, bf),
            pltpu.VMEM(main, bf),
            pltpu.VMEM(side, bf),
            pltpu.VMEM(edges, bf),
            pltpu.VMEM((crops, slices, voxels, LANES), bf),
            pltpu.VMEM((planes // 2, tables["plane"].shape[1], 2 * LANES), bf),
            pltpu.VMEM((crops, slices, voxels, LANES), bf),
            pltpu.VMEM((K * SUB, K * LANES), f32),
            pltpu.VMEM((K, spec // 2 * 3, LANES), f32),
            pltpu.VMEM((crops, planes, spec, LANES), f32),
            pltpu.VMEM((crops, planes, spec, LANES), f32),
            pltpu.VMEM((crops, slices, spec, LANES), f32),
            pltpu.VMEM((3 * spec, slices * LANES), bf),
            pltpu.VMEM((3 * spec, K * LANES), bf),
            pltpu.VMEM((slices, voxels, LANES), f32),
            pltpu.VMEM((SUB, LANES), f32),
            pltpu.VMEM((slices * voxels, LANES), f32),
            pltpu.VMEM((slices * voxels, LANES), f32),
            pltpu.VMEM((crops, slices * voxels, LANES), bf),
            pltpu.VMEM((voxels, hidden), f32),
            pltpu.VMEM((crops, slices, voxels, hidden), f32),
            pltpu.VMEM((crops, slices * voxels, hidden), bf),
            pltpu.VMEM((crops, slices * voxels, hidden), bf),
            pltpu.VMEM((SUB, hidden), f32),
            pltpu.VMEM((3, SUB, LANES), f32),
            *reduce_buffers(dense_tiles),
            pltpu.VMEM((taps_rows, LANES), f32),
        ]
        + [dma((crops, len(DIRS)))] * 4
        + [dma((cores,))] * 2 + [dma((squad,))] * 4 + [dma((cores, squad))] * 2,
        compiler_params=pltpu.CompilerParams(
            collective_id=0, has_side_effects=True, vmem_limit_bytes=60 * 1024 * 1024
        ),
        name="block",
    )(*operands)
    grad_input, grad_kernel, grad_bias, grad_film, grad_in_w, grad_in_b, grad_out_w = pl.pallas_call(
        functools.partial(finish_kernel, channels, row_of, factor),
        out_shape=(
            jax.ShapeDtypeStruct(volume.shape, bf),
            jax.ShapeDtypeStruct((K, K, K, 1, channels), f32),
            jax.ShapeDtypeStruct((channels,), f32),
            jax.ShapeDtypeStruct((2 * channels,), f32),
            jax.ShapeDtypeStruct((channels, hidden), f32),
            jax.ShapeDtypeStruct((hidden,), f32),
            jax.ShapeDtypeStruct((channels, hidden), f32),
        ),
        in_specs=[pl.BlockSpec(memory_space=pltpu.HBM)] * 2,
        out_specs=(pl.BlockSpec(memory_space=pltpu.VMEM),) * 7,
        scratch_shapes=[
            pltpu.VMEM((dense_tiles, SUB, LANES), bf),
            pltpu.VMEM((taps_rows, LANES), f32),
            dma((2,)),
        ],
        compiler_params=pltpu.CompilerParams(vmem_limit_bytes=60 * 1024 * 1024),
        name="finish",
    )(*gathered)
    grad_kernel = jnp.transpose(grad_kernel, (4, 3, 0, 1, 2))
    return (
        grad_input, grad_kernel, grad_bias, grad_film, grad_in_w, grad_in_b, grad_out_w.T
    )


def solution(mesh):
    split = P("groups", "depth", "rows", "cols")
    in_specs = (split, split, P("groups")) + (P(),) * 7
    out_specs = (
        split,
        P("groups", None, None, None, None),
        P("groups"),
        P("groups"),
        P("groups", None),
        P("groups"),
        P("groups", None),
    )
    counts = tuple(mesh.shape[name] for name in ("depth", "rows", "cols"))
    return jax.shard_map(
        functools.partial(local, counts),
        mesh=mesh,
        in_specs=in_specs,
        out_specs=out_specs,
        check_vma=False,
    )
```
